128 devices in a mesh: row: 8 (over z, core), col: 16 (over x, y).
Axes of the slice: x: 4, y: 4, z: 4, core: 2. Of those that a mesh axis runs over, the one named last changes fastest.
Arguments:
- embed: bfloat16 [262144, 64], P(('row', 'col')), may hold values from -6 to 6
- tiles: bfloat16 [8192, 128, 128], P(('row', 'col'))
- tile_rows: int32 [8192], P(('row', 'col')), may hold values from 0 to 2047, as said below
- tile_cols: int32 [8192], P(('row', 'col')), may hold values from 0 to 2047, as said below
- chg_tiles: bfloat16 [24576, 128, 128], P(('row', 'col'))
- chg_rows: int32 [24576], P(('row', 'col')), may hold values from 0 to 2047, as said below
- chg_cols: int32 [24576], P(('row', 'col')), may hold values from 0 to 2047, as said below
Outputs:
- embedding: float32 [262144, 64], P(('row', 'col'))
The draws below stay inside these ranges and needn't reach their ends.
Inputs may be any that keep to these rules, and one draw needn't show every extreme that they name: Tile n lies in the row group of the device that holds it: tile_rows[n] // 256 equals (n // 64) // 16. Tile n lies in the column group of the device that holds it: tile_cols[n] // 128 equals (n // 64) % 16. `chg_rows`: one device's list names each transpose owner at most 3 times; in every draw some owner is named exactly 3 times by every device's list. `chg_cols`: read with chg_rows to give the transpose owner.
All inputs are finite; a program needn't handle non-finite values.
Results may differ from the reference program's by a relative error of at most 0.025.
Values may be sent and summed in bfloat16 or wider, within the bound.
A program may use at most 192 MiB of HBM per device.

```python
import math
import jax
import jax.numpy as jnp
from jax import lax

K = 64
TILE = 128
ITERS = 3
CAP = 3
ROWS_DEV = 2048
TILES_DEV = 64
NODES = 262144
BLOCKS = 2048
ROW_BLK = 256
COL_BLK = 128
COL_ROWS = 16384
SUB = 16
CHG_DEV = 192
N_ROW = 8
N_COL = 16
DEVICES = 128


def tile_values(key, count, groups):
    reach = 1.15
    spread = 1.0
    mean_size = 0.8 * (math.sinh(reach) / reach) ** 2
    along = TILES_DEV * TILE / ROWS_DEV + CAP * DEVICES * TILE / (2.0 * ROWS_DEV)
    base = 1.0 / (along * TILE * mean_size)
    levels = base * jnp.power(10.0, -spread * groups.astype(jnp.float32) / (N_ROW - 1))
    levels = levels.reshape(DEVICES, count)

    def one_device(inputs):
        device, level = inputs
        device_key = jax.random.fold_in(key, device)
        shape = (count, TILE, TILE)
        values = jax.random.normal(jax.random.fold_in(device_key, 1), shape, jnp.float32)
        row_scale = jnp.exp(jax.random.uniform(jax.random.fold_in(device_key, 2), (count, TILE, 1), jnp.float32, -reach, reach))
        col_scale = jnp.exp(jax.random.uniform(jax.random.fold_in(device_key, 3), (count, 1, TILE), jnp.float32, -reach, reach))
        return (values * row_scale * col_scale * level[:, None, None]).astype(jnp.bfloat16)
    blocks = lax.map(one_device, (jnp.arange(DEVICES, dtype=jnp.int32), levels))
    return blocks.reshape(DEVICES * count, TILE, TILE)


def draw_tiles(key, part):
    holder = jnp.arange(DEVICES * TILES_DEV, dtype=jnp.int32) // TILES_DEV
    return tile_values(jax.random.fold_in(key, 5), TILES_DEV, holder // N_COL)


def draw_chg_tiles(key, part):
    owners = owner_table(key)
    return tile_values(jax.random.fold_in(key, 6), CHG_DEV, owners // N_COL)


def draw_tile_rows(key, part):
    holder = jnp.arange(DEVICES * TILES_DEV, dtype=jnp.int32) // TILES_DEV
    offset = jax.random.randint(jax.random.fold_in(key, 21), (DEVICES * TILES_DEV,), 0, ROW_BLK, dtype=jnp.int32)
    return holder // N_COL * ROW_BLK + offset


def draw_tile_cols(key, part):
    holder = jnp.arange(DEVICES * TILES_DEV, dtype=jnp.int32) // TILES_DEV
    offset = jax.random.randint(jax.random.fold_in(key, 22), (DEVICES * TILES_DEV,), 0, COL_BLK, dtype=jnp.int32)
    return holder % N_COL * COL_BLK + offset


def owner_table(key):
    half_count = CHG_DEV // 2
    spare = half_count - 1
    rank_order = jnp.argsort(jax.random.permutation(jax.random.fold_in(key, 31), DEVICES)).astype(jnp.int32)
    extra_weight = jnp.where(rank_order == 0, 100 * DEVICES, jnp.where(rank_order < DEVICES // 8, 3 * DEVICES, 0))
    random_jitter = jax.random.randint(jax.random.fold_in(key, 32), (DEVICES, DEVICES), 0, 4 * DEVICES, dtype=jnp.int32)
    score_values = (random_jitter + extra_weight[None, :]) * DEVICES + jnp.arange(DEVICES, dtype=jnp.int32)[None, :]
    chosen = jnp.argsort(-score_values, axis=1)[:, :half_count].astype(jnp.int32)
    first_keys = jax.random.randint(jax.random.fold_in(key, 33), (DEVICES, spare), 0, 1 << 20, dtype=jnp.int32) * spare + jnp.arange(spare, dtype=jnp.int32)[None, :]
    second_keys = jax.random.randint(jax.random.fold_in(key, 34), (DEVICES, spare), 0, 1 << 20, dtype=jnp.int32) * spare + jnp.arange(spare, dtype=jnp.int32)[None, :]
    first_picks = jnp.argsort(first_keys, axis=1)[:, :half_count // 2 - 1].astype(jnp.int32) + 1
    second_picks = jnp.argsort(second_keys, axis=1)[:, :half_count // 2 - 1].astype(jnp.int32) + 1
    zero_pick = jnp.zeros((DEVICES, 1), jnp.int32)
    every_once = jnp.broadcast_to(jnp.arange(half_count, dtype=jnp.int32)[None, :], (DEVICES, half_count))
    picks = jnp.concatenate([every_once, zero_pick, first_picks, zero_pick, second_picks], axis=1)
    return jnp.take_along_axis(chosen, picks, axis=1).reshape(DEVICES * CHG_DEV)


def draw_chg_rows(key, part):
    owners = owner_table(key)
    offset = jax.random.randint(jax.random.fold_in(key, 41), (DEVICES * CHG_DEV,), 0, COL_BLK, dtype=jnp.int32)
    return owners % N_COL * COL_BLK + offset


def draw_chg_cols(key, part):
    owners = owner_table(key)
    offset = jax.random.randint(jax.random.fold_in(key, 42), (DEVICES * CHG_DEV,), 0, ROW_BLK, dtype=jnp.int32)
    return owners // N_COL * ROW_BLK + offset


def level_of(key, shape, split, low, high):
    loudness, own = 1.0, jax.random.fold_in(key, 6)
    for dim, parts in split:
        steps = jnp.exp(jax.random.uniform(jax.random.fold_in(own, dim), (parts,), jnp.float32, low / len(split), high / len(split)))
        loudness = loudness * jnp.repeat(steps, shape[dim] // parts).reshape([-1 if axis == dim else 1 for axis in range(len(shape))])
    return loudness


def bell_draw(stream_key, dims, width, bound, cuts=(), kind=jnp.bfloat16):
    array = width * jax.random.normal(stream_key, dims, jnp.float32)
    if cuts:
        array = array * level_of(stream_key, dims, cuts, -0.22, 0.18)
    return jnp.clip(array, -bound, bound).astype(kind)


def setup_inputs(seed: int = 0) -> dict:
    streams_of = jax.random.split(jax.random.key(seed), 8)
    embed = bell_draw(streams_of[0], (NODES, K), 1.0, 6.0, ((0, 128),))
    tiles = draw_tiles(jax.random.fold_in(streams_of[7], 71), 0)
    tile_rows = draw_tile_rows(jax.random.fold_in(streams_of[7], 71), 0)
    tile_cols = draw_tile_cols(jax.random.fold_in(streams_of[7], 71), 0)
    chg_tiles = draw_chg_tiles(jax.random.fold_in(streams_of[7], 71), 0)
    chg_rows = draw_chg_rows(jax.random.fold_in(streams_of[7], 71), 0)
    chg_cols = draw_chg_cols(jax.random.fold_in(streams_of[7], 71), 0)
    return {"embed": embed, "tiles": tiles, "tile_rows": tile_rows, "tile_cols": tile_cols, "chg_tiles": chg_tiles, "chg_rows": chg_rows, "chg_cols": chg_cols}


def column_order(vectors):
    feature_width = vectors.shape[1]
    pieces = vectors.reshape(DEVICES, N_ROW, N_COL, SUB, feature_width)
    return jnp.transpose(pieces, (2, 1, 0, 3, 4)).reshape(NODES, feature_width)

def mirror_table(chg_rows, chg_cols):
    owners = (chg_cols // ROW_BLK * N_COL + chg_rows // COL_BLK).astype(jnp.int32)
    listed = owners.reshape(DEVICES, CHG_DEV)
    position = jnp.arange(CHG_DEV, dtype=jnp.int32)
    earlier = position[None, :] < position[:, None]
    same_owner = listed[:, :, None] == listed[:, None, :]
    slot_rank = jnp.sum(jnp.logical_and(same_owner, earlier[None, :, :]), axis=2).astype(jnp.int32)
    entries = DEVICES * CHG_DEV
    sources = jnp.broadcast_to(jnp.arange(DEVICES, dtype=jnp.int32)[:, None], (DEVICES, CHG_DEV))
    numbers = jnp.arange(entries, dtype=jnp.int32).reshape(DEVICES, CHG_DEV)
    table = jnp.full((DEVICES, DEVICES * CAP), entries, jnp.int32)
    return table.at[listed, sources * CAP + slot_rank].set(numbers)

def reference(embed, tiles, tile_rows, tile_cols, chg_tiles, chg_rows, chg_cols):
    table = mirror_table(chg_rows, chg_cols)
    padded = jnp.concatenate([chg_tiles, jnp.zeros((1, TILE, TILE), chg_tiles.dtype)], axis=0)
    zero_index = jnp.zeros((1,), jnp.int32)
    mirror_rows = jnp.concatenate([(chg_cols % ROW_BLK).astype(jnp.int32), zero_index])
    mirror_cols = jnp.concatenate([(chg_rows % COL_BLK).astype(jnp.int32), zero_index])

    def device_tiles(device):
        start = (device * TILES_DEV).astype(jnp.int32)
        own = lax.dynamic_slice_in_dim(tiles, start, TILES_DEV, 0)
        own_rows = lax.dynamic_slice_in_dim(tile_rows, start, TILES_DEV, 0) % ROW_BLK
        own_cols = lax.dynamic_slice_in_dim(tile_cols, start, TILES_DEV, 0) % COL_BLK
        picked = table[device]
        return (own, own_rows, own_cols, padded[picked], mirror_rows[picked], mirror_cols[picked])

    def add_degree(degree_sum, device):
        own, own_rows, own_cols, taken, taken_rows, taken_cols = device_tiles(device)
        terms = jax.ops.segment_sum(jnp.sum(jnp.abs(own.astype(jnp.float32)), axis=2), own_rows, ROW_BLK)
        terms = terms + jax.ops.segment_sum(jnp.sum(jnp.abs(taken.astype(jnp.float32)), axis=1), taken_rows, ROW_BLK)
        begin = (device // N_COL * ROW_BLK).astype(jnp.int32)
        block = lax.dynamic_slice_in_dim(degree_sum, begin, ROW_BLK, 0)
        return (lax.dynamic_update_slice_in_dim(degree_sum, block + terms, begin, 0), None)
    device_list = jnp.arange(DEVICES, dtype=jnp.int32)
    degree_sum, unused = lax.scan(add_degree, jnp.zeros((BLOCKS, TILE), jnp.float32), device_list)
    degree = 1.0 + degree_sum.reshape(NODES, 1)
    current = embed
    final_output = embed.astype(jnp.float32)
    for iteration in range(ITERS):
        columns = column_order(current).astype(jnp.float32)

        def add_partial(summed, device, columns=columns):
            own, own_rows, own_cols, taken, taken_rows, taken_cols = device_tiles(device)
            begin = (device % N_COL * COL_ROWS).astype(jnp.int32)
            group = lax.dynamic_slice_in_dim(columns, begin, COL_ROWS, 0).reshape(COL_BLK, TILE, K)
            own_terms = jnp.einsum('nab,nbk->nak', own.astype(jnp.float32), group[own_cols], precision=lax.Precision.HIGHEST)
            taken_terms = jnp.einsum('nab,nak->nbk', taken.astype(jnp.float32), group[taken_cols], precision=lax.Precision.HIGHEST)
            partial_value = jax.ops.segment_sum(own_terms, own_rows, ROW_BLK) + jax.ops.segment_sum(taken_terms, taken_rows, ROW_BLK)
            rounded = lax.optimization_barrier(partial_value.astype(jnp.bfloat16)).astype(jnp.float32)
            row_begin = (device // N_COL * ROW_BLK).astype(jnp.int32)
            block = lax.dynamic_slice_in_dim(summed, row_begin, ROW_BLK, 0)
            return (lax.dynamic_update_slice_in_dim(summed, block + rounded, row_begin, 0), None)
        summed, unused = lax.scan(add_partial, jnp.zeros((BLOCKS, TILE, K), jnp.float32), device_list)
        scaled = summed.reshape(NODES, K) / degree
        gram = jnp.dot(scaled.T.astype(jnp.float32), scaled.astype(jnp.float32), precision=lax.Precision.HIGHEST, preferred_element_type=jnp.float32) / NODES
        lower = jnp.linalg.cholesky(gram)
        final_output = lax.linalg.triangular_solve(lower, scaled, left_side=False, lower=True, transpose_a=True)
        current = final_output.astype(jnp.bfloat16)
    return final_output
```

```python
import functools

import jax
import jax.numpy as jnp
from jax import lax
from jax.experimental import pallas as pl
from jax.experimental.pallas import tpu as pltpu
from jax.sharding import PartitionSpec as P

ITERS = 3
CAP = 3
K = 64
TILE = 128
NR = 8
NC = 16
DEV = NR * NC
ROWS_BLK = 256
SLOT_ROWS = CAP * TILE + 16
OWN = 64
NODES = 262144
BF = jnp.bfloat16
F32 = jnp.float32
ANY = pl.BlockSpec(memory_space=pl.ANY)
VMEM = pl.BlockSpec(memory_space=pltpu.VMEM)
SMEM = pl.BlockSpec(memory_space=pltpu.SMEM)
MIB = 1024 * 1024
ROW_ORDER = ((1, 0), (3, 1), (2, 0), (1, 1), (3, 0), (2, 1), (0, 1))


def dot(a, b, dims, precision=None):
    return lax.dot_general(a, b, (dims, ((), ())), precision=precision, preferred_element_type=F32)


def pack_kernel(pick_ref, tiles_ref, meta_ref, out_ref, tile_sem, meta_sem):
    meta_copy = pltpu.make_async_copy(meta_ref, out_ref.at[:, pl.ds(CAP * TILE, 16)], meta_sem)
    meta_copy.start()

    def body(owner, carry):
        for slot in range(CAP):
            pltpu.make_async_copy(
                tiles_ref.at[pick_ref[owner * CAP + slot]],
                out_ref.at[owner, pl.ds(slot * TILE, TILE)],
                tile_sem,
            ).start()
        return carry

    lax.fori_loop(0, DEV, body, 0)
    filled = out_ref.at[:, pl.ds(0, CAP * TILE)]
    pltpu.make_async_copy(filled, filled, tile_sem).wait()
    meta_copy.wait()


def pack(pick, chg_tiles, meta):
    return pl.pallas_call(
        pack_kernel,
        out_shape=jax.ShapeDtypeStruct((DEV, SLOT_ROWS, TILE), BF),
        in_specs=[SMEM, ANY, ANY],
        out_specs=ANY,
        scratch_shapes=[pltpu.SemaphoreType.DMA, pltpu.SemaphoreType.DMA],
        name="pack",
    )(pick, chg_tiles, meta)


def greet(row, col):
    barrier = pltpu.get_barrier_semaphore()

    def cols(k, carry):
        pl.semaphore_signal(barrier, inc=1, device_id={"col": lax.rem(col + k, NC)}, device_id_type=pl.DeviceIdType.MESH)
        return carry

    def rows(k, carry):
        pl.semaphore_signal(barrier, inc=1, device_id={"row": lax.rem(row + k, NR)}, device_id_type=pl.DeviceIdType.MESH)
        return carry

    lax.fori_loop(1, NC, cols, 0)
    lax.fori_loop(1, NR, rows, 0)
    pl.semaphore_wait(barrier, NC + NR - 2)


def remote(src, dst, send_sem, recv_sem, **peer):
    return pltpu.make_async_remote_copy(
        src_ref=src, dst_ref=dst, send_sem=send_sem, recv_sem=recv_sem,
        device_id=peer, device_id_type=pl.DeviceIdType.MESH,
    )


def wait_bytes(ref, sem):
    pltpu.make_async_copy(ref, ref, sem).wait()


def x_first(row, col, xs, xc, sems):
    own = pltpu.make_async_copy(xs.at[col], xc.at[row, col], sems["x_own"])
    own.start()

    def send(k, carry):
        peer = lax.rem(col + k, NC)
        remote(xs.at[peer], xc.at[row, col], sems["xa_send"], sems["xa_recv"], col=peer).start()
        return carry

    lax.fori_loop(1, NC, send, 0)


def x_second(row, col, xs, xc, sems):
    pltpu.make_async_copy(xs.at[col], xc.at[row, col], sems["x_own"]).wait()
    wait_bytes(xc.at[row, pl.ds(0, NC - 1)], sems["xa_recv"])

    def send(k, carry):
        peer = lax.rem(row + k, NR)
        remote(xc.at[row], xc.at[row], sems["xb_send"], sems["xb_recv"], row=peer).start()
        return carry

    lax.fori_loop(1, NR, send, 0)


def x_finish(row, col, xs, xc, sems):
    wait_bytes(xs.at[pl.ds(0, NC - 1)], sems["xa_send"])
    wait_bytes(xc.at[pl.ds(0, NR - 1)], sems["xb_recv"])
    wait_bytes(xc.at[pl.ds(0, NR - 1)], sems["xb_send"])


def exchange_kernel(send_ref, xs_ref, recv_ref, mid_ref, xc_ref,
                    x_own, xa_send, xa_recv, xb_send, xb_recv,
                    a_own, a_send, a_recv, b_send, b_recv):
    row = lax.axis_index("row")
    col = lax.axis_index("col")
    sems = dict(x_own=x_own, xa_send=xa_send, xa_recv=xa_recv, xb_send=xb_send, xb_recv=xb_recv)
    greet(row, col)
    x_first(row, col, xs_ref, xc_ref, sems)
    plane, core = row // 2, lax.rem(row, 2)
    targets = [
        lax.rem(plane + dz, 4) * 2 + (lax.rem(core + flip, 2)) for dz, flip in ROW_ORDER
    ]

    def first(step, target, dst_ref):
        pltpu.make_async_copy(send_ref.at[target, col], dst_ref.at[target, col], a_own.at[step]).start()

        def send(k, carry):
            peer = lax.rem(col + k, NC)
            remote(send_ref.at[target, peer], dst_ref.at[target, col], a_send.at[step], a_recv.at[step], col=peer).start()
            return carry

        lax.fori_loop(1, NC, send, 0)

    first(0, targets[0], mid_ref)
    x_second(row, col, xs_ref, xc_ref, sems)
    for step in range(1, NR - 1):
        first(step, targets[step], mid_ref)
    first(NR - 1, row, recv_ref)
    for step in range(NR - 1):
        target = targets[step]
        wait_bytes(mid_ref.at[target, pl.ds(0, NC - 1)], a_recv.at[step])
        pltpu.make_async_copy(send_ref.at[target, col], mid_ref.at[target, col], a_own.at[step]).wait()
        remote(mid_ref.at[target], recv_ref.at[row], b_send.at[step], b_recv.at[row], row=target).start()
    wait_bytes(recv_ref.at[row, pl.ds(0, NC - 1)], a_recv.at[NR - 1])
    pltpu.make_async_copy(send_ref.at[row, col], recv_ref.at[row, col], a_own.at[NR - 1]).wait()
    x_finish(row, col, xs_ref, xc_ref, sems)
    for step in range(NR):
        wait_bytes(send_ref.at[0, pl.ds(0, NC - 1)], a_send.at[step])
    for step in range(NR - 1):
        source = targets[step]
        wait_bytes(mid_ref.at[source], b_send.at[step])
        wait_bytes(recv_ref.at[source], b_recv.at[source])


def exchange(send, xs):
    dma = pltpu.SemaphoreType.DMA
    slots = jax.ShapeDtypeStruct((NR, NC, SLOT_ROWS, TILE), BF)
    recv, _, xc = pl.pallas_call(
        exchange_kernel,
        out_shape=(slots, slots, jax.ShapeDtypeStruct((NR, NC, 4, 16, TILE), BF)),
        in_specs=[ANY, ANY],
        out_specs=(ANY, ANY, ANY),
        scratch_shapes=[dma, dma, dma, dma, dma, dma((NR,)), dma((NR,)), dma((NR,)), dma((NR,)), dma((NR,))],
        compiler_params=pltpu.CompilerParams(collective_id=0, has_side_effects=True),
        name="exchange",
    )(send.reshape(NR, NC, SLOT_ROWS, TILE), xs)
    return recv, xc


def product_kernel(with_degree, rows_ref, cols_ref, own_rows_ref, own_cols_ref, x_ref, own_ref, slots_ref, *rest):
    if with_degree:
        part_ref, degree_ref, xt_ref, acc_ref = rest
    else:
        part_ref, xt_ref, acc_ref = rest
        degree_ref = None
    step = pl.program_id(0)
    ones = jnp.ones((8, TILE), BF)

    def run(terms):
        products = []
        for load, _, x_index, dims, valid in terms:
            tile = load()
            value = dot(xt_ref[x_index], tile, dims)
            sums = None
            if with_degree:
                scale = ones if valid is None else jnp.where(valid, ones, jnp.zeros_like(ones))
                sums = dot(scale, jnp.abs(tile), dims)[0:1]
            products.append((value, sums))
        for (_, target, _, _, _), (value, sums) in zip(terms, products):
            acc_ref[target] += value
            if with_degree:
                degree_ref[target] += sums

    @pl.when(step == 0)
    def _():
        acc_ref[...] = jnp.zeros_like(acc_ref)
        if with_degree:
            degree_ref[...] = jnp.zeros_like(degree_ref)

        def turn(q, carry):
            pair, j = q // 16, lax.rem(q, 16)
            block = x_ref[pl.ds(j * 8, 8), pair].reshape(TILE, TILE)
            xt_ref[pl.ds(q * 2, 2)] = block.T.reshape(2, K, TILE)
            return carry

        lax.fori_loop(0, 64, turn, 0)
        xt_ref[pl.ds(128, 2)] = jnp.zeros((2, K, TILE), BF)

        def own(i, carry):
            run([
                (functools.partial(lambda n: own_ref[n], i * 4 + u), own_rows_ref[i * 4 + u],
                 own_cols_ref[i * 4 + u], ((1,), (1,)), None)
                for u in range(4)
            ])
            return carry

        lax.fori_loop(0, OWN // 4, own, 0)

    def taken(i, carry):
        terms = []
        for u in range(2):
            for slot in range(CAP):
                source = i * 2 + u
                n = (step * 8 + source) * CAP + slot
                x_index = cols_ref[n]
                terms.append((
                    functools.partial(lambda s, k: slots_ref[s, pl.ds(k * TILE, TILE)], source, slot),
                    rows_ref[n], x_index, ((1,), (0,)), x_index < 128,
                ))
        run(terms)
        return carry

    lax.fori_loop(0, 4, taken, 0)

    @pl.when(step == pl.num_programs(0) - 1)
    def _():
        def flush(i, carry):
            part_ref[pl.ds(i * 8, 8)] = acc_ref[pl.ds(i * 8, 8)].astype(BF)
            return carry

        lax.fori_loop(0, ROWS_BLK // 8, flush, 0)


def product(with_degree, rows, cols, own_rows, own_cols, xc, own, slots):
    whole = lambda shape: pl.BlockSpec(shape, lambda i: (0,) * len(shape))
    out_shape = [jax.ShapeDtypeStruct((ROWS_BLK, K, TILE), BF)]
    out_specs = [whole((ROWS_BLK, K, TILE))]
    if with_degree:
        out_shape.append(jax.ShapeDtypeStruct((ROWS_BLK, 1, TILE), F32))
        out_specs.append(whole((ROWS_BLK, 1, TILE)))
    terms = DEV * CAP + OWN
    return pl.pallas_call(
        functools.partial(product_kernel, with_degree),
        grid=(DEV // 8,),
        out_shape=out_shape,
        in_specs=[SMEM, SMEM, SMEM, SMEM, whole((DEV, 4, 16, TILE)), whole((OWN, TILE, TILE)),
                  pl.BlockSpec((8, SLOT_ROWS, TILE), lambda i: (i, 0, 0))],
        out_specs=out_specs,
        scratch_shapes=[pltpu.VMEM((130, K, TILE), BF), pltpu.VMEM((ROWS_BLK, K, TILE), F32)],
        compiler_params=pltpu.CompilerParams(vmem_limit_bytes=48 * MIB),
        cost_estimate=pl.CostEstimate(flops=terms * 2 * K * TILE * TILE, bytes_accessed=terms * TILE * TILE * 2, transcendentals=0),
        name="product",
    )(rows, cols, own_rows, own_cols, xc.reshape(DEV, 4, 16, TILE), own, slots.reshape(DEV, SLOT_ROWS, TILE))


def inverse_factor(gram):
    eye = (lax.broadcasted_iota(jnp.int32, (K, K), 0) == lax.broadcasted_iota(jnp.int32, (K, K), 1)).astype(F32)
    work = jnp.concatenate([gram, eye], axis=1)
    index = lax.broadcasted_iota(jnp.int32, (K, 1), 0)
    pivots = jnp.ones((K, 1), F32)
    for j in range(K):
        pivot = work[j:j + 1, j:j + 1]
        pivots = jnp.where(index == j, pivot, pivots)
        factor = jnp.where(index > j, work[:, j:j + 1] * (1.0 / pivot), 0.0)
        work = work - factor * work[j:j + 1, :]
    return lax.rsqrt(pivots) * work[:, K:]


def normalize_kernel(first, last, part_ref, degree_in_ref, *rest):
    rest = list(rest)
    if last:
        z_ref = rest.pop(0)
        xc_ref = None
    else:
        xc_ref = rest.pop(0)
    degree_ref = rest.pop(0) if first else degree_in_ref
    y_ref, rs_ref, g1_ref, g2_ref = [rest.pop(0) for _ in range(4)]
    rs_own, rs_send, rs_recv, g1_send, g1_recv, g2_send, g2_recv = [rest.pop(0) for _ in range(7)]
    if first:
        dg_ref, dg_own, dg_send, dg_recv = [rest.pop(0) for _ in range(4)]
    if not last:
        xs_ref = rest.pop(0)
        sems = dict(zip(("x_own", "xa_send", "xa_recv", "xb_send", "xb_recv"), rest))
    row = lax.axis_index("row")
    col = lax.axis_index("col")
    greet(row, col)

    if first:
        pltpu.make_async_copy(degree_in_ref.at[pl.ds(col * 16, 16)], dg_ref.at[col], dg_own).start()
    pltpu.make_async_copy(part_ref.at[pl.ds(col * 16, 16)], rs_ref.at[col], rs_own).start()

    def send(k, carry):
        peer = lax.rem(col + k, NC)
        if first:
            remote(degree_in_ref.at[pl.ds(peer * 16, 16)], dg_ref.at[col], dg_send, dg_recv, col=peer).start()
        remote(part_ref.at[pl.ds(peer * 16, 16)], rs_ref.at[col], rs_send, rs_recv.at[col], col=peer).start()
        return carry

    lax.fori_loop(1, NC, send, 0)
    if first:
        pltpu.make_async_copy(degree_in_ref.at[pl.ds(col * 16, 16)], dg_ref.at[col], dg_own).wait()
        wait_bytes(dg_ref.at[pl.ds(0, NC - 1)], dg_recv)
        degree = dg_ref[0]
        for k in range(1, NC):
            degree = degree + dg_ref[k]
        degree_ref[...] = 1.0 + degree
    pltpu.make_async_copy(part_ref.at[pl.ds(col * 16, 16)], rs_ref.at[col], rs_own).wait()
    y_ref[...] = rs_ref[col].astype(F32)

    def gather(k, carry):
        peer = lax.rem(col + NC - k, NC)
        wait_bytes(rs_ref.at[peer], rs_recv.at[peer])
        y_ref[...] += rs_ref[peer].astype(F32)
        return carry

    lax.fori_loop(1, NC, gather, 0)

    gram = jnp.zeros((K, K), F32)
    for b in range(16):
        block = y_ref[b] * (1.0 / degree_ref[b])
        y_ref[b] = block
        gram = gram + dot(block, block, ((1,), (1,)), lax.Precision.HIGHEST)
    half = K // 2
    g1_ref[col] = jnp.concatenate([gram[:half], gram[half:]], axis=1)

    def send_g1(k, carry):
        peer = lax.rem(col + k, NC)
        remote(g1_ref.at[col], g1_ref.at[col], g1_send, g1_recv, col=peer).start()
        return carry

    lax.fori_loop(1, NC, send_g1, 0)
    wait_bytes(g1_ref.at[pl.ds(0, NC - 1)], g1_recv)
    total = g1_ref[0]
    for k in range(1, NC):
        total = total + g1_ref[k]
    g2_ref[row] = total

    def send_g2(k, carry):
        peer = lax.rem(row + k, NR)
        remote(g2_ref.at[row], g2_ref.at[row], g2_send, g2_recv, row=peer).start()
        return carry

    lax.fori_loop(1, NR, send_g2, 0)
    wait_bytes(g2_ref.at[pl.ds(0, NR - 1)], g2_recv)
    total = g2_ref[0]
    for k in range(1, NR):
        total = total + g2_ref[k]
    total = total * (1.0 / NODES)
    inverse = inverse_factor(jnp.concatenate([total[:, :K], total[:, K:]], axis=0))

    def solve(b):
        return dot(inverse, y_ref[b], ((1,), (0,)), lax.Precision.HIGHEST)

    if last:
        for b in range(0, 16, 2):
            both = jnp.concatenate([solve(b), solve(b + 1)], axis=0).T
            z_ref[b * TILE:(b + 1) * TILE] = both[:, :K]
            z_ref[(b + 1) * TILE:(b + 2) * TILE] = both[:, K:]
    else:
        for pair in range(4):
            for part in range(2):
                both = jnp.concatenate([solve(pair * 4 + part), solve(pair * 4 + 2 + part)], axis=0).T
                xs_ref[part * 8:(part + 1) * 8, pair] = both.astype(BF).reshape(8, 16, TILE)
        x_first(row, col, xs_ref, xc_ref, sems)
        x_second(row, col, xs_ref, xc_ref, sems)
        x_finish(row, col, xs_ref, xc_ref, sems)
    if first:
        wait_bytes(dg_ref.at[pl.ds(0, NC - 1)], dg_send)
    wait_bytes(rs_ref.at[pl.ds(0, NC - 1)], rs_send)
    wait_bytes(g1_ref.at[pl.ds(0, NC - 1)], g1_send)
    wait_bytes(g2_ref.at[pl.ds(0, NR - 1)], g2_send)


def normalize(first, last, part, degree):
    dma = pltpu.SemaphoreType.DMA
    out_shape, out_specs = [], []
    if last:
        out_shape.append(jax.ShapeDtypeStruct((16 * TILE, K), F32))
        out_specs.append(VMEM)
    else:
        out_shape.append(jax.ShapeDtypeStruct((NR, NC, 4, 16, TILE), BF))
        out_specs.append(ANY)
    if first:
        out_shape.append(jax.ShapeDtypeStruct((16, 1, TILE), F32))
        out_specs.append(VMEM)
    scratch = [
        pltpu.VMEM((16, K, TILE), F32), pltpu.VMEM((NC, 16, K, TILE), BF),
        pltpu.VMEM((NC, K // 2, TILE), F32), pltpu.VMEM((NR, K // 2, TILE), F32),
        dma, dma, dma((NC,)), dma, dma, dma, dma,
    ]
    if first:
        scratch += [pltpu.VMEM((NC, 16, 1, TILE), F32), dma, dma, dma]
    if not last:
        scratch += [pltpu.VMEM((NC, 4, 16, TILE), BF), dma, dma, dma, dma, dma]
    return pl.pallas_call(
        functools.partial(normalize_kernel, first, last),
        out_shape=out_shape,
        in_specs=[ANY, ANY if first else VMEM],
        out_specs=out_specs,
        scratch_shapes=scratch,
        compiler_params=pltpu.CompilerParams(
            collective_id=1 if first else (3 if last else 2), has_side_effects=True, vmem_limit_bytes=40 * MIB
        ),
        name="normalize",
    )(part, degree)


def block_index(block):
    return block // 32 * 32 + block % 16 * 2 + block // 16 % 2


def local(embed, tiles, tile_rows, tile_cols, chg_tiles, chg_rows, chg_cols):
    owners = chg_cols // 256 * NC + chg_rows // 128
    count = owners.shape[0]
    position = jnp.arange(count, dtype=jnp.int32)
    earlier = position[None, :] < position[:, None]
    rank = jnp.sum(jnp.logical_and(owners[:, None] == owners[None, :], earlier).astype(jnp.int32), axis=1)
    key = owners * CAP + rank
    hit = jnp.arange(DEV * CAP, dtype=jnp.int32)[:, None] == key[None, :]
    pick = jnp.sum(jnp.where(hit, position[None, :], 0), axis=1)
    code = jnp.sum(jnp.where(hit, (1 + chg_cols % 256 * 128 + block_index(chg_rows % 128))[None, :], 0), axis=1)
    slot_rows = jnp.where(code > 0, (code - 1) // 128, 0).reshape(DEV, CAP)
    slot_cols = jnp.where(code > 0, (code - 1) % 128, 128).reshape(DEV, CAP)
    meta = jnp.pad(jnp.concatenate([slot_rows, slot_cols], axis=1).astype(BF), ((0, 0), (0, TILE - 2 * CAP)))
    meta = jnp.broadcast_to(meta[:, None, :], (DEV, 16, TILE))
    send = pack(pick, chg_tiles, meta)
    xs = embed.reshape(4, 2, NC, 16, K).transpose(2, 0, 3, 1, 4).reshape(NC, 4, 16, TILE)
    slots, xc = exchange(send, xs)
    places = slots.reshape(DEV, SLOT_ROWS, TILE)[:, CAP * TILE, :2 * CAP].astype(jnp.int32)
    rows = places[:, :CAP].reshape(DEV * CAP)
    cols = places[:, CAP:].reshape(DEV * CAP)
    own_rows = tile_rows % 256
    own_cols = block_index(tile_cols % 128)
    degree = None
    for iteration in range(ITERS):
        first, last = iteration == 0, iteration == ITERS - 1
        outs = product(first, rows, cols, own_rows, own_cols, xc, tiles, slots)
        if first:
            xc, degree = normalize(first, last, outs[0], outs[1])
        else:
            (xc,) = normalize(first, last, outs[0], degree)
    return xc


def solution(mesh):
    placed = (
        P(("row", "col"), None),
        P(("row", "col"), None, None),
        P(("row", "col")),
        P(("row", "col")),
        P(("row", "col"), None, None),
        P(("row", "col")),
        P(("row", "col")),
    )
    return jax.shard_map(
        local, mesh=mesh, in_specs=placed, out_specs=P(("row", "col"), None), check_vma=False
    )
```

```python
import functools

import jax
import jax.numpy as jnp
from jax import lax
from jax.experimental import pallas as pl
from jax.experimental.pallas import tpu as pltpu
from jax.sharding import PartitionSpec as P

ITERS = 3
CAP = 3
K = 64
TILE = 128
NR = 8
NC = 16
DEV = NR * NC
ROWS_BLK = 256
SLOT_ROWS = CAP * TILE + 16
OWN = 64
NODES = 262144
BF = jnp.bfloat16
F32 = jnp.float32
ANY = pl.BlockSpec(memory_space=pl.ANY)
VMEM = pl.BlockSpec(memory_space=pltpu.VMEM)
SMEM = pl.BlockSpec(memory_space=pltpu.SMEM)
MIB = 1024 * 1024
ROW_ORDER = ((1, 0), (3, 1), (2, 0), (1, 1), (3, 0), (2, 1), (0, 1))


def dot(a, b, dims, precision=None):
    return lax.dot_general(a, b, (dims, ((), ())), precision=precision, preferred_element_type=F32)


def pack_kernel(pick_ref, tiles_ref, meta_ref, out_ref):
    step = pl.program_id(0)

    def body(i, carry):
        for slot in range(CAP):
            tile = tiles_ref[pick_ref[(step * 8 + i) * CAP + slot]]
            out_ref[i, slot * TILE:(slot + 1) * TILE] = tile
        out_ref[i, CAP * TILE:] = meta_ref[i]
        return carry

    lax.fori_loop(0, 8, body, 0)


def pack(pick, chg_tiles, meta):
    return pl.pallas_call(
        pack_kernel,
        grid=(DEV // 8,),
        out_shape=jax.ShapeDtypeStruct((DEV, SLOT_ROWS, TILE), BF),
        in_specs=[SMEM, pl.BlockSpec(chg_tiles.shape, lambda i: (0, 0, 0)),
                  pl.BlockSpec((8, 16, TILE), lambda i: (i, 0, 0))],
        out_specs=pl.BlockSpec((8, SLOT_ROWS, TILE), lambda i: (i, 0, 0)),
        compiler_params=pltpu.CompilerParams(vmem_limit_bytes=32 * MIB),
        name="pack",
    )(pick, chg_tiles, meta)


def greet(row, col):
    barrier = pltpu.get_barrier_semaphore()

    def cols(k, carry):
        pl.semaphore_signal(barrier, inc=1, device_id={"col": lax.rem(col + k, NC)}, device_id_type=pl.DeviceIdType.MESH)
        return carry

    def rows(k, carry):
        pl.semaphore_signal(barrier, inc=1, device_id={"row": lax.rem(row + k, NR)}, device_id_type=pl.DeviceIdType.MESH)
        return carry

    lax.fori_loop(1, NC, cols, 0)
    lax.fori_loop(1, NR, rows, 0)
    pl.semaphore_wait(barrier, NC + NR - 2)


def remote(src, dst, send_sem, recv_sem, **peer):
    return pltpu.make_async_remote_copy(
        src_ref=src, dst_ref=dst, send_sem=send_sem, recv_sem=recv_sem,
        device_id=peer, device_id_type=pl.DeviceIdType.MESH,
    )


def wait_bytes(ref, sem):
    pltpu.make_async_copy(ref, ref, sem).wait()


def x_first(row, col, xs, xc, sems):
    own = pltpu.make_async_copy(xs.at[col], xc.at[row, col], sems["x_own"])
    own.start()

    def send(k, carry):
        peer = lax.rem(col + k, NC)
        remote(xs.at[peer], xc.at[row, col], sems["xa_send"], sems["xa_recv"], col=peer).start()
        return carry

    lax.fori_loop(1, NC, send, 0)


def x_second(row, col, xs, xc, sems):
    pltpu.make_async_copy(xs.at[col], xc.at[row, col], sems["x_own"]).wait()
    wait_bytes(xc.at[row, pl.ds(0, NC - 1)], sems["xa_recv"])

    def send(k, carry):
        peer = lax.rem(row + k, NR)
        remote(xc.at[row], xc.at[row], sems["xb_send"], sems["xb_recv"], row=peer).start()
        return carry

    lax.fori_loop(1, NR, send, 0)


def x_finish(row, col, xs, xc, sems):
    wait_bytes(xs.at[pl.ds(0, NC - 1)], sems["xa_send"])
    wait_bytes(xc.at[pl.ds(0, NR - 1)], sems["xb_recv"])
    wait_bytes(xc.at[pl.ds(0, NR - 1)], sems["xb_send"])


def exchange_kernel(send_ref, xs_ref, recv_ref, mid_ref, xc_ref,
                    x_own, xa_send, xa_recv, xb_send, xb_recv,
                    a_own, a_send, a_recv, b_send, b_recv):
    row = lax.axis_index("row")
    col = lax.axis_index("col")
    sems = dict(x_own=x_own, xa_send=xa_send, xa_recv=xa_recv, xb_send=xb_send, xb_recv=xb_recv)
    greet(row, col)
    x_first(row, col, xs_ref, xc_ref, sems)
    plane, core = row // 2, lax.rem(row, 2)
    targets = [
        lax.rem(plane + dz, 4) * 2 + (lax.rem(core + flip, 2)) for dz, flip in ROW_ORDER
    ]

    def first(step, target, dst_ref):
        pltpu.make_async_copy(send_ref.at[target, col], dst_ref.at[target, col], a_own.at[step]).start()

        def send(k, carry):
            peer = lax.rem(col + k, NC)
            remote(send_ref.at[target, peer], dst_ref.at[target, col], a_send.at[step], a_recv.at[step], col=peer).start()
            return carry

        lax.fori_loop(1, NC, send, 0)

    first(0, targets[0], mid_ref)
    x_second(row, col, xs_ref, xc_ref, sems)
    for step in range(1, NR - 1):
        first(step, targets[step], mid_ref)
    first(NR - 1, row, recv_ref)
    for step in range(NR - 1):
        target = targets[step]
        wait_bytes(mid_ref.at[target, pl.ds(0, NC - 1)], a_recv.at[step])
        pltpu.make_async_copy(send_ref.at[target, col], mid_ref.at[target, col], a_own.at[step]).wait()
        remote(mid_ref.at[target], recv_ref.at[row], b_send.at[step], b_recv.at[row], row=target).start()
    wait_bytes(recv_ref.at[row, pl.ds(0, NC - 1)], a_recv.at[NR - 1])
    pltpu.make_async_copy(send_ref.at[row, col], recv_ref.at[row, col], a_own.at[NR - 1]).wait()
    x_finish(row, col, xs_ref, xc_ref, sems)
    for step in range(NR):
        wait_bytes(send_ref.at[0, pl.ds(0, NC - 1)], a_send.at[step])
    for step in range(NR - 1):
        source = targets[step]
        wait_bytes(mid_ref.at[source], b_send.at[step])
        wait_bytes(recv_ref.at[source], b_recv.at[source])


def exchange(send, xs):
    dma = pltpu.SemaphoreType.DMA
    slots = jax.ShapeDtypeStruct((NR, NC, SLOT_ROWS, TILE), BF)
    recv, _, xc = pl.pallas_call(
        exchange_kernel,
        out_shape=(slots, slots, jax.ShapeDtypeStruct((NR, NC, 4, 16, TILE), BF)),
        in_specs=[ANY, ANY],
        out_specs=(ANY, ANY, ANY),
        scratch_shapes=[dma, dma, dma, dma, dma, dma((NR,)), dma((NR,)), dma((NR,)), dma((NR,)), dma((NR,))],
        compiler_params=pltpu.CompilerParams(collective_id=0, has_side_effects=True),
        name="exchange",
    )(send.reshape(NR, NC, SLOT_ROWS, TILE), xs)
    return recv, xc


def product_kernel(with_degree, rows_ref, cols_ref, own_rows_ref, own_cols_ref, x_ref, own_ref, slots_ref, *rest):
    if with_degree:
        part_ref, degree_out_ref, xt_ref, acc_ref, degree_ref = rest
    else:
        part_ref, xt_ref, acc_ref = rest
        degree_ref = None
    step = pl.program_id(0)
    ones = jnp.ones((8, TILE), BF)

    def run(terms):
        products = []
        for load, _, x_index, dims, valid in terms:
            tile = load()
            value = dot(xt_ref[x_index], tile, dims)
            sums = None
            if with_degree:
                scale = ones if valid is None else jnp.where(valid, ones, jnp.zeros_like(ones))
                sums = dot(scale, jnp.abs(tile), dims)[0:1]
            products.append((value, sums))
        for (_, target, _, _, _), (value, sums) in zip(terms, products):
            acc_ref[target] += value
            if with_degree:
                degree_ref[target] += sums

    @pl.when(step == 0)
    def _():
        acc_ref[...] = jnp.zeros_like(acc_ref)
        if with_degree:
            degree_ref[...] = jnp.zeros_like(degree_ref)

        def turn(q, carry):
            pair, j = q // 16, lax.rem(q, 16)
            block = x_ref[pl.ds(j * 8, 8), pair].reshape(TILE, TILE)
            xt_ref[pl.ds(q * 2, 2)] = block.T.reshape(2, K, TILE)
            return carry

        lax.fori_loop(0, 64, turn, 0)
        xt_ref[pl.ds(128, 2)] = jnp.zeros((2, K, TILE), BF)

        def own(i, carry):
            run([
                (functools.partial(lambda n: own_ref[n], i * 4 + u), own_rows_ref[i * 4 + u],
                 own_cols_ref[i * 4 + u], ((1,), (1,)), None)
                for u in range(4)
            ])
            return carry

        lax.fori_loop(0, OWN // 4, own, 0)

    def taken(i, carry):
        terms = []
        for u in range(2):
            for slot in range(CAP):
                source = i * 2 + u
                n = (step * 8 + source) * CAP + slot
                x_index = cols_ref[n]
                terms.append((
                    functools.partial(lambda s, k: slots_ref[s, pl.ds(k * TILE, TILE)], source, slot),
                    rows_ref[n], x_index, ((1,), (0,)), x_index < 128,
                ))
        run(terms)
        return carry

    lax.fori_loop(0, 4, taken, 0)

    @pl.when(step == pl.num_programs(0) - 1)
    def _():
        def flush(i, carry):
            part_ref[pl.ds(i * 8, 8)] = acc_ref[pl.ds(i * 8, 8)].astype(BF)
            return carry

        lax.fori_loop(0, ROWS_BLK // 8, flush, 0)
        if with_degree:
            degree_out_ref[...] = degree_ref[...].reshape(ROWS_BLK, TILE)


def product(with_degree, rows, cols, own_rows, own_cols, xc, own, slots):
    whole = lambda shape: pl.BlockSpec(shape, lambda i: (0,) * len(shape))
    out_shape = [jax.ShapeDtypeStruct((ROWS_BLK, K, TILE), BF)]
    out_specs = [whole((ROWS_BLK, K, TILE))]
    if with_degree:
        out_shape.append(jax.ShapeDtypeStruct((ROWS_BLK, TILE), F32))
        out_specs.append(whole((ROWS_BLK, TILE)))
    scratch = [pltpu.VMEM((130, K, TILE), BF), pltpu.VMEM((ROWS_BLK, K, TILE), F32)]
    if with_degree:
        scratch.append(pltpu.VMEM((ROWS_BLK, 1, TILE), F32))
    terms = DEV * CAP + OWN
    return pl.pallas_call(
        functools.partial(product_kernel, with_degree),
        grid=(DEV // 8,),
        out_shape=out_shape,
        in_specs=[SMEM, SMEM, SMEM, SMEM, whole((DEV, 4, 16, TILE)), whole((OWN, TILE, TILE)),
                  pl.BlockSpec((8, SLOT_ROWS, TILE), lambda i: (i, 0, 0))],
        out_specs=out_specs,
        scratch_shapes=scratch,
        compiler_params=pltpu.CompilerParams(vmem_limit_bytes=48 * MIB),
        cost_estimate=pl.CostEstimate(flops=terms * 2 * K * TILE * TILE, bytes_accessed=terms * TILE * TILE * 2, transcendentals=0),
        name="product",
    )(rows, cols, own_rows, own_cols, xc.reshape(DEV, 4, 16, TILE), own, slots.reshape(DEV, SLOT_ROWS, TILE))


def inverse_factor(gram):
    eye = (lax.broadcasted_iota(jnp.int32, (K, K), 0) == lax.broadcasted_iota(jnp.int32, (K, K), 1)).astype(F32)
    work = jnp.concatenate([gram, eye], axis=1)
    index = lax.broadcasted_iota(jnp.int32, (K, 1), 0)
    pivots = jnp.ones((K, 1), F32)
    for j in range(K):
        pivot = work[j:j + 1, j:j + 1]
        pivots = jnp.where(index == j, pivot, pivots)
        factor = jnp.where(index > j, work[:, j:j + 1] * (1.0 / pivot), 0.0)
        work = work - factor * work[j:j + 1, :]
    return lax.rsqrt(pivots) * work[:, K:]


def normalize_kernel(first, last, part_ref, degree_in_ref, *rest):
    rest = list(rest)
    if last:
        z_ref = rest.pop(0)
        xc_ref = None
    else:
        xc_ref = rest.pop(0)
    degree_ref = rest.pop(0) if first else degree_in_ref
    y_ref, rs_ref, g1_ref, g2_ref = [rest.pop(0) for _ in range(4)]
    rs_own, rs_send, rs_recv, g1_send, g1_recv, g2_send, g2_recv = [rest.pop(0) for _ in range(7)]
    if first:
        dg_ref, dg_own, dg_send, dg_recv = [rest.pop(0) for _ in range(4)]
    if not last:
        xs_ref = rest.pop(0)
        sems = dict(zip(("x_own", "xa_send", "xa_recv", "xb_send", "xb_recv"), rest))
    row = lax.axis_index("row")
    col = lax.axis_index("col")
    greet(row, col)

    if first:
        pltpu.make_async_copy(degree_in_ref.at[pl.ds(col * 16, 16)], dg_ref.at[col], dg_own).start()
    pltpu.make_async_copy(part_ref.at[pl.ds(col * 16, 16)], rs_ref.at[col], rs_own).start()

    def send(k, carry):
        peer = lax.rem(col + k, NC)
        if first:
            remote(degree_in_ref.at[pl.ds(peer * 16, 16)], dg_ref.at[col], dg_send, dg_recv, col=peer).start()
        remote(part_ref.at[pl.ds(peer * 16, 16)], rs_ref.at[col], rs_send, rs_recv.at[col], col=peer).start()
        return carry

    lax.fori_loop(1, NC, send, 0)
    if first:
        pltpu.make_async_copy(degree_in_ref.at[pl.ds(col * 16, 16)], dg_ref.at[col], dg_own).wait()
        wait_bytes(dg_ref.at[pl.ds(0, NC - 1)], dg_recv)
        degree = dg_ref[0]
        for k in range(1, NC):
            degree = degree + dg_ref[k]
        degree_ref[...] = 1.0 + degree
    pltpu.make_async_copy(part_ref.at[pl.ds(col * 16, 16)], rs_ref.at[col], rs_own).wait()
    y_ref[...] = rs_ref[col].astype(F32)

    def gather(k, carry):
        peer = lax.rem(col + NC - k, NC)
        wait_bytes(rs_ref.at[peer], rs_recv.at[peer])
        y_ref[...] += rs_ref[peer].astype(F32)
        return carry

    lax.fori_loop(1, NC, gather, 0)

    gram = jnp.zeros((K, K), F32)
    for b in range(16):
        block = y_ref[b] * (1.0 / degree_ref[b:b + 1])
        y_ref[b] = block
        gram = gram + dot(block, block, ((1,), (1,)), lax.Precision.HIGHEST)
    half = K // 2
    g1_ref[col] = jnp.concatenate([gram[:half], gram[half:]], axis=1)

    def send_g1(k, carry):
        peer = lax.rem(col + k, NC)
        remote(g1_ref.at[col], g1_ref.at[col], g1_send, g1_recv, col=peer).start()
        return carry

    lax.fori_loop(1, NC, send_g1, 0)
    wait_bytes(g1_ref.at[pl.ds(0, NC - 1)], g1_recv)
    total = g1_ref[0]
    for k in range(1, NC):
        total = total + g1_ref[k]
    g2_ref[row] = total

    def send_g2(k, carry):
        peer = lax.rem(row + k, NR)
        remote(g2_ref.at[row], g2_ref.at[row], g2_send, g2_recv, row=peer).start()
        return carry

    lax.fori_loop(1, NR, send_g2, 0)
    wait_bytes(g2_ref.at[pl.ds(0, NR - 1)], g2_recv)
    total = g2_ref[0]
    for k in range(1, NR):
        total = total + g2_ref[k]
    total = total * (1.0 / NODES)
    inverse = inverse_factor(jnp.concatenate([total[:, :K], total[:, K:]], axis=0))

    def solve(b):
        return dot(inverse, y_ref[b], ((1,), (0,)), lax.Precision.HIGHEST)

    if last:
        for b in range(0, 16, 2):
            both = jnp.concatenate([solve(b), solve(b + 1)], axis=0).T
            z_ref[b * TILE:(b + 1) * TILE] = both[:, :K]
            z_ref[(b + 1) * TILE:(b + 2) * TILE] = both[:, K:]
    else:
        for pair in range(4):
            for part in range(2):
                both = jnp.concatenate([solve(pair * 4 + part), solve(pair * 4 + 2 + part)], axis=0).T
                xs_ref[part * 8:(part + 1) * 8, pair] = both.astype(BF).reshape(8, 16, TILE)
        x_first(row, col, xs_ref, xc_ref, sems)
        x_second(row, col, xs_ref, xc_ref, sems)
        x_finish(row, col, xs_ref, xc_ref, sems)
    if first:
        wait_bytes(dg_ref.at[pl.ds(0, NC - 1)], dg_send)
    wait_bytes(rs_ref.at[pl.ds(0, NC - 1)], rs_send)
    wait_bytes(g1_ref.at[pl.ds(0, NC - 1)], g1_send)
    wait_bytes(g2_ref.at[pl.ds(0, NR - 1)], g2_send)


def normalize(first, last, part, degree):
    dma = pltpu.SemaphoreType.DMA
    out_shape, out_specs = [], []
    if last:
        out_shape.append(jax.ShapeDtypeStruct((16 * TILE, K), F32))
        out_specs.append(VMEM)
    else:
        out_shape.append(jax.ShapeDtypeStruct((NR, NC, 4, 16, TILE), BF))
        out_specs.append(ANY)
    if first:
        out_shape.append(jax.ShapeDtypeStruct((16, TILE), F32))
        out_specs.append(VMEM)
    scratch = [
        pltpu.VMEM((16, K, TILE), F32), pltpu.VMEM((NC, 16, K, TILE), BF),
        pltpu.VMEM((NC, K // 2, TILE), F32), pltpu.VMEM((NR, K // 2, TILE), F32),
        dma, dma, dma((NC,)), dma, dma, dma, dma,
    ]
    if first:
        scratch += [pltpu.VMEM((NC, 16, TILE), F32), dma, dma, dma]
    if not last:
        scratch += [pltpu.VMEM((NC, 4, 16, TILE), BF), dma, dma, dma, dma, dma]
    return pl.pallas_call(
        functools.partial(normalize_kernel, first, last),
        out_shape=out_shape,
        in_specs=[ANY, ANY if first else VMEM],
        out_specs=out_specs,
        scratch_shapes=scratch,
        compiler_params=pltpu.CompilerParams(
            collective_id=1 if first else (3 if last else 2), has_side_effects=True, vmem_limit_bytes=40 * MIB
        ),
        name="normalize",
    )(part, degree)


def block_index(block):
    return block // 32 * 32 + block % 16 * 2 + block // 16 % 2


def local(embed, tiles, tile_rows, tile_cols, chg_tiles, chg_rows, chg_cols):
    owners = chg_cols // 256 * NC + chg_rows // 128
    count = owners.shape[0]
    position = jnp.arange(count, dtype=jnp.int32)
    earlier = position[None, :] < position[:, None]
    rank = jnp.sum(jnp.logical_and(owners[:, None] == owners[None, :], earlier).astype(jnp.int32), axis=1)
    key = owners * CAP + rank
    hit = jnp.arange(DEV * CAP, dtype=jnp.int32)[:, None] == key[None, :]
    pick = jnp.sum(jnp.where(hit, position[None, :], 0), axis=1)
    code = jnp.sum(jnp.where(hit, (1 + chg_cols % 256 * 128 + block_index(chg_rows % 128))[None, :], 0), axis=1)
    slot_rows = jnp.where(code > 0, (code - 1) // 128, 0).reshape(DEV, CAP)
    slot_cols = jnp.where(code > 0, (code - 1) % 128, 128).reshape(DEV, CAP)
    meta = jnp.pad(jnp.concatenate([slot_rows, slot_cols], axis=1).astype(BF), ((0, 0), (0, TILE - 2 * CAP)))
    meta = jnp.broadcast_to(meta[:, None, :], (DEV, 16, TILE))
    send = pack(pick, chg_tiles, meta)
    xs = embed.reshape(4, 2, NC, 16, K).transpose(2, 0, 3, 1, 4).reshape(NC, 4, 16, TILE)
    slots, xc = exchange(send, xs)
    places = slots.reshape(DEV, SLOT_ROWS, TILE)[:, CAP * TILE, :2 * CAP].astype(jnp.int32)
    rows = places[:, :CAP].reshape(DEV * CAP)
    cols = places[:, CAP:].reshape(DEV * CAP)
    own_rows = tile_rows % 256
    own_cols = block_index(tile_cols % 128)
    degree = None
    for iteration in range(ITERS):
        first, last = iteration == 0, iteration == ITERS - 1
        outs = product(first, rows, cols, own_rows, own_cols, xc, tiles, slots)
        if first:
            xc, degree = normalize(first, last, outs[0], outs[1])
        else:
            (xc,) = normalize(first, last, outs[0], degree)
    return xc


def solution(mesh):
    placed = (
        P(("row", "col"), None),
        P(("row", "col"), None, None),
        P(("row", "col")),
        P(("row", "col")),
        P(("row", "col"), None, None),
        P(("row", "col")),
        P(("row", "col")),
    )
    return jax.shard_map(
        local, mesh=mesh, in_specs=placed, out_specs=P(("row", "col"), None), check_vma=False
    )
```

```python
import functools

import jax
import jax.numpy as jnp
from jax import lax
from jax.experimental import pallas as pl
from jax.experimental.pallas import tpu as pltpu
from jax.sharding import PartitionSpec as P

ITERS = 3
CAP = 3
K = 64
TILE = 128
NR = 8
NC = 16
DEV = NR * NC
ROWS_BLK = 256
SLOT_ROWS = CAP * TILE + 16
OWN = 64
NODES = 262144
BF = jnp.bfloat16
F32 = jnp.float32
ANY = pl.BlockSpec(memory_space=pl.ANY)
VMEM = pl.BlockSpec(memory_space=pltpu.VMEM)
SMEM = pl.BlockSpec(memory_space=pltpu.SMEM)
MIB = 1024 * 1024
ROW_ORDER = ((1, 0), (3, 1), (2, 0), (1, 1), (3, 0), (2, 1), (0, 1))


def dot(a, b, dims, precision=None):
    return lax.dot_general(a, b, (dims, ((), ())), precision=precision, preferred_element_type=F32)


def pack_kernel(pick_ref, tiles_ref, meta_ref, out_ref):
    step = pl.program_id(0)

    def body(i, carry):
        for slot in range(CAP):
            tile = tiles_ref[pick_ref[(step * 8 + i) * CAP + slot]]
            out_ref[i, slot * TILE:(slot + 1) * TILE] = tile
        out_ref[i, CAP * TILE:] = meta_ref[i]
        return carry

    lax.fori_loop(0, 8, body, 0)


def pack(pick, chg_tiles, meta):
    return pl.pallas_call(
        pack_kernel,
        grid=(DEV // 8,),
        out_shape=jax.ShapeDtypeStruct((DEV, SLOT_ROWS, TILE), BF),
        in_specs=[SMEM, pl.BlockSpec(chg_tiles.shape, lambda i: (0, 0, 0)),
                  pl.BlockSpec((8, 16, TILE), lambda i: (i, 0, 0))],
        out_specs=pl.BlockSpec((8, SLOT_ROWS, TILE), lambda i: (i, 0, 0)),
        compiler_params=pltpu.CompilerParams(vmem_limit_bytes=32 * MIB),
        name="pack",
    )(pick, chg_tiles, meta)


def greet(row, col):
    barrier = pltpu.get_barrier_semaphore()

    def cols(k, carry):
        pl.semaphore_signal(barrier, inc=1, device_id={"col": lax.rem(col + k, NC)}, device_id_type=pl.DeviceIdType.MESH)
        return carry

    def rows(k, carry):
        pl.semaphore_signal(barrier, inc=1, device_id={"row": lax.rem(row + k, NR)}, device_id_type=pl.DeviceIdType.MESH)
        return carry

    lax.fori_loop(1, NC, cols, 0)
    lax.fori_loop(1, NR, rows, 0)
    pl.semaphore_wait(barrier, NC + NR - 2)


def remote(src, dst, send_sem, recv_sem, **peer):
    return pltpu.make_async_remote_copy(
        src_ref=src, dst_ref=dst, send_sem=send_sem, recv_sem=recv_sem,
        device_id=peer, device_id_type=pl.DeviceIdType.MESH,
    )


def wait_bytes(ref, sem):
    pltpu.make_async_copy(ref, ref, sem).wait()


def col_peer(col, k):
    return lax.rem(col // 4 + k // 4, 4) * 4 + lax.rem(lax.rem(col, 4) + lax.rem(k, 4), 4)


def row_peer(row, dz, flip=0):
    return lax.rem(row // 2 + dz, 4) * 2 + lax.rem(row + flip, 2)


def x_first(row, col, xs, xc, sems):
    pltpu.make_async_copy(xs.at[col], xc.at[row, col], sems["x_own"]).start()

    def send(k, carry):
        peer = col_peer(col, k)
        remote(xs.at[peer], xc.at[row, col], sems["xa_send"], sems["xa_recv"], col=peer).start()
        return carry

    lax.fori_loop(1, NC, send, 0)


def x_second(row, col, xs, xc, sems):
    pltpu.make_async_copy(xs.at[col], xc.at[row, col], sems["x_own"]).wait()
    wait_bytes(xc.at[row, pl.ds(0, NC - 1)], sems["xa_recv"])
    for i, (dz, flip) in enumerate(((1, 0), (3, 0), (2, 0), (0, 1))):
        remote(xc.at[row], xc.at[row], sems["xb_send"].at[i], sems["xb_recv"].at[row], row=row_peer(row, dz, flip)).start()


def x_third(row, col, xs, xc, sems):
    for i, dz in enumerate((1, 3, 2)):
        source = row_peer(row, dz)
        wait_bytes(xc.at[source], sems["xb_recv"].at[source])
        remote(xc.at[source], xc.at[source], sems["xb_send"].at[4 + i], sems["xb_recv"].at[source], row=row_peer(row, 0, 1)).start()


def x_finish(row, col, xs, xc, sems):
    for dz in range(4):
        source = row_peer(row, dz, 1)
        wait_bytes(xc.at[source], sems["xb_recv"].at[source])
    wait_bytes(xs.at[pl.ds(0, NC - 1)], sems["xa_send"])
    for i in range(7):
        wait_bytes(xc.at[row], sems["xb_send"].at[i])


X_SEMS = ("x_own", "xa_send", "xa_recv", "xb_send", "xb_recv")


def x_sems():
    dma = pltpu.SemaphoreType.DMA
    return [dma, dma, dma, dma((7,)), dma((NR,))]


def exchange_kernel(send_ref, xs_ref, recv_ref, mid_ref, xc_ref,
                    x_own, xa_send, xa_recv, xb_send, xb_recv,
                    a_own, a_send, a_recv, b_send, b_recv):
    row = lax.axis_index("row")
    col = lax.axis_index("col")
    sems = dict(x_own=x_own, xa_send=xa_send, xa_recv=xa_recv, xb_send=xb_send, xb_recv=xb_recv)
    greet(row, col)
    x_first(row, col, xs_ref, xc_ref, sems)
    plane, core = row // 2, lax.rem(row, 2)
    targets = [
        lax.rem(plane + dz, 4) * 2 + (lax.rem(core + flip, 2)) for dz, flip in ROW_ORDER
    ]

    def first(step, target, dst_ref):
        pltpu.make_async_copy(send_ref.at[target, col], dst_ref.at[target, col], a_own.at[step]).start()

        def send(k, carry):
            peer = col_peer(col, k)
            remote(send_ref.at[target, peer], dst_ref.at[target, col], a_send.at[step], a_recv.at[step], col=peer).start()
            return carry

        lax.fori_loop(1, NC, send, 0)

    first(0, targets[0], mid_ref)
    x_second(row, col, xs_ref, xc_ref, sems)
    for step in range(1, NR - 1):
        first(step, targets[step], mid_ref)
    first(NR - 1, row, recv_ref)
    x_third(row, col, xs_ref, xc_ref, sems)
    for step in range(NR - 1):
        target = targets[step]
        wait_bytes(mid_ref.at[target, pl.ds(0, NC - 1)], a_recv.at[step])
        pltpu.make_async_copy(send_ref.at[target, col], mid_ref.at[target, col], a_own.at[step]).wait()
        remote(mid_ref.at[target], recv_ref.at[row], b_send.at[step], b_recv.at[row], row=target).start()
    wait_bytes(recv_ref.at[row, pl.ds(0, NC - 1)], a_recv.at[NR - 1])
    pltpu.make_async_copy(send_ref.at[row, col], recv_ref.at[row, col], a_own.at[NR - 1]).wait()
    x_finish(row, col, xs_ref, xc_ref, sems)
    for step in range(NR):
        wait_bytes(send_ref.at[0, pl.ds(0, NC - 1)], a_send.at[step])
    for step in range(NR - 1):
        source = targets[step]
        wait_bytes(mid_ref.at[source], b_send.at[step])
        wait_bytes(recv_ref.at[source], b_recv.at[source])


def exchange(send, xs):
    dma = pltpu.SemaphoreType.DMA
    slots = jax.ShapeDtypeStruct((NR, NC, SLOT_ROWS, TILE), BF)
    recv, _, xc = pl.pallas_call(
        exchange_kernel,
        out_shape=(slots, slots, jax.ShapeDtypeStruct((NR, NC, 4, 16, TILE), BF)),
        in_specs=[ANY, ANY],
        out_specs=(ANY, ANY, ANY),
        scratch_shapes=x_sems() + [dma((NR,)), dma((NR,)), dma((NR,)), dma((NR,)), dma((NR,))],
        compiler_params=pltpu.CompilerParams(collective_id=0, has_side_effects=True),
        name="exchange",
    )(send.reshape(NR, NC, SLOT_ROWS, TILE), xs)
    return recv, xc


def product_kernel(with_degree, rows_ref, cols_ref, own_rows_ref, own_cols_ref, x_ref, own_ref, slots_ref, *rest):
    if with_degree:
        part_ref, degree_out_ref, xt_ref, acc_ref, degree_ref = rest
    else:
        part_ref, xt_ref, acc_ref = rest
        degree_ref = None
    step = pl.program_id(0)
    ones = jnp.ones((8, TILE), BF)

    def run(terms):
        products = []
        for load, _, x_index, dims, valid in terms:
            tile = load()
            value = dot(xt_ref[x_index], tile, dims)
            sums = None
            if with_degree:
                scale = ones if valid is None else jnp.where(valid, ones, jnp.zeros_like(ones))
                sums = dot(scale, jnp.abs(tile), dims)[0:1]
            products.append((value, sums))
        for (_, target, _, _, _), (value, sums) in zip(terms, products):
            acc_ref[target] += value
            if with_degree:
                degree_ref[target] += sums

    @pl.when(step == 0)
    def _():
        acc_ref[...] = jnp.zeros_like(acc_ref)
        if with_degree:
            degree_ref[...] = jnp.zeros_like(degree_ref)

        def turn(q, carry):
            pair, j = q // 16, lax.rem(q, 16)
            block = x_ref[pl.ds(j * 8, 8), pair].reshape(TILE, TILE)
            xt_ref[pl.ds(q * 2, 2)] = block.T.reshape(2, K, TILE)
            return carry

        lax.fori_loop(0, 64, turn, 0)
        xt_ref[pl.ds(128, 2)] = jnp.zeros((2, K, TILE), BF)

        def own(i, carry):
            run([
                (functools.partial(lambda n: own_ref[n], i * 4 + u), own_rows_ref[i * 4 + u],
                 own_cols_ref[i * 4 + u], ((1,), (1,)), None)
                for u in range(4)
            ])
            return carry

        lax.fori_loop(0, OWN // 4, own, 0)

    def taken(i, carry):
        terms = []
        for u in range(2):
            for slot in range(CAP):
                source = i * 2 + u
                n = (step * 8 + source) * CAP + slot
                x_index = cols_ref[n]
                terms.append((
                    functools.partial(lambda s, k: slots_ref[s, pl.ds(k * TILE, TILE)], source, slot),
                    rows_ref[n], x_index, ((1,), (0,)), x_index < 128,
                ))
        run(terms)
        return carry

    lax.fori_loop(0, 4, taken, 0)

    @pl.when(step == pl.num_programs(0) - 1)
    def _():
        def flush(i, carry):
            part_ref[pl.ds(i * 8, 8)] = acc_ref[pl.ds(i * 8, 8)].astype(BF)
            return carry

        lax.fori_loop(0, ROWS_BLK // 8, flush, 0)
        if with_degree:
            degree_out_ref[...] = degree_ref[...].reshape(ROWS_BLK, TILE)


def product(with_degree, rows, cols, own_rows, own_cols, xc, own, slots):
    whole = lambda shape: pl.BlockSpec(shape, lambda i: (0,) * len(shape))
    out_shape = [jax.ShapeDtypeStruct((ROWS_BLK, K, TILE), BF)]
    out_specs = [whole((ROWS_BLK, K, TILE))]
    if with_degree:
        out_shape.append(jax.ShapeDtypeStruct((ROWS_BLK, TILE), F32))
        out_specs.append(whole((ROWS_BLK, TILE)))
    scratch = [pltpu.VMEM((130, K, TILE), BF), pltpu.VMEM((ROWS_BLK, K, TILE), F32)]
    if with_degree:
        scratch.append(pltpu.VMEM((ROWS_BLK, 1, TILE), F32))
    terms = DEV * CAP + OWN
    return pl.pallas_call(
        functools.partial(product_kernel, with_degree),
        grid=(DEV // 8,),
        out_shape=out_shape,
        in_specs=[SMEM, SMEM, SMEM, SMEM, whole((DEV, 4, 16, TILE)), whole((OWN, TILE, TILE)),
                  pl.BlockSpec((8, SLOT_ROWS, TILE), lambda i: (i, 0, 0))],
        out_specs=out_specs,
        scratch_shapes=scratch,
        compiler_params=pltpu.CompilerParams(vmem_limit_bytes=48 * MIB),
        cost_estimate=pl.CostEstimate(flops=terms * 2 * K * TILE * TILE, bytes_accessed=terms * TILE * TILE * 2, transcendentals=0),
        name="product",
    )(rows, cols, own_rows, own_cols, xc.reshape(DEV, 4, 16, TILE), own, slots.reshape(DEV, SLOT_ROWS, TILE))


def inverse_factor(gram):
    eye = (lax.broadcasted_iota(jnp.int32, (K, K), 0) == lax.broadcasted_iota(jnp.int32, (K, K), 1)).astype(F32)
    work = jnp.concatenate([gram, eye], axis=1)
    index = lax.broadcasted_iota(jnp.int32, (K, 1), 0)
    pivots = jnp.ones((K, 1), F32)
    for j in range(K):
        pivot = work[j:j + 1, j:j + 1]
        pivots = jnp.where(index == j, pivot, pivots)
        factor = jnp.where(index > j, work[:, j:j + 1] * (1.0 / pivot), 0.0)
        work = work - factor * work[j:j + 1, :]
    return lax.rsqrt(pivots) * work[:, K:]


def gram_pack(gram):
    return jnp.concatenate([gram[:K // 2], gram[K // 2:]], axis=1)


def gram_unpack(packed):
    return jnp.concatenate([packed[:, :K], packed[:, K:]], axis=0)


def normalize_kernel(first, last, part_ref, degree_in_ref, *rest):
    rest = list(rest)
    take = lambda count: [rest.pop(0) for _ in range(count)]
    gram_in_ref = None if first else rest.pop(0)
    if last:
        (z_ref,) = take(1)
    else:
        xc_ref, gram_ref = take(2)
    degree_ref = rest.pop(0) if first else degree_in_ref
    y_ref, a1_ref, r1_ref, a2_ref, g1_ref, g2_ref, g3_ref = take(7)
    s1_send, s1_recv, s2_send, s2_recv, g_send, g_recv = take(6)
    if first:
        dg_ref, dg_own, dg_send, dg_recv = take(4)
    if not last:
        xs_ref = rest.pop(0)
        sems = dict(zip(X_SEMS, rest))
    row = lax.axis_index("row")
    col = lax.axis_index("col")
    x, y = col // 4, lax.rem(col, 4)
    x_peer = lambda k: lax.rem(x + k, 4) * 4 + y
    y_peer = lambda k: x * 4 + lax.rem(y + k, 4)
    greet(row, col)

    for k in (1, 3, 2):
        remote(part_ref.at[lax.rem(x + k, 4), :, pl.ds(0, 8)], a1_ref.at[0, k - 1],
               s1_send.at[0, k - 1], s1_recv.at[0, k - 1], col=x_peer(k)).start()
        remote(part_ref.at[:, lax.rem(y + k, 4), pl.ds(8, 8)], a1_ref.at[1, k - 1],
               s1_send.at[1, k - 1], s1_recv.at[1, k - 1], col=y_peer(k)).start()
    if first:
        pltpu.make_async_copy(degree_in_ref.at[pl.ds(col * 16, 16)], dg_ref.at[col], dg_own).start()

        def send(k, carry):
            peer = col_peer(col, k)
            remote(degree_in_ref.at[pl.ds(peer * 16, 16)], dg_ref.at[col], dg_send, dg_recv, col=peer).start()
            return carry

        lax.fori_loop(1, NC, send, 0)
    else:
        inverse = inverse_factor(gram_unpack(gram_in_ref[...]))
    for h in range(2):
        for k in range(3):
            wait_bytes(a1_ref.at[h, k], s1_recv.at[h, k])
        for k in (1, 3, 2, 0):
            target = lax.rem((x if h else y) + k, 4)

            def add(b, carry):
                mine = part_ref[target, y, 8 + b] if h else part_ref[x, target, b]
                value = mine.astype(F32)
                for source in range(3):
                    value = value + a1_ref[h, source, target, b].astype(F32)
                if k:
                    r1_ref[h, k - 1, b] = value.astype(BF)
                else:
                    y_ref[h * 8 + b] = value
                return carry

            lax.fori_loop(0, 8, add, 0)
            if k:
                remote(r1_ref.at[h, k - 1], a2_ref.at[h, k - 1], s2_send.at[h, k - 1], s2_recv.at[h, k - 1],
                       col=x_peer(k) if h else y_peer(k)).start()
    if first:
        pltpu.make_async_copy(degree_in_ref.at[pl.ds(col * 16, 16)], dg_ref.at[col], dg_own).wait()
        wait_bytes(dg_ref.at[pl.ds(0, NC - 1)], dg_recv)
        degree = dg_ref[0]
        for k in range(1, NC):
            degree = degree + dg_ref[k]
        degree_ref[...] = 1.0 + degree
    for h in range(2):
        for k in range(3):
            wait_bytes(a2_ref.at[h, k], s2_recv.at[h, k])
        for b in range(8):
            value = y_ref[h * 8 + b]
            for k in range(3):
                value = value + a2_ref[h, k, b].astype(F32)
            value = value * (1.0 / degree_ref[h * 8 + b:h * 8 + b + 1])
            if not first:
                value = dot(inverse, value, ((1,), (0,)), lax.Precision.HIGHEST)
            y_ref[h * 8 + b] = value

    if not last:
        for pair in range(4):
            for part in range(2):
                both = jnp.concatenate([y_ref[pair * 4 + part], y_ref[pair * 4 + 2 + part]], axis=0).T
                xs_ref[part * 8:(part + 1) * 8, pair] = both.astype(BF).reshape(8, 16, TILE)
        x_first(row, col, xs_ref, xc_ref, sems)

    gram = jnp.zeros((K, K), F32)
    for b in range(16):
        block = y_ref[b]
        gram = gram + dot(block, block, ((1,), (1,)), lax.Precision.HIGHEST)

    def share(buffer, place, value, peers, base):
        buffer[place] = value
        for i, peer in enumerate(peers):
            remote(buffer.at[place], buffer.at[place], g_send.at[base + i], g_recv.at[base], **peer).start()

    def collect(buffer, count, base):
        wait_bytes(buffer.at[pl.ds(0, count - 1)], g_recv.at[base])
        total = buffer[0]
        for k in range(1, count):
            total = total + buffer[k]
        return total

    share(g1_ref, x, gram_pack(gram), [dict(col=x_peer(k)) for k in (1, 3, 2)], 0)
    if not last:
        x_second(row, col, xs_ref, xc_ref, sems)
    share(g2_ref, y, collect(g1_ref, 4, 0), [dict(col=y_peer(k)) for k in (1, 3, 2)], 3)
    share(g3_ref, row, collect(g2_ref, 4, 3), [dict(row=row_peer(row, dz, flip)) for dz, flip in ROW_ORDER], 6)
    if not last:
        x_third(row, col, xs_ref, xc_ref, sems)
    total = collect(g3_ref, NR, 6) * (1.0 / NODES)
    if last:
        final = inverse_factor(gram_unpack(total))
        for b in range(0, 16, 2):
            both = [dot(final, y_ref[b + i], ((1,), (0,)), lax.Precision.HIGHEST) for i in range(2)]
            both = jnp.concatenate(both, axis=0).T
            z_ref[b * TILE:(b + 1) * TILE] = both[:, :K]
            z_ref[(b + 1) * TILE:(b + 2) * TILE] = both[:, K:]
    else:
        gram_ref[...] = total
        x_finish(row, col, xs_ref, xc_ref, sems)
    for h in range(2):
        for k in range(3):
            wait_bytes(a1_ref.at[h, k], s1_send.at[h, k])
            wait_bytes(a2_ref.at[h, k], s2_send.at[h, k])
    if first:
        wait_bytes(dg_ref.at[pl.ds(0, NC - 1)], dg_send)
    for i in range(13):
        wait_bytes(g1_ref.at[0], g_send.at[i])


def normalize(first, last, part, degree, gram):
    dma = pltpu.SemaphoreType.DMA
    half = (K // 2, TILE)
    out_shape, out_specs = [], []
    if last:
        out_shape.append(jax.ShapeDtypeStruct((16 * TILE, K), F32))
        out_specs.append(VMEM)
    else:
        out_shape += [jax.ShapeDtypeStruct((NR, NC, 4, 16, TILE), BF), jax.ShapeDtypeStruct(half, F32)]
        out_specs += [ANY, VMEM]
    if first:
        out_shape.append(jax.ShapeDtypeStruct((16, TILE), F32))
        out_specs.append(VMEM)
    scratch = [
        pltpu.VMEM((16, K, TILE), F32), pltpu.VMEM((2, 3, 4, 8, K, TILE), BF),
        pltpu.VMEM((2, 3, 8, K, TILE), BF), pltpu.VMEM((2, 3, 8, K, TILE), BF),
        pltpu.VMEM((4,) + half, F32), pltpu.VMEM((4,) + half, F32), pltpu.VMEM((NR,) + half, F32),
        dma((2, 3)), dma((2, 3)), dma((2, 3)), dma((2, 3)), dma((13,)), dma((13,)),
    ]
    if first:
        scratch += [pltpu.VMEM((NC, 16, TILE), F32), dma, dma, dma]
    if not last:
        scratch += [pltpu.VMEM((NC, 4, 16, TILE), BF)] + x_sems()
    args = [part.reshape(4, 4, 16, K, TILE), degree] + ([] if first else [gram])
    return pl.pallas_call(
        functools.partial(normalize_kernel, first, last),
        out_shape=out_shape,
        in_specs=[VMEM, VMEM] + ([] if first else [VMEM]),
        out_specs=out_specs,
        scratch_shapes=scratch,
        compiler_params=pltpu.CompilerParams(
            collective_id=1 if first else (3 if last else 2), has_side_effects=True, vmem_limit_bytes=40 * MIB
        ),
        name="normalize",
    )(*args)


def block_index(block):
    return block // 32 * 32 + block % 16 * 2 + block // 16 % 2


def local(embed, tiles, tile_rows, tile_cols, chg_tiles, chg_rows, chg_cols):
    owners = chg_cols // 256 * NC + chg_rows // 128
    count = owners.shape[0]
    position = jnp.arange(count, dtype=jnp.int32)
    earlier = position[None, :] < position[:, None]
    rank = jnp.sum(jnp.logical_and(owners[:, None] == owners[None, :], earlier).astype(jnp.int32), axis=1)
    key = owners * CAP + rank
    hit = jnp.arange(DEV * CAP, dtype=jnp.int32)[:, None] == key[None, :]
    pick = jnp.sum(jnp.where(hit, position[None, :], 0), axis=1)
    code = jnp.sum(jnp.where(hit, (1 + chg_cols % 256 * 128 + block_index(chg_rows % 128))[None, :], 0), axis=1)
    slot_rows = jnp.where(code > 0, (code - 1) // 128, 0).reshape(DEV, CAP)
    slot_cols = jnp.where(code > 0, (code - 1) % 128, 128).reshape(DEV, CAP)
    meta = jnp.pad(jnp.concatenate([slot_rows, slot_cols], axis=1).astype(BF), ((0, 0), (0, TILE - 2 * CAP)))
    meta = jnp.broadcast_to(meta[:, None, :], (DEV, 16, TILE))
    send = pack(pick, chg_tiles, meta)
    xs = embed.reshape(4, 2, NC, 16, K).transpose(2, 0, 3, 1, 4).reshape(NC, 4, 16, TILE)
    slots, xc = exchange(send, xs)
    places = slots.reshape(DEV, SLOT_ROWS, TILE)[:, CAP * TILE, :2 * CAP].astype(jnp.int32)
    rows = places[:, :CAP].reshape(DEV * CAP)
    cols = places[:, CAP:].reshape(DEV * CAP)
    own_rows = tile_rows % 256
    own_cols = block_index(tile_cols % 128)
    part, degree = product(True, rows, cols, own_rows, own_cols, xc, tiles, slots)
    xc, gram, degree = normalize(True, False, part, degree, None)
    for iteration in range(1, ITERS):
        (part,) = product(False, rows, cols, own_rows, own_cols, xc, tiles, slots)
        last = iteration == ITERS - 1
        outs = normalize(False, last, part, degree, gram)
        if last:
            return outs[0]
        xc, gram = outs


def solution(mesh):
    placed = (
        P(("row", "col"), None),
        P(("row", "col"), None, None),
        P(("row", "col")),
        P(("row", "col")),
        P(("row", "col"), None, None),
        P(("row", "col")),
        P(("row", "col")),
    )
    return jax.shard_map(
        local, mesh=mesh, in_specs=placed, out_specs=P(("row", "col"), None), check_vma=False
    )
```

```python
import functools

import jax
import jax.numpy as jnp
from jax import lax
from jax.experimental import pallas as pl
from jax.experimental.pallas import tpu as pltpu
from jax.sharding import PartitionSpec as P

ITERS = 3
CAP = 3
K = 64
TILE = 128
NR = 8
NC = 16
DEV = NR * NC
ROWS_BLK = 256
SLOT_ROWS = CAP * TILE
X_BLOCKS = 130
OWN = 64
NODES = 262144
BF = jnp.bfloat16
F32 = jnp.float32
ANY = pl.BlockSpec(memory_space=pl.ANY)

VMEM = pl.BlockSpec(memory_space=pltpu.VMEM)
SMEM = pl.BlockSpec(memory_space=pltpu.SMEM)
MIB = 1024 * 1024
ROW_ORDER = ((1, 0), (3, 1), (2, 0), (1, 1), (3, 0), (2, 1), (0, 1))


def dot(a, b, dims, precision=None):
    return lax.dot_general(a, b, (dims, ((), ())), precision=precision, preferred_element_type=F32)


def greet(row, col):
    barrier = pltpu.get_barrier_semaphore()

    def cols(k, carry):
        pl.semaphore_signal(barrier, inc=1, device_id={"col": lax.rem(col + k, NC)}, device_id_type=pl.DeviceIdType.MESH)
        return carry

    def rows(k, carry):
        pl.semaphore_signal(barrier, inc=1, device_id={"row": lax.rem(row + k, NR)}, device_id_type=pl.DeviceIdType.MESH)
        return carry

    lax.fori_loop(1, NC, cols, 0)
    lax.fori_loop(1, NR, rows, 0)
    pl.semaphore_wait(barrier, NC + NR - 2)


def remote(src, dst, send_sem, recv_sem, **peer):
    return pltpu.make_async_remote_copy(
        src_ref=src, dst_ref=dst, send_sem=send_sem, recv_sem=recv_sem,
        device_id=peer, device_id_type=pl.DeviceIdType.MESH,
    )


def wait_bytes(ref, sem):
    pltpu.make_async_copy(ref, ref, sem).wait()


def col_peer(col, k):
    return lax.rem(col // 4 + k // 4, 4) * 4 + lax.rem(lax.rem(col, 4) + lax.rem(k, 4), 4)


def row_peer(row, dz, flip=0):
    return lax.rem(row // 2 + dz, 4) * 2 + lax.rem(row + flip, 2)


def x_first(row, col, xs, xc, sems):
    pltpu.make_async_copy(xs.at[col], xc.at[row, col], sems["x_own"]).start()

    def send(k, carry):
        peer = col_peer(col, k)
        remote(xs.at[peer], xc.at[row, col], sems["xa_send"], sems["xa_recv"], col=peer).start()
        return carry

    lax.fori_loop(1, NC, send, 0)


def x_second(row, col, xs, xc, sems):
    pltpu.make_async_copy(xs.at[col], xc.at[row, col], sems["x_own"]).wait()
    wait_bytes(xc.at[row, pl.ds(0, NC - 1)], sems["xa_recv"])
    for i, (dz, flip) in enumerate(((1, 0), (3, 0), (2, 0), (0, 1))):
        remote(xc.at[row], xc.at[row], sems["xb_send"].at[i], sems["xb_recv"].at[row], row=row_peer(row, dz, flip)).start()


def x_third(row, col, xs, xc, sems):
    for i, dz in enumerate((1, 3, 2)):
        source = row_peer(row, dz)
        wait_bytes(xc.at[source], sems["xb_recv"].at[source])
        remote(xc.at[source], xc.at[source], sems["xb_send"].at[4 + i], sems["xb_recv"].at[source], row=row_peer(row, 0, 1)).start()


def x_finish(row, col, xs, xc, xt, sems):
    xt[X_BLOCKS - 2:] = jnp.zeros((2, K, TILE), BF)
    for dz in range(4):
        turn(row_peer(row, dz), xc, xt)
    for dz in (0, 1, 3, 2):
        source = row_peer(row, dz, 1)
        wait_bytes(xc.at[source], sems["xb_recv"].at[source])
        turn(source, xc, xt)
    wait_bytes(xs.at[pl.ds(0, NC - 1)], sems["xa_send"])
    for i in range(7):
        wait_bytes(xc.at[row], sems["xb_send"].at[i])


def turn(source, xc, xt):
    for part in range(2):
        for pair in range(4):
            block = xc[source, part * 8:(part + 1) * 8, pair].reshape(TILE, TILE)
            xt[pl.ds((pair * 16 + source * 2 + part) * 2, 2)] = block.T.reshape(2, K, TILE)


X_SEMS = ("x_own", "xa_send", "xa_recv", "xb_send", "xb_recv")


def x_sems():
    dma = pltpu.SemaphoreType.DMA
    return [dma, dma, dma, dma((7,)), dma((NR,))]


def exchange_kernel(pick_ref, tiles_ref, own_ref, meta_ref, xs_ref,
                    recv_ref, mid_ref, own_out_ref, places_ref, xt_ref,
                    send_ref, xc_ref, meta_mid_ref, meta_next_ref, *sem_refs):
    sems = dict(zip(X_SEMS, sem_refs))
    a_send, a_recv, b_send, b_recv, m_send, m_recv, n_send, n_recv, own_sem = sem_refs[len(X_SEMS):]
    row = lax.axis_index("row")
    col = lax.axis_index("col")
    greet(row, col)
    x_first(row, col, xs_ref, xc_ref, sems)
    targets = [row_peer(row, dz, flip) for dz, flip in ROW_ORDER] + [row]

    def send_meta(k, carry):
        peer = col_peer(col, k)
        remote(meta_ref.at[peer], meta_mid_ref.at[col], m_send, m_recv, col=peer).start()
        return carry

    lax.fori_loop(1, NC, send_meta, 0)
    meta_mid_ref[col] = meta_ref[col]

    def first(step):
        target = targets[step]
        dst_ref = mid_ref if step < NR - 1 else recv_ref

        def fill(k, carry):
            peer = col_peer(col, k)
            for slot in range(CAP):
                send_ref[target, peer, slot * TILE:(slot + 1) * TILE] = tiles_ref[pick_ref[(target * NC + peer) * CAP + slot]]

            @pl.when(k > 0)
            def _():
                remote(send_ref.at[target, peer], dst_ref.at[target, col], a_send.at[step], a_recv.at[step], col=peer).start()

            return carry

        lax.fori_loop(0, NC, fill, 0)
        pltpu.make_async_copy(send_ref.at[target, col], dst_ref.at[target, col], own_sem.at[step]).start()

    first(0)
    x_second(row, col, xs_ref, xc_ref, sems)
    for step in range(1, NR):
        first(step)
    wait_bytes(meta_mid_ref.at[pl.ds(0, NC - 1)], m_recv)
    for c in range(NC):
        for r in range(NR):
            meta_next_ref[r, c:c + 1] = meta_mid_ref[c, r:r + 1]
    for step in range(NR - 1):
        remote(meta_next_ref.at[targets[step]], places_ref.at[row], n_send, n_recv, row=targets[step]).start()
    places_ref[row] = meta_next_ref[row]
    x_third(row, col, xs_ref, xc_ref, sems)

    def flip_own(i, carry):
        for u in range(4):
            own_out_ref[i * 4 + u] = own_ref[i * 4 + u].T
        return carry

    lax.fori_loop(0, OWN // 4, flip_own, 0)
    for step in range(NR - 1):
        target = targets[step]
        wait_bytes(mid_ref.at[target, pl.ds(0, NC - 1)], a_recv.at[step])
        pltpu.make_async_copy(send_ref.at[target, col], mid_ref.at[target, col], own_sem.at[step]).wait()
        remote(mid_ref.at[target], recv_ref.at[row], b_send.at[step], b_recv.at[row], row=target).start()
    x_finish(row, col, xs_ref, xc_ref, xt_ref, sems)
    wait_bytes(recv_ref.at[row, pl.ds(0, NC - 1)], a_recv.at[NR - 1])
    pltpu.make_async_copy(send_ref.at[row, col], recv_ref.at[row, col], own_sem.at[NR - 1]).wait()
    wait_bytes(meta_mid_ref.at[pl.ds(0, NC - 1)], m_send)
    wait_bytes(places_ref.at[pl.ds(0, NR - 1)], n_send)
    wait_bytes(places_ref.at[pl.ds(0, NR - 1)], n_recv)
    for step in range(NR):
        wait_bytes(send_ref.at[0, pl.ds(0, NC - 1)], a_send.at[step])
    for step in range(NR - 1):
        source = targets[step]
        wait_bytes(mid_ref.at[source], b_send.at[step])
        wait_bytes(recv_ref.at[source], b_recv.at[source])


def exchange(pick, chg_tiles, own, meta, xs):
    dma = pltpu.SemaphoreType.DMA
    slots = (NR, NC, SLOT_ROWS, TILE)
    recv, _, own, places, xt = pl.pallas_call(
        exchange_kernel,
        out_shape=(jax.ShapeDtypeStruct(slots, BF), jax.ShapeDtypeStruct(slots, BF), pltpu.VMEM((OWN, TILE, TILE), BF),
                   jax.ShapeDtypeStruct((NR, NC, TILE), F32), pltpu.VMEM((X_BLOCKS, K, TILE), BF)),
        in_specs=[SMEM, VMEM, VMEM, VMEM, VMEM],
        out_specs=(ANY, ANY, VMEM, VMEM, VMEM),
        scratch_shapes=[
            pltpu.VMEM(slots, BF), pltpu.VMEM((NR, NC, 4, 16, TILE), BF),
            pltpu.VMEM((NC, NR, TILE), F32), pltpu.VMEM((NR, NC, TILE), F32),
        ] + x_sems() + [dma((NR,)), dma((NR,)), dma((NR,)), dma((NR,)), dma, dma, dma, dma, dma((NR,))],
        compiler_params=pltpu.CompilerParams(collective_id=0, has_side_effects=True, vmem_limit_bytes=42 * MIB),
        name="exchange",
    )(pick, chg_tiles, own, meta, xs)
    return recv, own, places, xt


def product_kernel(with_degree, rows_ref, cols_ref, own_rows_ref, own_cols_ref, xt_ref, own_ref, slots_in_ref, acc_ref, *rest):
    slots_ref, slot_sem = rest[-2:]
    loads = [
        pltpu.make_async_copy(slots_in_ref.at[pl.ds(i * 16, 16)], slots_ref.at[pl.ds(i * 16, 16)], slot_sem.at[i])
        for i in range(DEV // 16)
    ]
    for load in loads:
        load.start()
    ones = jnp.ones((8, TILE), BF)
    plain = ((1,), (0,))
    if with_degree:
        degree_out_ref, degree_ref = rest[:2]
        degree_ref[...] = jnp.zeros_like(degree_ref)

    def clear(i, carry):
        acc_ref[pl.ds(i * 8, 8)] = jnp.zeros((8, K, TILE), F32)
        return carry

    lax.fori_loop(0, ROWS_BLK // 8, clear, 0)

    def run(tiles, rows, cols):
        values = [dot(xt_ref[col], tile, plain) for tile, col in zip(tiles, cols)]
        sums = []
        if with_degree:
            sums = [
                dot(jnp.where(col < 128, ones, jnp.zeros_like(ones)), jnp.abs(tile), plain)[0:1]
                for tile, col in zip(tiles, cols)
            ]
        for row, value in zip(rows, values):
            acc_ref[row] += value
        for row, value in zip(rows, sums):
            degree_ref[row] += value

    def own(i, carry):
        places = [i * 4 + u for u in range(4)]
        run([own_ref[n] for n in places], [own_rows_ref[n] for n in places], [own_cols_ref[n] for n in places])
        return carry

    def taken(i, carry):
        for u in range(2):
            source = i * 2 + u
            places = [source * CAP + slot for slot in range(CAP)]
            run([slots_ref[source, slot * TILE:(slot + 1) * TILE] for slot in range(CAP)],
                [rows_ref[n] for n in places], [cols_ref[n] for n in places])
        return carry

    lax.fori_loop(0, OWN // 4, own, 0)
    for i, load in enumerate(loads):
        load.wait()
        lax.fori_loop(i * 8, i * 8 + 8, taken, 0)
    if with_degree:
        degree_out_ref[...] = degree_ref[...].reshape(ROWS_BLK, TILE)


def product(with_degree, rows, cols, own_rows, own_cols, xt, own, slots):
    out_shape = [pltpu.VMEM((ROWS_BLK, K, TILE), F32)]
    if with_degree:
        out_shape.append(jax.ShapeDtypeStruct((ROWS_BLK, TILE), F32))
    terms = DEV * CAP + OWN
    return pl.pallas_call(
        functools.partial(product_kernel, with_degree),
        out_shape=out_shape,
        in_specs=[SMEM, SMEM, SMEM, SMEM, VMEM, VMEM, ANY],
        out_specs=[VMEM] * len(out_shape),
        scratch_shapes=([pltpu.VMEM((ROWS_BLK, 1, TILE), F32)] if with_degree else []) + [
            pltpu.VMEM((DEV, SLOT_ROWS, TILE), BF), pltpu.SemaphoreType.DMA((DEV // 16,)),
        ],
        compiler_params=pltpu.CompilerParams(vmem_limit_bytes=40 * MIB),
        cost_estimate=pl.CostEstimate(flops=terms * 2 * K * TILE * TILE, bytes_accessed=terms * TILE * TILE * 2, transcendentals=0),
        name="product",
    )(rows, cols, own_rows, own_cols, xt, own, slots.reshape(DEV, SLOT_ROWS, TILE))


def inverse_factor(gram):
    eye = (lax.broadcasted_iota(jnp.int32, (K, K), 0) == lax.broadcasted_iota(jnp.int32, (K, K), 1)).astype(F32)
    work = jnp.concatenate([gram, eye], axis=1)
    index = lax.broadcasted_iota(jnp.int32, (K, 1), 0)
    pivots = jnp.ones((K, 1), F32)
    for j in range(K):
        pivot = work[j:j + 1, j:j + 1]
        pivots = jnp.where(index == j, pivot, pivots)
        factor = jnp.where(index > j, work[:, j:j + 1] * (1.0 / pivot), 0.0)
        work = work - factor * work[j:j + 1, :]
    return lax.rsqrt(pivots) * work[:, K:]


def gram_pack(gram):
    return jnp.concatenate([gram[:K // 2], gram[K // 2:]], axis=1)


def gram_unpack(packed):
    return jnp.concatenate([packed[:, :K], packed[:, K:]], axis=0)


def normalize_kernel(first, last, part_ref, degree_in_ref, *rest):
    rest = list(rest)
    take = lambda count: [rest.pop(0) for _ in range(count)]
    gram_in_ref = None if first else rest.pop(0)
    if last:
        (z_ref,) = take(1)
    else:
        xt_ref, gram_ref = take(2)
    degree_ref = rest.pop(0) if first else degree_in_ref
    y_ref, s1_ref, a1_ref, r1_ref, a2_ref, g1_ref, g2_ref, g3_ref = take(8)
    s1_send, s1_recv, s2_send, s2_recv, g_send, g_recv = take(6)
    if first:
        dg_ref, dg_own, dg_send, dg_recv = take(4)
    if not last:
        xs_ref, xc_ref = take(2)
        sems = dict(zip(X_SEMS, rest))
    row = lax.axis_index("row")
    col = lax.axis_index("col")
    x, y = col // 4, lax.rem(col, 4)
    x_peer = lambda k: lax.rem(x + k, 4) * 4 + y
    y_peer = lambda k: x * 4 + lax.rem(y + k, 4)
    greet(row, col)

    for k in (1, 3, 2):
        for h in range(2):
            target = lax.rem((y if h else x) + k, 4)

            def narrow(other, carry):
                chunk = part_ref[other, target, 8:16] if h else part_ref[target, other, 0:8]
                s1_ref[h, k - 1, other] = chunk.astype(BF)
                return carry

            lax.fori_loop(0, 4, narrow, 0)
            remote(s1_ref.at[h, k - 1], a1_ref.at[h, k - 1], s1_send.at[h, k - 1], s1_recv.at[h, k - 1],
                   col=y_peer(k) if h else x_peer(k)).start()
    if first:
        pltpu.make_async_copy(degree_in_ref.at[pl.ds(col * 16, 16)], dg_ref.at[col], dg_own).start()

        def send(k, carry):
            peer = col_peer(col, k)
            remote(degree_in_ref.at[pl.ds(peer * 16, 16)], dg_ref.at[col], dg_send, dg_recv, col=peer).start()
            return carry

        lax.fori_loop(1, NC, send, 0)
    else:
        inverse = inverse_factor(gram_unpack(gram_in_ref[...]))
    for h in range(2):
        for k in range(3):
            wait_bytes(a1_ref.at[h, k], s1_recv.at[h, k])
        for k in (1, 3, 2, 0):
            target = lax.rem((x if h else y) + k, 4)

            def add(b, carry):
                mine = part_ref[target, y, 8 + b] if h else part_ref[x, target, b]
                value = mine
                for source in range(3):
                    value = value + a1_ref[h, source, target, b].astype(F32)
                if k:
                    r1_ref[h, k - 1, b] = value.astype(BF)
                else:
                    y_ref[h * 8 + b] = value
                return carry

            lax.fori_loop(0, 8, add, 0)
            if k:
                remote(r1_ref.at[h, k - 1], a2_ref.at[h, k - 1], s2_send.at[h, k - 1], s2_recv.at[h, k - 1],
                       col=x_peer(k) if h else y_peer(k)).start()
    if first:
        pltpu.make_async_copy(degree_in_ref.at[pl.ds(col * 16, 16)], dg_ref.at[col], dg_own).wait()
        wait_bytes(dg_ref.at[pl.ds(0, NC - 1)], dg_recv)
        degree = dg_ref[0]
        for k in range(1, NC):
            degree = degree + dg_ref[k]
        degree_ref[...] = 1.0 + degree
    for h in range(2):
        for k in range(3):
            wait_bytes(a2_ref.at[h, k], s2_recv.at[h, k])
        for b in range(8):
            value = y_ref[h * 8 + b]
            for k in range(3):
                value = value + a2_ref[h, k, b].astype(F32)
            value = value * (1.0 / degree_ref[h * 8 + b:h * 8 + b + 1])
            if not first:
                value = dot(inverse, value, ((1,), (0,)), lax.Precision.HIGHEST)
            y_ref[h * 8 + b] = value

    if not last:
        for pair in range(4):
            for part in range(2):
                both = jnp.concatenate([y_ref[pair * 4 + part], y_ref[pair * 4 + 2 + part]], axis=0).T
                xs_ref[part * 8:(part + 1) * 8, pair] = both.astype(BF).reshape(8, 16, TILE)
        x_first(row, col, xs_ref, xc_ref, sems)

    gram = jnp.zeros((K, K), F32)
    for b in range(16):
        block = y_ref[b]
        gram = gram + dot(block, block, ((1,), (1,)), lax.Precision.HIGHEST)

    def share(buffer, place, value, peers, base):
        buffer[place] = value
        for i, peer in enumerate(peers):
            remote(buffer.at[place], buffer.at[place], g_send.at[base + i], g_recv.at[base], **peer).start()

    def collect(buffer, count, base):
        wait_bytes(buffer.at[pl.ds(0, count - 1)], g_recv.at[base])
        total = buffer[0]
        for k in range(1, count):
            total = total + buffer[k]
        return total

    share(g1_ref, x, gram_pack(gram), [dict(col=x_peer(k)) for k in (1, 3, 2)], 0)
    if not last:
        x_second(row, col, xs_ref, xc_ref, sems)
    share(g2_ref, y, collect(g1_ref, 4, 0), [dict(col=y_peer(k)) for k in (1, 3, 2)], 3)
    share(g3_ref, row, collect(g2_ref, 4, 3), [dict(row=row_peer(row, dz, flip)) for dz, flip in ROW_ORDER], 6)
    if not last:
        x_third(row, col, xs_ref, xc_ref, sems)
    total = collect(g3_ref, NR, 6) * (1.0 / NODES)
    if last:
        final = inverse_factor(gram_unpack(total))
        for b in range(0, 16, 2):
            both = [dot(final, y_ref[b + i], ((1,), (0,)), lax.Precision.HIGHEST) for i in range(2)]
            both = jnp.concatenate(both, axis=0).T
            z_ref[b * TILE:(b + 1) * TILE] = both[:, :K]
            z_ref[(b + 1) * TILE:(b + 2) * TILE] = both[:, K:]
    else:
        gram_ref[...] = total
        x_finish(row, col, xs_ref, xc_ref, xt_ref, sems)
    for h in range(2):
        for k in range(3):
            wait_bytes(a1_ref.at[h, k], s1_send.at[h, k])
            wait_bytes(a2_ref.at[h, k], s2_send.at[h, k])
    if first:
        wait_bytes(dg_ref.at[pl.ds(0, NC - 1)], dg_send)
    for i in range(13):
        wait_bytes(g1_ref.at[0], g_send.at[i])


def normalize(first, last, part, degree, gram):
    dma = pltpu.SemaphoreType.DMA
    half = (K // 2, TILE)
    out_shape, out_specs = [], []
    if last:
        out_shape.append(jax.ShapeDtypeStruct((16 * TILE, K), F32))
        out_specs.append(VMEM)
    else:
        out_shape += [pltpu.VMEM((X_BLOCKS, K, TILE), BF), jax.ShapeDtypeStruct(half, F32)]
        out_specs += [VMEM, VMEM]
    if first:
        out_shape.append(jax.ShapeDtypeStruct((16, TILE), F32))
        out_specs.append(VMEM)
    scratch = [
        pltpu.VMEM((16, K, TILE), F32), pltpu.VMEM((2, 3, 4, 8, K, TILE), BF), pltpu.VMEM((2, 3, 4, 8, K, TILE), BF),
        pltpu.VMEM((2, 3, 8, K, TILE), BF), pltpu.VMEM((2, 3, 8, K, TILE), BF),
        pltpu.VMEM((4,) + half, F32), pltpu.VMEM((4,) + half, F32), pltpu.VMEM((NR,) + half, F32),
        dma((2, 3)), dma((2, 3)), dma((2, 3)), dma((2, 3)), dma((13,)), dma((13,)),
    ]
    if first:
        scratch += [pltpu.VMEM((NC, 16, TILE), F32), dma, dma, dma]
    if not last:
        scratch += [pltpu.VMEM((NC, 4, 16, TILE), BF), pltpu.VMEM((NR, NC, 4, 16, TILE), BF)] + x_sems()
    args = [part.reshape(4, 4, 16, K, TILE), degree] + ([] if first else [gram])
    return pl.pallas_call(
        functools.partial(normalize_kernel, first, last),
        out_shape=out_shape,
        in_specs=[VMEM, VMEM] + ([] if first else [VMEM]),
        out_specs=out_specs,
        scratch_shapes=scratch,
        compiler_params=pltpu.CompilerParams(
            collective_id=1 if first else (3 if last else 2), has_side_effects=True, vmem_limit_bytes=16 * MIB
        ),
        name="normalize",
    )(*args)


def block_index(block):
    return block // 32 * 32 + block % 16 * 2 + block // 16 % 2


def local(embed, tiles, tile_rows, tile_cols, chg_tiles, chg_rows, chg_cols):
    owners = chg_cols // 256 * NC + chg_rows // 128
    count = owners.shape[0]
    position = jnp.arange(count, dtype=jnp.int32)
    earlier = position[None, :] < position[:, None]
    rank = jnp.sum(jnp.logical_and(owners[:, None] == owners[None, :], earlier).astype(jnp.int32), axis=1)
    key = owners * CAP + rank
    hit = jnp.arange(DEV * CAP, dtype=jnp.int32)[:, None] == key[None, :]
    pick = jnp.sum(jnp.where(hit, position[None, :], 0), axis=1)
    code = jnp.sum(jnp.where(hit, (1 + chg_cols % 256 * 128 + block_index(chg_rows % 128))[None, :], 0), axis=1)
    slot_rows = jnp.where(code > 0, (code - 1) // 128, 0).reshape(DEV, CAP)
    slot_cols = jnp.where(code > 0, (code - 1) % 128, 128).reshape(DEV, CAP)
    meta = jnp.concatenate([slot_rows, slot_cols], axis=1).reshape(NR, NC, 2 * CAP).transpose(1, 0, 2)
    meta = jnp.pad(meta.astype(F32), ((0, 0), (0, 0), (0, TILE - 2 * CAP)))
    xs = embed.reshape(4, 2, NC, 16, K).transpose(2, 0, 3, 1, 4).reshape(NC, 4, 16, TILE)
    slots, tiles, places, xc = exchange(pick, chg_tiles, tiles, meta, xs)
    places = places.reshape(DEV, TILE)[:, :2 * CAP].astype(jnp.int32)
    rows = places[:, :CAP].reshape(DEV * CAP)
    cols = places[:, CAP:].reshape(DEV * CAP)
    own_rows = tile_rows % 256
    own_cols = block_index(tile_cols % 128)
    part, degree = product(True, rows, cols, own_rows, own_cols, xc, tiles, slots)
    xc, gram, degree = normalize(True, False, part, degree, None)
    for iteration in range(1, ITERS):
        (part,) = product(False, rows, cols, own_rows, own_cols, xc, tiles, slots)
        last = iteration == ITERS - 1
        outs = normalize(False, last, part, degree, gram)
        if last:
            return outs[0]
        xc, gram = outs


def solution(mesh):
    placed = (
        P(("row", "col"), None),
        P(("row", "col"), None, None),
        P(("row", "col")),
        P(("row", "col")),
        P(("row", "col"), None, None),
        P(("row", "col")),
        P(("row", "col")),
    )
    return jax.shard_map(
        local, mesh=mesh, in_specs=placed, out_specs=P(("row", "col"), None), check_vma=False
    )
```

```python
import functools

import jax
import jax.numpy as jnp
from jax import lax
from jax.experimental import pallas as pl
from jax.experimental.pallas import tpu as pltpu
from jax.sharding import PartitionSpec as P

ITERS = 3
CAP = 3
K = 64
TILE = 128
NR = 8
NC = 16
DEV = NR * NC
ROWS_BLK = 256
SLOT_ROWS = CAP * TILE
X_BLOCKS = 130
OWN = 64
NODES = 262144
BF = jnp.bfloat16
F32 = jnp.float32
ANY = pl.BlockSpec(memory_space=pl.ANY)

VMEM = pl.BlockSpec(memory_space=pltpu.VMEM)
SMEM = pl.BlockSpec(memory_space=pltpu.SMEM)
MIB = 1024 * 1024
ROW_ORDER = ((1, 0), (3, 1), (2, 0), (1, 1), (3, 0), (2, 1), (0, 1))


def dot(a, b, dims, precision=None):
    return lax.dot_general(a, b, (dims, ((), ())), precision=precision, preferred_element_type=F32)


def greet(row, col):
    barrier = pltpu.get_barrier_semaphore()

    def cols(k, carry):
        pl.semaphore_signal(barrier, inc=1, device_id={"col": lax.rem(col + k, NC)}, device_id_type=pl.DeviceIdType.MESH)
        return carry

    def rows(k, carry):
        pl.semaphore_signal(barrier, inc=1, device_id={"row": lax.rem(row + k, NR)}, device_id_type=pl.DeviceIdType.MESH)
        return carry

    lax.fori_loop(1, NC, cols, 0)
    lax.fori_loop(1, NR, rows, 0)
    pl.semaphore_wait(barrier, NC + NR - 2)


def remote(src, dst, send_sem, recv_sem, **peer):
    return pltpu.make_async_remote_copy(
        src_ref=src, dst_ref=dst, send_sem=send_sem, recv_sem=recv_sem,
        device_id=peer, device_id_type=pl.DeviceIdType.MESH,
    )


def wait_bytes(ref, sem):
    pltpu.make_async_copy(ref, ref, sem).wait()


def col_peer(col, k):
    return lax.rem(col // 4 + k // 4, 4) * 4 + lax.rem(lax.rem(col, 4) + lax.rem(k, 4), 4)


def row_peer(row, dz, flip=0):
    return lax.rem(row // 2 + dz, 4) * 2 + lax.rem(row + flip, 2)


def x_first(row, col, xs, xc, sems):
    pltpu.make_async_copy(xs.at[col], xc.at[row, col], sems["x_own"]).start()

    def send(k, carry):
        peer = col_peer(col, k)
        remote(xs.at[peer], xc.at[row, col], sems["xa_send"], sems["xa_recv"], col=peer).start()
        return carry

    lax.fori_loop(1, NC, send, 0)


def x_second(row, col, xs, xc, sems):
    pltpu.make_async_copy(xs.at[col], xc.at[row, col], sems["x_own"]).wait()
    wait_bytes(xc.at[row, pl.ds(0, NC - 1)], sems["xa_recv"])
    for i, (dz, flip) in enumerate(((1, 0), (3, 0), (2, 0), (0, 1))):
        remote(xc.at[row], xc.at[row], sems["xb_send"].at[i], sems["xb_recv"].at[row], row=row_peer(row, dz, flip)).start()


def x_third(row, col, xs, xc, sems):
    for i, dz in enumerate((1, 3, 2)):
        source = row_peer(row, dz)
        wait_bytes(xc.at[source], sems["xb_recv"].at[source])
        remote(xc.at[source], xc.at[source], sems["xb_send"].at[4 + i], sems["xb_recv"].at[source], row=row_peer(row, 0, 1)).start()


def x_finish(row, col, xs, xc, xt, sems):
    xt[X_BLOCKS - 2:] = jnp.zeros((2, K, TILE), BF)
    for dz in range(4):
        turn(row_peer(row, dz), xc, xt)
    for dz in (0, 1, 3, 2):
        source = row_peer(row, dz, 1)
        wait_bytes(xc.at[source], sems["xb_recv"].at[source])
        turn(source, xc, xt)
    wait_bytes(xs.at[pl.ds(0, NC - 1)], sems["xa_send"])
    for i in range(7):
        wait_bytes(xc.at[row], sems["xb_send"].at[i])


def turn(source, xc, xt):
    for part in range(2):
        for pair in range(4):
            block = xc[source, part * 8:(part + 1) * 8, pair].reshape(TILE, TILE)
            xt[pl.ds((pair * 16 + source * 2 + part) * 2, 2)] = block.T.reshape(2, K, TILE)


X_SEMS = ("x_own", "xa_send", "xa_recv", "xb_send", "xb_recv")


def x_sems():
    dma = pltpu.SemaphoreType.DMA
    return [dma, dma, dma, dma((7,)), dma((NR,))]


def exchange_kernel(pick_ref, tiles_ref, own_ref, meta_ref, xs_ref,
                    recv_ref, mid_ref, own_out_ref, places_ref, xt_ref,
                    send_ref, xc_ref, meta_mid_ref, meta_next_ref, *sem_refs):
    sems = dict(zip(X_SEMS, sem_refs))
    a_send, a_recv, b_send, b_recv, m_send, m_recv, n_send, n_recv, own_sem = sem_refs[len(X_SEMS):]
    row = lax.axis_index("row")
    col = lax.axis_index("col")
    greet(row, col)
    x_first(row, col, xs_ref, xc_ref, sems)
    targets = [row_peer(row, dz, flip) for dz, flip in ROW_ORDER] + [row]

    def send_meta(k, carry):
        peer = col_peer(col, k)
        remote(meta_ref.at[peer], meta_mid_ref.at[col], m_send, m_recv, col=peer).start()
        return carry

    lax.fori_loop(1, NC, send_meta, 0)
    meta_mid_ref[col] = meta_ref[col]

    def first(step):
        target = targets[step]
        dst_ref = mid_ref if step < NR - 1 else recv_ref

        def fill(k, carry):
            peer = col_peer(col, k)
            for slot in range(CAP):
                send_ref[target, peer, slot * TILE:(slot + 1) * TILE] = tiles_ref[pick_ref[(target * NC + peer) * CAP + slot]]

            @pl.when(k > 0)
            def _():
                remote(send_ref.at[target, peer], dst_ref.at[target, col], a_send.at[step], a_recv.at[step], col=peer).start()

            return carry

        lax.fori_loop(0, NC, fill, 0)
        pltpu.make_async_copy(send_ref.at[target, col], dst_ref.at[target, col], own_sem.at[step]).start()

    first(0)
    x_second(row, col, xs_ref, xc_ref, sems)
    for step in range(1, NR):
        first(step)
    wait_bytes(meta_mid_ref.at[pl.ds(0, NC - 1)], m_recv)
    for c in range(NC):
        for r in range(NR):
            meta_next_ref[r, c:c + 1] = meta_mid_ref[c, r:r + 1]
    for step in range(NR - 1):
        remote(meta_next_ref.at[targets[step]], places_ref.at[row], n_send, n_recv, row=targets[step]).start()
    places_ref[row] = meta_next_ref[row]
    x_third(row, col, xs_ref, xc_ref, sems)

    def flip_own(i, carry):
        for u in range(4):
            own_out_ref[i * 4 + u] = own_ref[i * 4 + u].T
        return carry

    lax.fori_loop(0, OWN // 4, flip_own, 0)
    for step in range(NR - 1):
        target = targets[step]
        wait_bytes(mid_ref.at[target, pl.ds(0, NC - 1)], a_recv.at[step])
        pltpu.make_async_copy(send_ref.at[target, col], mid_ref.at[target, col], own_sem.at[step]).wait()
        remote(mid_ref.at[target], recv_ref.at[row], b_send.at[step], b_recv.at[row], row=target).start()
    x_finish(row, col, xs_ref, xc_ref, xt_ref, sems)
    wait_bytes(recv_ref.at[row, pl.ds(0, NC - 1)], a_recv.at[NR - 1])
    pltpu.make_async_copy(send_ref.at[row, col], recv_ref.at[row, col], own_sem.at[NR - 1]).wait()
    wait_bytes(meta_mid_ref.at[pl.ds(0, NC - 1)], m_send)
    wait_bytes(places_ref.at[pl.ds(0, NR - 1)], n_send)
    wait_bytes(places_ref.at[pl.ds(0, NR - 1)], n_recv)
    for step in range(NR):
        wait_bytes(send_ref.at[0, pl.ds(0, NC - 1)], a_send.at[step])
    for step in range(NR - 1):
        source = targets[step]
        wait_bytes(mid_ref.at[source], b_send.at[step])
        wait_bytes(recv_ref.at[source], b_recv.at[source])


def exchange(pick, chg_tiles, own, meta, xs):
    dma = pltpu.SemaphoreType.DMA
    slots = (NR, NC, SLOT_ROWS, TILE)
    recv, _, own, places, xt = pl.pallas_call(
        exchange_kernel,
        out_shape=(jax.ShapeDtypeStruct(slots, BF), jax.ShapeDtypeStruct(slots, BF), pltpu.VMEM((OWN, TILE, TILE), BF),
                   jax.ShapeDtypeStruct((NR, NC, TILE), F32), pltpu.VMEM((X_BLOCKS, K, TILE), BF)),
        in_specs=[SMEM, VMEM, VMEM, VMEM, VMEM],
        out_specs=(ANY, ANY, VMEM, VMEM, VMEM),
        scratch_shapes=[
            pltpu.VMEM(slots, BF), pltpu.VMEM((NR, NC, 4, 16, TILE), BF),
            pltpu.VMEM((NC, NR, TILE), F32), pltpu.VMEM((NR, NC, TILE), F32),
        ] + x_sems() + [dma((NR,)), dma((NR,)), dma((NR,)), dma((NR,)), dma, dma, dma, dma, dma((NR,))],
        compiler_params=pltpu.CompilerParams(collective_id=0, has_side_effects=True, vmem_limit_bytes=42 * MIB),
        name="exchange",
    )(pick, chg_tiles, own, meta, xs)
    return recv, own, places, xt


def product_kernel(with_degree, rows_ref, cols_ref, own_rows_ref, own_cols_ref, xt_ref, own_ref, slots_in_ref, acc_ref, *rest):
    slots_ref, slot_sem = rest[-2:]
    loads = [
        pltpu.make_async_copy(slots_in_ref.at[pl.ds(i * 16, 16)], slots_ref.at[pl.ds(i * 16, 16)], slot_sem.at[i])
        for i in range(DEV // 16)
    ]
    for load in loads:
        load.start()
    ones = jnp.ones((8, TILE), BF)
    plain = ((1,), (0,))
    if with_degree:
        degree_out_ref, degree_ref = rest[:2]
        degree_ref[...] = jnp.zeros_like(degree_ref)

    def clear(i, carry):
        acc_ref[pl.ds(i * 8, 8)] = jnp.zeros((8, K, TILE), F32)
        return carry

    lax.fori_loop(0, ROWS_BLK // 8, clear, 0)

    def run(tiles, rows, cols):
        values = [dot(xt_ref[col], tile, plain) for tile, col in zip(tiles, cols)]
        sums = []
        if with_degree:
            sums = [
                dot(jnp.where(col < 128, ones, jnp.zeros_like(ones)), jnp.abs(tile), plain)[0:1]
                for tile, col in zip(tiles, cols)
            ]
        for row, value in zip(rows, values):
            acc_ref[row] += value
        for row, value in zip(rows, sums):
            degree_ref[row] += value

    def own(i, carry):
        places = [i * 16 + u for u in range(16)]
        run([own_ref[n] for n in places], [own_rows_ref[n] for n in places], [own_cols_ref[n] for n in places])
        return carry

    def taken(i, carry):
        sources = [i * 16 + u for u in range(16)]
        places = [source * CAP + slot for source in sources for slot in range(CAP)]
        run([slots_ref[source, slot * TILE:(slot + 1) * TILE] for source in sources for slot in range(CAP)],
            [rows_ref[n] for n in places], [cols_ref[n] for n in places])
        return carry

    lax.fori_loop(0, OWN // 16, own, 0)
    for i, load in enumerate(loads):
        load.wait()
        lax.fori_loop(i, i + 1, taken, 0)
    if with_degree:
        degree_out_ref[...] = degree_ref[...].reshape(ROWS_BLK, TILE)


def product(with_degree, rows, cols, own_rows, own_cols, xt, own, slots):
    out_shape = [pltpu.VMEM((ROWS_BLK, K, TILE), F32)]
    if with_degree:
        out_shape.append(jax.ShapeDtypeStruct((ROWS_BLK, TILE), F32))
    terms = DEV * CAP + OWN
    return pl.pallas_call(
        functools.partial(product_kernel, with_degree),
        out_shape=out_shape,
        in_specs=[SMEM, SMEM, SMEM, SMEM, VMEM, VMEM, ANY],
        out_specs=[VMEM] * len(out_shape),
        scratch_shapes=([pltpu.VMEM((ROWS_BLK, 1, TILE), F32)] if with_degree else []) + [
            pltpu.VMEM((DEV, SLOT_ROWS, TILE), BF), pltpu.SemaphoreType.DMA((DEV // 16,)),
        ],
        compiler_params=pltpu.CompilerParams(vmem_limit_bytes=40 * MIB),
        cost_estimate=pl.CostEstimate(flops=terms * 2 * K * TILE * TILE, bytes_accessed=terms * TILE * TILE * 2, transcendentals=0),
        name="product",
    )(rows, cols, own_rows, own_cols, xt, own, slots.reshape(DEV, SLOT_ROWS, TILE))


def inverse_factor(gram):
    eye = (lax.broadcasted_iota(jnp.int32, (K, K), 0) == lax.broadcasted_iota(jnp.int32, (K, K), 1)).astype(F32)
    work = jnp.concatenate([gram, eye], axis=1)
    index = lax.broadcasted_iota(jnp.int32, (K, 1), 0)
    pivots = jnp.ones((K, 1), F32)
    for j in range(K):
        pivot = work[j:j + 1, j:j + 1]
        pivots = jnp.where(index == j, pivot, pivots)
        factor = jnp.where(index > j, work[:, j:j + 1] * (1.0 / pivot), 0.0)
        work = work - factor * work[j:j + 1, :]
    return lax.rsqrt(pivots) * work[:, K:]


def gram_pack(gram):
    return jnp.concatenate([gram[:K // 2], gram[K // 2:]], axis=1)


def gram_unpack(packed):
    return jnp.concatenate([packed[:, :K], packed[:, K:]], axis=0)


def normalize_kernel(first, last, part_ref, degree_in_ref, *rest):
    rest = list(rest)
    take = lambda count: [rest.pop(0) for _ in range(count)]
    gram_in_ref = None if first else rest.pop(0)
    if last:
        (z_ref,) = take(1)
    else:
        xt_ref, gram_ref = take(2)
    degree_ref = rest.pop(0) if first else degree_in_ref
    y_ref, s1_ref, a1_ref, s2_ref, a2_ref, v_ref, g1_ref, g2_ref, g3_ref = take(9)
    s1_send, s1_recv, s2_send, s2_recv, g_send, g_recv = take(6)
    if first:
        dg_ref, dg_own, dg_send, dg_recv = take(4)
    if not last:
        xs_ref, xc_ref = take(2)
        sems = dict(zip(X_SEMS, rest))
    row = lax.axis_index("row")
    col = lax.axis_index("col")
    x, y = col // 4, lax.rem(col, 4)
    x_peer = lambda k: lax.rem(x + k, 4) * 4 + y
    y_peer = lambda k: x * 4 + lax.rem(y + k, 4)
    greet(row, col)

    ways = ((1, 3) * 3)

    def ring(stage, h, message):
        along_x = (h == 0) == (stage == 1)
        k = ways[message]
        src, dst, send_sem, recv_sem = (s1_ref, a1_ref, s1_send, s1_recv) if stage == 1 else (s2_ref, a2_ref, s2_send, s2_recv)
        return remote(src.at[h, message], dst.at[h, message], send_sem.at[h, message], recv_sem.at[h, message],
                      col=x_peer(k) if along_x else y_peer(k))

    def arrived(stage, h, message):
        dst, recv_sem = (a1_ref, s1_recv) if stage == 1 else (a2_ref, s2_recv)
        wait_bytes(dst.at[h, message], recv_sem.at[h, message])

    def mine(h, k, other, half):
        target = lax.rem((y if h else x) + k, 4)
        blocks = slice(h * 8 + half * 4, h * 8 + half * 4 + 4)
        return part_ref[other, target, blocks] if h else part_ref[target, other, blocks]

    plan = ((0, 2, 0), (1, 2, 1), (2, 1, 1), (3, 3, 0))
    for message, k, half in plan:
        for h in range(2):
            def narrow(other, carry):
                s1_ref[h, message, other] = mine(h, k, other, half).astype(BF)
                return carry

            lax.fori_loop(0, 4, narrow, 0)
            ring(1, h, message).start()
    if first:
        pltpu.make_async_copy(degree_in_ref.at[pl.ds(col * 16, 16)], dg_ref.at[col], dg_own).start()

        def send(k, carry):
            peer = col_peer(col, k)
            remote(degree_in_ref.at[pl.ds(peer * 16, 16)], dg_ref.at[col], dg_send, dg_recv, col=peer).start()
            return carry

        lax.fori_loop(1, NC, send, 0)
    else:
        inverse = inverse_factor(gram_unpack(gram_in_ref[...]))
    for message, k, half in ((4, 1, 0), (5, 3, 1)):
        for h in range(2):
            arrived(1, h, message - 4)

            def pass_on(other, carry):
                s1_ref[h, message, other] = (mine(h, k, other, half) + a1_ref[h, message - 4, other].astype(F32)).astype(BF)
                return carry

            lax.fori_loop(0, 4, pass_on, 0)
            ring(1, h, message).start()
    for h in range(2):
        for message in range(2, 6):
            arrived(1, h, message)
        place = x if h else y

        def value(k, half):
            other = lax.rem(place + k, 4)
            near, far = (3, 4) if half == 0 else (2, 5)
            return mine(h, 0, other, half) + a1_ref[h, near, other].astype(F32) + a1_ref[h, far, other].astype(F32)

        for message, k, half in plan:
            s2_ref[h, message] = value(k, half).astype(BF)
            ring(2, h, message).start()
        v_ref[h, 0] = value(1, 0)
        v_ref[h, 1] = value(3, 1)
        for half in range(2):
            y_ref[h * 8 + half * 4:h * 8 + half * 4 + 4] = value(0, half)
    for h in range(2):
        for message in (4, 5):
            arrived(2, h, message - 4)
            s2_ref[h, message] = (v_ref[h, message - 4] + a2_ref[h, message - 4].astype(F32)).astype(BF)
            ring(2, h, message).start()
    if first:
        pltpu.make_async_copy(degree_in_ref.at[pl.ds(col * 16, 16)], dg_ref.at[col], dg_own).wait()
        wait_bytes(dg_ref.at[pl.ds(0, NC - 1)], dg_recv)
        degree = dg_ref[0]
        for k in range(1, NC):
            degree = degree + dg_ref[k]
        degree_ref[...] = 1.0 + degree
    for h in range(2):
        for message in range(2, 6):
            arrived(2, h, message)
        for b in range(8):
            near, far = (3, 4) if b < 4 else (2, 5)
            value = y_ref[h * 8 + b] + a2_ref[h, near, b % 4].astype(F32) + a2_ref[h, far, b % 4].astype(F32)
            value = value * (1.0 / degree_ref[h * 8 + b:h * 8 + b + 1])
            if not first:
                value = dot(inverse, value, ((1,), (0,)), lax.Precision.HIGHEST)
            y_ref[h * 8 + b] = value

    if not last:
        for pair in range(4):
            for part in range(2):
                both = jnp.concatenate([y_ref[pair * 4 + part], y_ref[pair * 4 + 2 + part]], axis=0).T
                xs_ref[part * 8:(part + 1) * 8, pair] = both.astype(BF).reshape(8, 16, TILE)
        x_first(row, col, xs_ref, xc_ref, sems)

    gram = jnp.zeros((K, K), F32)
    for b in range(16):
        block = y_ref[b]
        gram = gram + dot(block, block, ((1,), (1,)), lax.Precision.HIGHEST)

    def share(buffer, place, value, peers, base):
        buffer[place] = value
        for i, peer in enumerate(peers):
            remote(buffer.at[place], buffer.at[place], g_send.at[base + i], g_recv.at[base], **peer).start()

    def collect(buffer, count, base):
        wait_bytes(buffer.at[pl.ds(0, count - 1)], g_recv.at[base])
        total = buffer[0]
        for k in range(1, count):
            total = total + buffer[k]
        return total

    share(g1_ref, x, gram_pack(gram), [dict(col=x_peer(k)) for k in (1, 3, 2)], 0)
    if not last:
        x_second(row, col, xs_ref, xc_ref, sems)
    share(g2_ref, y, collect(g1_ref, 4, 0), [dict(col=y_peer(k)) for k in (1, 3, 2)], 3)
    share(g3_ref, row, collect(g2_ref, 4, 3), [dict(row=row_peer(row, dz, flip)) for dz, flip in ROW_ORDER], 6)
    if not last:
        x_third(row, col, xs_ref, xc_ref, sems)
    total = collect(g3_ref, NR, 6) * (1.0 / NODES)
    if last:
        final = inverse_factor(gram_unpack(total))
        for b in range(0, 16, 2):
            both = [dot(final, y_ref[b + i], ((1,), (0,)), lax.Precision.HIGHEST) for i in range(2)]
            both = jnp.concatenate(both, axis=0).T
            z_ref[b * TILE:(b + 1) * TILE] = both[:, :K]
            z_ref[(b + 1) * TILE:(b + 2) * TILE] = both[:, K:]
    else:
        gram_ref[...] = total
        x_finish(row, col, xs_ref, xc_ref, xt_ref, sems)
    for h in range(2):
        for message in range(6):
            wait_bytes(a1_ref.at[h, message], s1_send.at[h, message])
            wait_bytes(a2_ref.at[h, message], s2_send.at[h, message])
    if first:
        wait_bytes(dg_ref.at[pl.ds(0, NC - 1)], dg_send)
    for i in range(13):
        wait_bytes(g1_ref.at[0], g_send.at[i])


def normalize(first, last, part, degree, gram):
    dma = pltpu.SemaphoreType.DMA
    half = (K // 2, TILE)
    out_shape, out_specs = [], []
    if last:
        out_shape.append(jax.ShapeDtypeStruct((16 * TILE, K), F32))
        out_specs.append(VMEM)
    else:
        out_shape += [pltpu.VMEM((X_BLOCKS, K, TILE), BF), jax.ShapeDtypeStruct(half, F32)]
        out_specs += [VMEM, VMEM]
    if first:
        out_shape.append(jax.ShapeDtypeStruct((16, TILE), F32))
        out_specs.append(VMEM)
    scratch = [
        pltpu.VMEM((16, K, TILE), F32), pltpu.VMEM((2, 6, 4, 4, K, TILE), BF), pltpu.VMEM((2, 6, 4, 4, K, TILE), BF),
        pltpu.VMEM((2, 6, 4, K, TILE), BF), pltpu.VMEM((2, 6, 4, K, TILE), BF), pltpu.VMEM((2, 2, 4, K, TILE), F32),
        pltpu.VMEM((4,) + half, F32), pltpu.VMEM((4,) + half, F32), pltpu.VMEM((NR,) + half, F32),
        dma((2, 6)), dma((2, 6)), dma((2, 6)), dma((2, 6)), dma((13,)), dma((13,)),
    ]
    if first:
        scratch += [pltpu.VMEM((NC, 16, TILE), F32), dma, dma, dma]
    if not last:
        scratch += [pltpu.VMEM((NC, 4, 16, TILE), BF), pltpu.VMEM((NR, NC, 4, 16, TILE), BF)] + x_sems()
    args = [part.reshape(4, 4, 16, K, TILE), degree] + ([] if first else [gram])
    return pl.pallas_call(
        functools.partial(normalize_kernel, first, last),
        out_shape=out_shape,
        in_specs=[VMEM, VMEM] + ([] if first else [VMEM]),
        out_specs=out_specs,
        scratch_shapes=scratch,
        compiler_params=pltpu.CompilerParams(
            collective_id=1 if first else (3 if last else 2), has_side_effects=True, vmem_limit_bytes=16 * MIB
        ),
        name="normalize",
    )(*args)


def block_index(block):
    return block // 32 * 32 + block % 16 * 2 + block // 16 % 2


def local(embed, tiles, tile_rows, tile_cols, chg_tiles, chg_rows, chg_cols):
    owners = chg_cols // 256 * NC + chg_rows // 128
    count = owners.shape[0]
    position = jnp.arange(count, dtype=jnp.int32)
    earlier = position[None, :] < position[:, None]
    rank = jnp.sum(jnp.logical_and(owners[:, None] == owners[None, :], earlier).astype(jnp.int32), axis=1)
    key = owners * CAP + rank
    hit = jnp.arange(DEV * CAP, dtype=jnp.int32)[:, None] == key[None, :]
    pick = jnp.sum(jnp.where(hit, position[None, :], 0), axis=1)
    code = jnp.sum(jnp.where(hit, (1 + chg_cols % 256 * 128 + block_index(chg_rows % 128))[None, :], 0), axis=1)
    slot_rows = jnp.where(code > 0, (code - 1) // 128, 0).reshape(DEV, CAP)
    slot_cols = jnp.where(code > 0, (code - 1) % 128, 128).reshape(DEV, CAP)
    meta = jnp.concatenate([slot_rows, slot_cols], axis=1).reshape(NR, NC, 2 * CAP).transpose(1, 0, 2)
    meta = jnp.pad(meta.astype(F32), ((0, 0), (0, 0), (0, TILE - 2 * CAP)))
    xs = embed.reshape(4, 2, NC, 16, K).transpose(2, 0, 3, 1, 4).reshape(NC, 4, 16, TILE)
    slots, tiles, places, xc = exchange(pick, chg_tiles, tiles, meta, xs)
    places = places.reshape(DEV, TILE)[:, :2 * CAP].astype(jnp.int32)
    rows = places[:, :CAP].reshape(DEV * CAP)
    cols = places[:, CAP:].reshape(DEV * CAP)
    own_rows = tile_rows % 256
    own_cols = block_index(tile_cols % 128)
    part, degree = product(True, rows, cols, own_rows, own_cols, xc, tiles, slots)
    xc, gram, degree = normalize(True, False, part, degree, None)
    for iteration in range(1, ITERS):
        (part,) = product(False, rows, cols, own_rows, own_cols, xc, tiles, slots)
        last = iteration == ITERS - 1
        outs = normalize(False, last, part, degree, gram)
        if last:
            return outs[0]
        xc, gram = outs


def solution(mesh):
    placed = (
        P(("row", "col"), None),
        P(("row", "col"), None, None),
        P(("row", "col")),
        P(("row", "col")),
        P(("row", "col"), None, None),
        P(("row", "col")),
        P(("row", "col")),
    )
    return jax.shard_map(
        local, mesh=mesh, in_specs=placed, out_specs=P(("row", "col"), None), check_vma=False
    )
```

```python
import functools

import jax
import jax.numpy as jnp
from jax import lax
from jax.experimental import pallas as pl
from jax.experimental.pallas import tpu as pltpu
from jax.sharding import PartitionSpec as P

ITERS = 3
CAP = 3
K = 64
TILE = 128
NR = 8
NC = 16
DEV = NR * NC
ROWS_BLK = 256
SLOT_ROWS = CAP * TILE
X_BLOCKS = 130
OWN = 64
NODES = 262144
BF = jnp.bfloat16
F32 = jnp.float32
ANY = pl.BlockSpec(memory_space=pl.ANY)

VMEM = pl.BlockSpec(memory_space=pltpu.VMEM)
SMEM = pl.BlockSpec(memory_space=pltpu.SMEM)
MIB = 1024 * 1024
ROW_ORDER = ((1, 0), (3, 1), (2, 0), (1, 1), (3, 0), (2, 1), (0, 1))


def dot(a, b, dims, precision=None):
    return lax.dot_general(a, b, (dims, ((), ())), precision=precision, preferred_element_type=F32)


def greet(row, col):
    barrier = pltpu.get_barrier_semaphore()

    def cols(k, carry):
        pl.semaphore_signal(barrier, inc=1, device_id={"col": lax.rem(col + k, NC)}, device_id_type=pl.DeviceIdType.MESH)
        return carry

    def rows(k, carry):
        pl.semaphore_signal(barrier, inc=1, device_id={"row": lax.rem(row + k, NR)}, device_id_type=pl.DeviceIdType.MESH)
        return carry

    lax.fori_loop(1, NC, cols, 0)
    lax.fori_loop(1, NR, rows, 0)
    pl.semaphore_wait(barrier, NC + NR - 2)


def remote(src, dst, send_sem, recv_sem, **peer):
    return pltpu.make_async_remote_copy(
        src_ref=src, dst_ref=dst, send_sem=send_sem, recv_sem=recv_sem,
        device_id=peer, device_id_type=pl.DeviceIdType.MESH,
    )


def wait_bytes(ref, sem):
    pltpu.make_async_copy(ref, ref, sem).wait()


def col_peer(col, k):
    return lax.rem(col // 4 + k // 4, 4) * 4 + lax.rem(lax.rem(col, 4) + lax.rem(k, 4), 4)


def row_peer(row, dz, flip=0):
    return lax.rem(row // 2 + dz, 4) * 2 + lax.rem(row + flip, 2)


def x_first(row, col, xs, xc, sems):
    pltpu.make_async_copy(xs.at[col], xc.at[row, col], sems["x_own"]).start()

    def send(k, carry):
        peer = col_peer(col, k)
        remote(xs.at[peer], xc.at[row, col], sems["xa_send"], sems["xa_recv"], col=peer).start()
        return carry

    lax.fori_loop(1, NC, send, 0)


def x_second(row, col, xs, xc, sems):
    pltpu.make_async_copy(xs.at[col], xc.at[row, col], sems["x_own"]).wait()
    wait_bytes(xc.at[row, pl.ds(0, NC - 1)], sems["xa_recv"])
    for i, (dz, flip) in enumerate(((1, 0), (3, 0), (2, 0), (0, 1))):
        remote(xc.at[row], xc.at[row], sems["xb_send"].at[i], sems["xb_recv"].at[row], row=row_peer(row, dz, flip)).start()


def x_third(row, col, xs, xc, sems):
    for i, dz in enumerate((1, 3, 2)):
        source = row_peer(row, dz)
        wait_bytes(xc.at[source], sems["xb_recv"].at[source])
        remote(xc.at[source], xc.at[source], sems["xb_send"].at[4 + i], sems["xb_recv"].at[source], row=row_peer(row, 0, 1)).start()


def x_finish(row, col, xs, xc, xt, sems):
    xt[X_BLOCKS - 2:] = jnp.zeros((2, K, TILE), BF)
    for dz in range(4):
        turn(row_peer(row, dz), xc, xt)
    for dz in (0, 1, 3, 2):
        source = row_peer(row, dz, 1)
        wait_bytes(xc.at[source], sems["xb_recv"].at[source])
        turn(source, xc, xt)
    wait_bytes(xs.at[pl.ds(0, NC - 1)], sems["xa_send"])
    for i in range(7):
        wait_bytes(xc.at[row], sems["xb_send"].at[i])


def turn(source, xc, xt):
    for part in range(2):
        for pair in range(4):
            block = xc[source, part * 8:(part + 1) * 8, pair].reshape(TILE, TILE)
            xt[pl.ds((pair * 16 + source * 2 + part) * 2, 2)] = block.T.reshape(2, K, TILE)


X_SEMS = ("x_own", "xa_send", "xa_recv", "xb_send", "xb_recv")


def x_sems():
    dma = pltpu.SemaphoreType.DMA
    return [dma, dma, dma, dma((7,)), dma((NR,))]


def exchange_kernel(pick_ref, tiles_ref, own_ref, meta_ref, xs_ref,
                    recv_ref, mid_ref, far_ref, own_out_ref, places_ref, xt_ref,
                    send_ref, xc_ref, meta_mid_ref, meta_next_ref, *sem_refs):
    sems = dict(zip(X_SEMS, sem_refs))
    (a_send, a_recv, b_send, b_recv, c_send, c_recv, d_send, d_recv,
     m_send, m_recv, n_send, n_recv, own_sem, far_sem) = sem_refs[len(X_SEMS):]
    half = SLOT_ROWS // 2
    head, tail = pl.ds(0, half), pl.ds(half, half)
    row = lax.axis_index("row")
    col = lax.axis_index("col")
    greet(row, col)
    x_first(row, col, xs_ref, xc_ref, sems)
    targets = [row_peer(row, dz, flip) for dz, flip in ROW_ORDER] + [row]
    sources = [row_peer(row, (4 - dz) % 4, flip) for dz, flip in ROW_ORDER]

    def send_meta(k, carry):
        peer = col_peer(col, k)
        remote(meta_ref.at[peer], meta_mid_ref.at[col], m_send, m_recv, col=peer).start()
        return carry

    lax.fori_loop(1, NC, send_meta, 0)
    meta_mid_ref[col] = meta_ref[col]

    def fill(target):
        def tiles(c, carry):
            for slot in range(CAP):
                send_ref[target, c, slot * TILE:(slot + 1) * TILE] = tiles_ref[pick_ref[(target * NC + c) * CAP + slot]]
            return carry

        lax.fori_loop(0, NC, tiles, 0)

    def first_own(step):
        target = targets[step]
        if step < NR - 1:
            return pltpu.make_async_copy(send_ref.at[target, col, head], mid_ref.at[target, col], own_sem.at[step])
        return pltpu.make_async_copy(send_ref.at[target, col, head], recv_ref.at[target, col, head], own_sem.at[step])

    def first(step):
        target = targets[step]

        def send(k, carry):
            peer = col_peer(col, k)
            dst = mid_ref.at[target, col] if step < NR - 1 else recv_ref.at[target, col, head]
            remote(send_ref.at[target, peer, head], dst, a_send.at[step], a_recv.at[step], col=peer).start()
            return carry

        lax.fori_loop(1, NC, send, 0)
        first_own(step).start()

    def second_own(step):
        if step < NR - 1:
            return pltpu.make_async_copy(far_ref.at[sources[step], col], recv_ref.at[sources[step], col, tail], far_sem.at[step])
        return pltpu.make_async_copy(send_ref.at[row, col, tail], recv_ref.at[row, col, tail], far_sem.at[step])

    def second(step):
        def send(k, carry):
            peer = col_peer(col, k)
            source = sources[step] if step < NR - 1 else row
            src = far_ref.at[source, peer] if step < NR - 1 else send_ref.at[row, peer, tail]
            remote(src, recv_ref.at[source, col, tail], d_send.at[step], d_recv.at[source], col=peer).start()
            return carry

        lax.fori_loop(1, NC, send, 0)
        second_own(step).start()

    for step in range(NR):
        fill(targets[step])
        if step < NR - 1:
            remote(send_ref.at[targets[step], :, tail], far_ref.at[row], c_send.at[step], c_recv.at[row], row=targets[step]).start()
            first(step)
        if step == 0:
            x_second(row, col, xs_ref, xc_ref, sems)
    wait_bytes(meta_mid_ref.at[pl.ds(0, NC - 1)], m_recv)
    for c in range(NC):
        for r in range(NR):
            meta_next_ref[r, c:c + 1] = meta_mid_ref[c, r:r + 1]
    for step in range(NR - 1):
        remote(meta_next_ref.at[targets[step]], places_ref.at[row], n_send, n_recv, row=targets[step]).start()
    places_ref[row] = meta_next_ref[row]
    x_third(row, col, xs_ref, xc_ref, sems)

    def flip_own(i, carry):
        for u in range(4):
            own_out_ref[i * 4 + u] = own_ref[i * 4 + u].T
        return carry

    lax.fori_loop(0, OWN // 4, flip_own, 0)
    for step in range(NR - 1):
        target, source = targets[step], sources[step]
        wait_bytes(mid_ref.at[target, pl.ds(0, NC - 1)], a_recv.at[step])
        first_own(step).wait()
        remote(mid_ref.at[target], recv_ref.at[row, :, head], b_send.at[step], b_recv.at[row], row=target).start()
        wait_bytes(far_ref.at[source], c_recv.at[source])
        second(step)
    first(NR - 1)
    second(NR - 1)
    x_finish(row, col, xs_ref, xc_ref, xt_ref, sems)
    some = mid_ref.at[0, pl.ds(0, NC - 1)]
    wait_bytes(some, a_recv.at[NR - 1])
    first_own(NR - 1).wait()
    wait_bytes(meta_mid_ref.at[pl.ds(0, NC - 1)], m_send)
    wait_bytes(places_ref.at[pl.ds(0, NR - 1)], n_send)
    wait_bytes(places_ref.at[pl.ds(0, NR - 1)], n_recv)
    for step in range(NR):
        wait_bytes(some, a_send.at[step])
        wait_bytes(some, d_send.at[step])
        wait_bytes(some, d_recv.at[sources[step] if step < NR - 1 else row])
        second_own(step).wait()
    for step in range(NR - 1):
        wait_bytes(mid_ref.at[0], b_send.at[step])
        wait_bytes(mid_ref.at[0], c_send.at[step])
        wait_bytes(mid_ref.at[0], b_recv.at[targets[step]])


def exchange(pick, chg_tiles, own, meta, xs):
    dma = pltpu.SemaphoreType.DMA
    slots = (NR, NC, SLOT_ROWS, TILE)
    halves = jax.ShapeDtypeStruct((NR, NC, SLOT_ROWS // 2, TILE), BF)
    recv, _, _, own, places, xt = pl.pallas_call(
        exchange_kernel,
        out_shape=(jax.ShapeDtypeStruct(slots, BF), halves, halves, pltpu.VMEM((OWN, TILE, TILE), BF),
                   jax.ShapeDtypeStruct((NR, NC, TILE), F32), pltpu.VMEM((X_BLOCKS, K, TILE), BF)),
        in_specs=[SMEM, VMEM, VMEM, VMEM, VMEM],
        out_specs=(ANY, ANY, ANY, VMEM, VMEM, VMEM),
        scratch_shapes=[
            pltpu.VMEM(slots, BF), pltpu.VMEM((NR, NC, 4, 16, TILE), BF),
            pltpu.VMEM((NC, NR, TILE), F32), pltpu.VMEM((NR, NC, TILE), F32),
        ] + x_sems() + [dma((NR,))] * 8 + [dma, dma, dma, dma, dma((NR,)), dma((NR,))],
        compiler_params=pltpu.CompilerParams(collective_id=0, has_side_effects=True, vmem_limit_bytes=42 * MIB),
        name="exchange",
    )(pick, chg_tiles, own, meta, xs)
    return recv, own, places, xt


def product_kernel(with_degree, rows_ref, cols_ref, own_rows_ref, own_cols_ref, xt_ref, own_ref, slots_in_ref, acc_ref, *rest):
    slots_ref, slot_sem = rest[-2:]
    loads = [
        pltpu.make_async_copy(slots_in_ref.at[pl.ds(i * 16, 16)], slots_ref.at[pl.ds(i * 16, 16)], slot_sem.at[i])
        for i in range(DEV // 16)
    ]
    for load in loads:
        load.start()
    ones = jnp.ones((8, TILE), BF)
    plain = ((1,), (0,))
    if with_degree:
        degree_out_ref, degree_ref = rest[:2]
        degree_ref[...] = jnp.zeros_like(degree_ref)

    def clear(i, carry):
        acc_ref[pl.ds(i * 8, 8)] = jnp.zeros((8, K, TILE), F32)
        return carry

    lax.fori_loop(0, ROWS_BLK // 8, clear, 0)

    def run(tiles, rows, cols):
        values = [dot(xt_ref[col], tile, plain) for tile, col in zip(tiles, cols)]
        sums = []
        if with_degree:
            sums = [
                dot(jnp.where(col < 128, ones, jnp.zeros_like(ones)), jnp.abs(tile), plain)[0:1]
                for tile, col in zip(tiles, cols)
            ]
        for row, value in zip(rows, values):
            acc_ref[row] += value
        for row, value in zip(rows, sums):
            degree_ref[row] += value

    def own(i, carry):
        places = [i * 16 + u for u in range(16)]
        run([own_ref[n] for n in places], [own_rows_ref[n] for n in places], [own_cols_ref[n] for n in places])
        return carry

    def taken(i, carry):
        sources = [i * 16 + u for u in range(16)]
        places = [source * CAP + slot for source in sources for slot in range(CAP)]
        run([slots_ref[source, slot * TILE:(slot + 1) * TILE] for source in sources for slot in range(CAP)],
            [rows_ref[n] for n in places], [cols_ref[n] for n in places])
        return carry

    lax.fori_loop(0, OWN // 16, own, 0)
    for i, load in enumerate(loads):
        load.wait()
        lax.fori_loop(i, i + 1, taken, 0)
    if with_degree:
        degree_out_ref[...] = degree_ref[...].reshape(ROWS_BLK, TILE)


def product(with_degree, rows, cols, own_rows, own_cols, xt, own, slots):
    out_shape = [pltpu.VMEM((ROWS_BLK, K, TILE), F32)]
    if with_degree:
        out_shape.append(jax.ShapeDtypeStruct((ROWS_BLK, TILE), F32))
    terms = DEV * CAP + OWN
    return pl.pallas_call(
        functools.partial(product_kernel, with_degree),
        out_shape=out_shape,
        in_specs=[SMEM, SMEM, SMEM, SMEM, VMEM, VMEM, ANY],
        out_specs=[VMEM] * len(out_shape),
        scratch_shapes=([pltpu.VMEM((ROWS_BLK, 1, TILE), F32)] if with_degree else []) + [
            pltpu.VMEM((DEV, SLOT_ROWS, TILE), BF), pltpu.SemaphoreType.DMA((DEV // 16,)),
        ],
        compiler_params=pltpu.CompilerParams(vmem_limit_bytes=40 * MIB),
        cost_estimate=pl.CostEstimate(flops=terms * 2 * K * TILE * TILE, bytes_accessed=terms * TILE * TILE * 2, transcendentals=0),
        name="product",
    )(rows, cols, own_rows, own_cols, xt, own, slots.reshape(DEV, SLOT_ROWS, TILE))


def inverse_factor(gram):
    eye = (lax.broadcasted_iota(jnp.int32, (K, K), 0) == lax.broadcasted_iota(jnp.int32, (K, K), 1)).astype(F32)
    work = jnp.concatenate([gram, eye], axis=1)
    index = lax.broadcasted_iota(jnp.int32, (K, 1), 0)
    pivots = jnp.ones((K, 1), F32)
    for j in range(K):
        pivot = work[j:j + 1, j:j + 1]
        pivots = jnp.where(index == j, pivot, pivots)
        factor = jnp.where(index > j, work[:, j:j + 1] * (1.0 / pivot), 0.0)
        work = work - factor * work[j:j + 1, :]
    return lax.rsqrt(pivots) * work[:, K:]


def gram_pack(gram):
    return jnp.concatenate([gram[:K // 2], gram[K // 2:]], axis=1)


def gram_unpack(packed):
    return jnp.concatenate([packed[:, :K], packed[:, K:]], axis=0)


def normalize_kernel(first, last, part_ref, degree_in_ref, *rest):
    rest = list(rest)
    take = lambda count: [rest.pop(0) for _ in range(count)]
    gram_in_ref = None if first else rest.pop(0)
    if last:
        (z_ref,) = take(1)
    else:
        xt_ref, gram_ref = take(2)
    degree_ref = rest.pop(0) if first else degree_in_ref
    y_ref, s1_ref, a1_ref, s2_ref, a2_ref, v_ref, g1_ref, g2_ref, g3_ref = take(9)
    s1_send, s1_recv, s2_send, s2_recv, g_send, g_recv = take(6)
    if first:
        dg_ref, dg_own, dg_send, dg_recv = take(4)
    if not last:
        xs_ref, xc_ref = take(2)
        sems = dict(zip(X_SEMS, rest))
    row = lax.axis_index("row")
    col = lax.axis_index("col")
    x, y = col // 4, lax.rem(col, 4)
    x_peer = lambda k: lax.rem(x + k, 4) * 4 + y
    y_peer = lambda k: x * 4 + lax.rem(y + k, 4)
    greet(row, col)

    ways = ((1, 3) * 3)

    def ring(stage, h, message):
        along_x = (h == 0) == (stage == 1)
        k = ways[message]
        src, dst, send_sem, recv_sem = (s1_ref, a1_ref, s1_send, s1_recv) if stage == 1 else (s2_ref, a2_ref, s2_send, s2_recv)
        return remote(src.at[h, message], dst.at[h, message], send_sem.at[h, message], recv_sem.at[h, message],
                      col=x_peer(k) if along_x else y_peer(k))

    def arrived(stage, h, message):
        dst, recv_sem = (a1_ref, s1_recv) if stage == 1 else (a2_ref, s2_recv)
        wait_bytes(dst.at[h, message], recv_sem.at[h, message])

    def mine(h, k, other, half):
        target = lax.rem((y if h else x) + k, 4)
        blocks = slice(h * 8 + half * 4, h * 8 + half * 4 + 4)
        return part_ref[other, target, blocks] if h else part_ref[target, other, blocks]

    plan = ((0, 2, 0), (1, 2, 1), (2, 1, 1), (3, 3, 0))
    for message, k, half in plan:
        for h in range(2):
            def narrow(other, carry):
                s1_ref[h, message, other] = mine(h, k, other, half).astype(BF)
                return carry

            lax.fori_loop(0, 4, narrow, 0)
            ring(1, h, message).start()
    if first:
        pltpu.make_async_copy(degree_in_ref.at[pl.ds(col * 16, 16)], dg_ref.at[col], dg_own).start()

        def send(k, carry):
            peer = col_peer(col, k)
            remote(degree_in_ref.at[pl.ds(peer * 16, 16)], dg_ref.at[col], dg_send, dg_recv, col=peer).start()
            return carry

        lax.fori_loop(1, NC, send, 0)
    else:
        inverse = inverse_factor(gram_unpack(gram_in_ref[...]))
    for message, k, half in ((4, 1, 0), (5, 3, 1)):
        for h in range(2):
            arrived(1, h, message - 4)

            def pass_on(other, carry):
                s1_ref[h, message, other] = (mine(h, k, other, half) + a1_ref[h, message - 4, other].astype(F32)).astype(BF)
                return carry

            lax.fori_loop(0, 4, pass_on, 0)
            ring(1, h, message).start()
    for h in range(2):
        for message in range(2, 6):
            arrived(1, h, message)
        place = x if h else y

        def value(k, half):
            other = lax.rem(place + k, 4)
            near, far = (3, 4) if half == 0 else (2, 5)
            return mine(h, 0, other, half) + a1_ref[h, near, other].astype(F32) + a1_ref[h, far, other].astype(F32)

        for message, k, half in plan:
            s2_ref[h, message] = value(k, half).astype(BF)
            ring(2, h, message).start()
        v_ref[h, 0] = value(1, 0)
        v_ref[h, 1] = value(3, 1)
        for half in range(2):
            y_ref[h * 8 + half * 4:h * 8 + half * 4 + 4] = value(0, half)
    for h in range(2):
        for message in (4, 5):
            arrived(2, h, message - 4)
            s2_ref[h, message] = (v_ref[h, message - 4] + a2_ref[h, message - 4].astype(F32)).astype(BF)
            ring(2, h, message).start()
    if first:
        pltpu.make_async_copy(degree_in_ref.at[pl.ds(col * 16, 16)], dg_ref.at[col], dg_own).wait()
        wait_bytes(dg_ref.at[pl.ds(0, NC - 1)], dg_recv)
        degree = dg_ref[0]
        for k in range(1, NC):
            degree = degree + dg_ref[k]
        degree_ref[...] = 1.0 + degree
    for h in range(2):
        for message in range(2, 6):
            arrived(2, h, message)
        for b in range(8):
            near, far = (3, 4) if b < 4 else (2, 5)
            value = y_ref[h * 8 + b] + a2_ref[h, near, b % 4].astype(F32) + a2_ref[h, far, b % 4].astype(F32)
            value = value * (1.0 / degree_ref[h * 8 + b:h * 8 + b + 1])
            if not first:
                value = dot(inverse, value, ((1,), (0,)), lax.Precision.HIGHEST)
            y_ref[h * 8 + b] = value

    if not last:
        for pair in range(4):
            for part in range(2):
                both = jnp.concatenate([y_ref[pair * 4 + part], y_ref[pair * 4 + 2 + part]], axis=0).T
                xs_ref[part * 8:(part + 1) * 8, pair] = both.astype(BF).reshape(8, 16, TILE)
        x_first(row, col, xs_ref, xc_ref, sems)

    gram = jnp.zeros((K, K), F32)
    for b in range(16):
        block = y_ref[b]
        gram = gram + dot(block, block, ((1,), (1,)), lax.Precision.HIGHEST)

    def share(buffer, place, value, peers, base):
        buffer[place] = value
        for i, peer in enumerate(peers):
            remote(buffer.at[place], buffer.at[place], g_send.at[base + i], g_recv.at[base], **peer).start()

    def collect(buffer, count, base):
        wait_bytes(buffer.at[pl.ds(0, count - 1)], g_recv.at[base])
        total = buffer[0]
        for k in range(1, count):
            total = total + buffer[k]
        return total

    share(g1_ref, x, gram_pack(gram), [dict(col=x_peer(k)) for k in (1, 3, 2)], 0)
    if not last:
        x_second(row, col, xs_ref, xc_ref, sems)
    share(g2_ref, y, collect(g1_ref, 4, 0), [dict(col=y_peer(k)) for k in (1, 3, 2)], 3)
    share(g3_ref, row, collect(g2_ref, 4, 3), [dict(row=row_peer(row, dz, flip)) for dz, flip in ROW_ORDER], 6)
    if not last:
        x_third(row, col, xs_ref, xc_ref, sems)
    total = collect(g3_ref, NR, 6) * (1.0 / NODES)
    if last:
        final = inverse_factor(gram_unpack(total))
        for b in range(0, 16, 2):
            both = [dot(final, y_ref[b + i], ((1,), (0,)), lax.Precision.HIGHEST) for i in range(2)]
            both = jnp.concatenate(both, axis=0).T
            z_ref[b * TILE:(b + 1) * TILE] = both[:, :K]
            z_ref[(b + 1) * TILE:(b + 2) * TILE] = both[:, K:]
    else:
        gram_ref[...] = total
        x_finish(row, col, xs_ref, xc_ref, xt_ref, sems)
    for h in range(2):
        for message in range(6):
            wait_bytes(a1_ref.at[h, message], s1_send.at[h, message])
            wait_bytes(a2_ref.at[h, message], s2_send.at[h, message])
    if first:
        wait_bytes(dg_ref.at[pl.ds(0, NC - 1)], dg_send)
    for i in range(13):
        wait_bytes(g1_ref.at[0], g_send.at[i])


def normalize(first, last, part, degree, gram):
    dma = pltpu.SemaphoreType.DMA
    half = (K // 2, TILE)
    out_shape, out_specs = [], []
    if last:
        out_shape.append(jax.ShapeDtypeStruct((16 * TILE, K), F32))
        out_specs.append(VMEM)
    else:
        out_shape += [pltpu.VMEM((X_BLOCKS, K, TILE), BF), jax.ShapeDtypeStruct(half, F32)]
        out_specs += [VMEM, VMEM]
    if first:
        out_shape.append(jax.ShapeDtypeStruct((16, TILE), F32))
        out_specs.append(VMEM)
    scratch = [
        pltpu.VMEM((16, K, TILE), F32), pltpu.VMEM((2, 6, 4, 4, K, TILE), BF), pltpu.VMEM((2, 6, 4, 4, K, TILE), BF),
        pltpu.VMEM((2, 6, 4, K, TILE), BF), pltpu.VMEM((2, 6, 4, K, TILE), BF), pltpu.VMEM((2, 2, 4, K, TILE), F32),
        pltpu.VMEM((4,) + half, F32), pltpu.VMEM((4,) + half, F32), pltpu.VMEM((NR,) + half, F32),
        dma((2, 6)), dma((2, 6)), dma((2, 6)), dma((2, 6)), dma((13,)), dma((13,)),
    ]
    if first:
        scratch += [pltpu.VMEM((NC, 16, TILE), F32), dma, dma, dma]
    if not last:
        scratch += [pltpu.VMEM((NC, 4, 16, TILE), BF), pltpu.VMEM((NR, NC, 4, 16, TILE), BF)] + x_sems()
    args = [part.reshape(4, 4, 16, K, TILE), degree] + ([] if first else [gram])
    return pl.pallas_call(
        functools.partial(normalize_kernel, first, last),
        out_shape=out_shape,
        in_specs=[VMEM, VMEM] + ([] if first else [VMEM]),
        out_specs=out_specs,
        scratch_shapes=scratch,
        compiler_params=pltpu.CompilerParams(
            collective_id=1 if first else (3 if last else 2), has_side_effects=True, vmem_limit_bytes=16 * MIB
        ),
        name="normalize",
    )(*args)


def block_index(block):
    return block // 32 * 32 + block % 16 * 2 + block // 16 % 2


def local(embed, tiles, tile_rows, tile_cols, chg_tiles, chg_rows, chg_cols):
    owners = chg_cols // 256 * NC + chg_rows // 128
    count = owners.shape[0]
    position = jnp.arange(count, dtype=jnp.int32)
    earlier = position[None, :] < position[:, None]
    rank = jnp.sum(jnp.logical_and(owners[:, None] == owners[None, :], earlier).astype(jnp.int32), axis=1)
    key = owners * CAP + rank
    hit = jnp.arange(DEV * CAP, dtype=jnp.int32)[:, None] == key[None, :]
    pick = jnp.sum(jnp.where(hit, position[None, :], 0), axis=1)
    code = jnp.sum(jnp.where(hit, (1 + chg_cols % 256 * 128 + block_index(chg_rows % 128))[None, :], 0), axis=1)
    slot_rows = jnp.where(code > 0, (code - 1) // 128, 0).reshape(DEV, CAP)
    slot_cols = jnp.where(code > 0, (code - 1) % 128, 128).reshape(DEV, CAP)
    meta = jnp.concatenate([slot_rows, slot_cols], axis=1).reshape(NR, NC, 2 * CAP).transpose(1, 0, 2)
    meta = jnp.pad(meta.astype(F32), ((0, 0), (0, 0), (0, TILE - 2 * CAP)))
    xs = embed.reshape(4, 2, NC, 16, K).transpose(2, 0, 3, 1, 4).reshape(NC, 4, 16, TILE)
    slots, tiles, places, xc = exchange(pick, chg_tiles, tiles, meta, xs)
    places = places.reshape(DEV, TILE)[:, :2 * CAP].astype(jnp.int32)
    rows = places[:, :CAP].reshape(DEV * CAP)
    cols = places[:, CAP:].reshape(DEV * CAP)
    own_rows = tile_rows % 256
    own_cols = block_index(tile_cols % 128)
    part, degree = product(True, rows, cols, own_rows, own_cols, xc, tiles, slots)
    xc, gram, degree = normalize(True, False, part, degree, None)
    for iteration in range(1, ITERS):
        (part,) = product(False, rows, cols, own_rows, own_cols, xc, tiles, slots)
        last = iteration == ITERS - 1
        outs = normalize(False, last, part, degree, gram)
        if last:
            return outs[0]
        xc, gram = outs


def solution(mesh):
    placed = (
        P(("row", "col"), None),
        P(("row", "col"), None, None),
        P(("row", "col")),
        P(("row", "col")),
        P(("row", "col"), None, None),
        P(("row", "col")),
        P(("row", "col")),
    )
    return jax.shard_map(
        local, mesh=mesh, in_specs=placed, out_specs=P(("row", "col"), None), check_vma=False
    )
```

```python
import functools

import jax
import jax.numpy as jnp
from jax import lax
from jax.experimental import pallas as pl
from jax.experimental.pallas import tpu as pltpu
from jax.sharding import PartitionSpec as P

ITERS = 3
CAP = 3
K = 64
TILE = 128
NR = 8
NC = 16
DEV = NR * NC
ROWS_BLK = 256
SLOT_ROWS = CAP * TILE
X_BLOCKS = 130
OWN = 64
NODES = 262144
BF = jnp.bfloat16
F32 = jnp.float32
ANY = pl.BlockSpec(memory_space=pl.ANY)

VMEM = pl.BlockSpec(memory_space=pltpu.VMEM)
SMEM = pl.BlockSpec(memory_space=pltpu.SMEM)
MIB = 1024 * 1024
ROW_ORDER = ((2, 0), (1, 1), (3, 0), (2, 1), (1, 0), (3, 1), (0, 1))


def dot(a, b, dims, precision=None):
    return lax.dot_general(a, b, (dims, ((), ())), precision=precision, preferred_element_type=F32)


def greet(row, col):
    barrier = pltpu.get_barrier_semaphore()

    def cols(k, carry):
        pl.semaphore_signal(barrier, inc=1, device_id={"col": lax.rem(col + k, NC)}, device_id_type=pl.DeviceIdType.MESH)
        return carry

    def rows(k, carry):
        pl.semaphore_signal(barrier, inc=1, device_id={"row": lax.rem(row + k, NR)}, device_id_type=pl.DeviceIdType.MESH)
        return carry

    lax.fori_loop(1, NC, cols, 0)
    lax.fori_loop(1, NR, rows, 0)
    pl.semaphore_wait(barrier, NC + NR - 2)


def remote(src, dst, send_sem, recv_sem, **peer):
    return pltpu.make_async_remote_copy(
        src_ref=src, dst_ref=dst, send_sem=send_sem, recv_sem=recv_sem,
        device_id=peer, device_id_type=pl.DeviceIdType.MESH,
    )


def wait_bytes(ref, sem):
    pltpu.make_async_copy(ref, ref, sem).wait()


def col_peer(col, k):
    return lax.rem(col // 4 + k // 4, 4) * 4 + lax.rem(lax.rem(col, 4) + lax.rem(k, 4), 4)


def row_peer(row, dz, flip=0):
    return lax.rem(row // 2 + dz, 4) * 2 + lax.rem(row + flip, 2)


def x_pieces(block, xs):
    for pair in range(4):
        for part in range(2):
            both = jnp.concatenate([block(pair * 4 + part), block(pair * 4 + 2 + part)], axis=0).T
            xs[part * 8:(part + 1) * 8, pair] = both.astype(BF).reshape(8, 16, TILE)


def x_first(row, col, xs, xc, sems):
    pltpu.make_async_copy(xs.at[col], xc.at[row, col], sems["x_own"]).start()

    def send(k, carry):
        peer = col_peer(col, k)
        remote(xs.at[peer], xc.at[row, col], sems["xa_send"], sems["xa_recv"], col=peer).start()
        return carry

    lax.fori_loop(1, NC, send, 0)


def x_second(row, col, xs, xc, sems):
    pltpu.make_async_copy(xs.at[col], xc.at[row, col], sems["x_own"]).wait()
    wait_bytes(xc.at[row, pl.ds(0, NC - 1)], sems["xa_recv"])
    for i, (dz, flip) in enumerate(((1, 0), (3, 0), (2, 0), (0, 1))):
        remote(xc.at[row], xc.at[row], sems["xb_send"].at[i], sems["xb_recv"].at[row], row=row_peer(row, dz, flip)).start()


def x_third(row, col, xs, xc, sems):
    for i, dz in enumerate((1, 3, 2)):
        source = row_peer(row, dz)
        wait_bytes(xc.at[source], sems["xb_recv"].at[source])
        remote(xc.at[source], xc.at[source], sems["xb_send"].at[4 + i], sems["xb_recv"].at[source], row=row_peer(row, 0, 1)).start()


def x_finish(row, col, xs, xc, xt, sems):
    xt[X_BLOCKS - 2:] = jnp.zeros((2, K, TILE), BF)
    for dz in range(4):
        turn(row_peer(row, dz), xc, xt)
    for dz in (0, 1, 3, 2):
        source = row_peer(row, dz, 1)
        wait_bytes(xc.at[source], sems["xb_recv"].at[source])
        turn(source, xc, xt)
    wait_bytes(xs.at[pl.ds(0, NC - 1)], sems["xa_send"])
    for i in range(7):
        wait_bytes(xc.at[row], sems["xb_send"].at[i])


def turn(source, xc, xt):
    for part in range(2):
        for pair in range(4):
            block = xc[source, part * 8:(part + 1) * 8, pair].reshape(TILE, TILE)
            xt[pl.ds((pair * 16 + source * 2 + part) * 2, 2)] = block.T.reshape(2, K, TILE)


X_SEMS = ("x_own", "xa_send", "xa_recv", "xb_send", "xb_recv")


def x_sems():
    dma = pltpu.SemaphoreType.DMA
    return [dma, dma, dma, dma((7,)), dma((NR,))]


def exchange_kernel(pick_ref, tiles_in_ref, own_in_ref, meta_ref, embed_ref,
                    recv_ref, mid_ref, far_ref, own_out_ref, places_ref, xt_ref,
                    send_ref, xc_ref, meta_mid_ref, meta_next_ref, xs_ref, tiles_ref, own_ref, tiles_sem, own_load_sem, *sem_refs):
    sems = dict(zip(X_SEMS, sem_refs))
    (a_send, a_recv, b_send, b_recv, c_send, c_recv, d_send, d_recv,
     m_send, m_recv, n_send, n_recv, own_sem, far_sem) = sem_refs[len(X_SEMS):]
    load_tiles = pltpu.make_async_copy(tiles_in_ref, tiles_ref, tiles_sem)
    load_own = pltpu.make_async_copy(own_in_ref, own_ref, own_load_sem)
    load_tiles.start()
    load_own.start()
    half = SLOT_ROWS // 2
    head, tail = pl.ds(0, half), pl.ds(half, half)
    row = lax.axis_index("row")
    col = lax.axis_index("col")
    greet(row, col)
    x_pieces(lambda b: embed_ref[:, b * TILE:(b + 1) * TILE], xs_ref)
    x_first(row, col, xs_ref, xc_ref, sems)
    targets = [row_peer(row, dz, flip) for dz, flip in ROW_ORDER] + [row]
    sources = [row_peer(row, (4 - dz) % 4, flip) for dz, flip in ROW_ORDER]

    def send_meta(k, carry):
        peer = col_peer(col, k)
        remote(meta_ref.at[peer], meta_mid_ref.at[col], m_send, m_recv, col=peer).start()
        return carry

    lax.fori_loop(1, NC, send_meta, 0)
    meta_mid_ref[col] = meta_ref[col]

    def fill(target):
        def tiles(c, carry):
            for slot in range(CAP):
                send_ref[target, c, slot * TILE:(slot + 1) * TILE] = tiles_ref[pick_ref[(target * NC + c) * CAP + slot]]
            return carry

        lax.fori_loop(0, NC, tiles, 0)

    def first_own(step):
        target = targets[step]
        if step < NR - 1:
            return pltpu.make_async_copy(send_ref.at[target, col, head], mid_ref.at[target, col], own_sem.at[step])
        return pltpu.make_async_copy(send_ref.at[target, col, head], recv_ref.at[target, col, head], own_sem.at[step])

    def first(step):
        target = targets[step]

        def send(k, carry):
            peer = col_peer(col, k)
            dst = mid_ref.at[target, col] if step < NR - 1 else recv_ref.at[target, col, head]
            remote(send_ref.at[target, peer, head], dst, a_send.at[step], a_recv.at[step], col=peer).start()
            return carry

        lax.fori_loop(1, NC, send, 0)
        first_own(step).start()

    def second_own(step):
        if step < NR - 1:
            return pltpu.make_async_copy(far_ref.at[sources[step], col], recv_ref.at[sources[step], col, tail], far_sem.at[step])
        return pltpu.make_async_copy(send_ref.at[row, col, tail], recv_ref.at[row, col, tail], far_sem.at[step])

    def second(step):
        def send(k, carry):
            peer = col_peer(col, k)
            source = sources[step] if step < NR - 1 else row
            src = far_ref.at[source, peer] if step < NR - 1 else send_ref.at[row, peer, tail]
            remote(src, recv_ref.at[source, col, tail], d_send.at[step], d_recv.at[source], col=peer).start()
            return carry

        lax.fori_loop(1, NC, send, 0)
        second_own(step).start()

    load_tiles.wait()
    for step in range(NR):
        fill(targets[step])
        if step < NR - 1:
            remote(send_ref.at[targets[step], :, tail], far_ref.at[row], c_send.at[step], c_recv.at[row], row=targets[step]).start()
            first(step)
        if step == 0:
            x_second(row, col, xs_ref, xc_ref, sems)
    wait_bytes(meta_mid_ref.at[pl.ds(0, NC - 1)], m_recv)
    for c in range(NC):
        for r in range(NR):
            meta_next_ref[r, c:c + 1] = meta_mid_ref[c, r:r + 1]
    for step in range(NR - 1):
        remote(meta_next_ref.at[targets[step]], places_ref.at[row], n_send, n_recv, row=targets[step]).start()
    places_ref[row] = meta_next_ref[row]
    x_third(row, col, xs_ref, xc_ref, sems)

    def flip_own(i, carry):
        for u in range(4):
            own_out_ref[i * 4 + u] = own_ref[i * 4 + u].T
        return carry

    load_own.wait()
    lax.fori_loop(0, OWN // 4, flip_own, 0)
    for step in range(NR - 1):
        target, source = targets[step], sources[step]
        wait_bytes(mid_ref.at[target, pl.ds(0, NC - 1)], a_recv.at[step])
        first_own(step).wait()
        remote(mid_ref.at[target], recv_ref.at[row, :, head], b_send.at[step], b_recv.at[row], row=target).start()
        wait_bytes(far_ref.at[source], c_recv.at[source])
        second(step)
    first(NR - 1)
    second(NR - 1)
    x_finish(row, col, xs_ref, xc_ref, xt_ref, sems)
    some = mid_ref.at[0, pl.ds(0, NC - 1)]
    wait_bytes(some, a_recv.at[NR - 1])
    first_own(NR - 1).wait()
    wait_bytes(meta_mid_ref.at[pl.ds(0, NC - 1)], m_send)
    wait_bytes(places_ref.at[pl.ds(0, NR - 1)], n_send)
    wait_bytes(places_ref.at[pl.ds(0, NR - 1)], n_recv)
    for step in range(NR):
        wait_bytes(some, a_send.at[step])
        wait_bytes(some, d_send.at[step])
        wait_bytes(some, d_recv.at[sources[step] if step < NR - 1 else row])
        second_own(step).wait()
    for step in range(NR - 1):
        wait_bytes(mid_ref.at[0], b_send.at[step])
        wait_bytes(mid_ref.at[0], c_send.at[step])
        wait_bytes(mid_ref.at[0], b_recv.at[targets[step]])


def exchange(pick, chg_tiles, own, meta, xs):
    dma = pltpu.SemaphoreType.DMA
    slots = (NR, NC, SLOT_ROWS, TILE)
    halves = jax.ShapeDtypeStruct((NR, NC, SLOT_ROWS // 2, TILE), BF)
    recv, _, _, own, places, xt = pl.pallas_call(
        exchange_kernel,
        out_shape=(jax.ShapeDtypeStruct(slots, BF), halves, halves, pltpu.VMEM((OWN, TILE, TILE), BF),
                   jax.ShapeDtypeStruct((NR, NC, TILE), jnp.int32), pltpu.VMEM((X_BLOCKS, K, TILE), BF)),
        in_specs=[SMEM, ANY, ANY, VMEM, VMEM],
        out_specs=(ANY, ANY, ANY, VMEM, VMEM, VMEM),
        scratch_shapes=[
            pltpu.VMEM(slots, BF), pltpu.VMEM((NR, NC, 4, 16, TILE), BF),
            pltpu.VMEM((NC, NR, TILE), jnp.int32), pltpu.VMEM((NR, NC, TILE), jnp.int32),
            pltpu.VMEM((NC, 4, 16, TILE), BF), pltpu.VMEM(chg_tiles.shape, BF), pltpu.VMEM(own.shape, BF), dma, dma,
        ] + x_sems() + [dma((NR,))] * 8 + [dma, dma, dma, dma, dma((NR,)), dma((NR,))],
        compiler_params=pltpu.CompilerParams(collective_id=0, has_side_effects=True, vmem_limit_bytes=58 * MIB),
        name="exchange",
    )(pick, chg_tiles, own, meta, xs)
    return recv, own, places, xt


def product_kernel(with_degree, places_ref, own_rows_ref, own_cols_ref, xt_ref, own_ref, slots_in_ref, acc_ref, *rest):
    slots_ref, slot_sem, table_ref, table_sem = rest[-4:]
    load_table = pltpu.make_async_copy(places_ref, table_ref, table_sem)
    load_table.start()
    loads = [
        pltpu.make_async_copy(slots_in_ref.at[i], slots_ref.at[i], slot_sem.at[i])
        for i in range(NR)
    ]
    for load in loads:
        load.start()
    ones = jnp.ones((8, TILE), BF)
    plain = ((1,), (0,))
    if with_degree:
        degree_out_ref, degree_ref = rest[:2]
        degree_ref[...] = jnp.zeros_like(degree_ref)

    def clear(i, carry):
        acc_ref[pl.ds(i * 8, 8)] = jnp.zeros((8, K, TILE), F32)
        return carry

    lax.fori_loop(0, ROWS_BLK // 8, clear, 0)

    def run(tiles, rows, cols):
        values = [dot(xt_ref[col], tile, plain) for tile, col in zip(tiles, cols)]
        sums = []
        if with_degree:
            sums = [
                dot(jnp.where(col < 128, ones, jnp.zeros_like(ones)), jnp.abs(tile), plain)[0:1]
                for tile, col in zip(tiles, cols)
            ]
        for row, value in zip(rows, values):
            acc_ref[row] += value
        for row, value in zip(rows, sums):
            degree_ref[row] += value

    def own(i, carry):
        places = [i * 16 + u for u in range(16)]
        run([own_ref[n] for n in places], [own_rows_ref[n] for n in places], [own_cols_ref[n] for n in places])
        return carry

    def taken(group, carry):
        places = [(source, slot) for source in range(NC) for slot in range(CAP)]
        run([slots_ref[group, source, slot * TILE:(slot + 1) * TILE] for source, slot in places],
            [table_ref[group, source, slot] for source, slot in places],
            [table_ref[group, source, CAP + slot] for source, slot in places])
        return carry

    lax.fori_loop(0, OWN // 16, own, 0)
    load_table.wait()
    for i, load in enumerate(loads):
        load.wait()
        lax.fori_loop(i, i + 1, taken, 0)
    if with_degree:
        degree_out_ref[...] = degree_ref[...].reshape(ROWS_BLK, TILE)


def product(with_degree, places, own_rows, own_cols, xt, own, slots):
    out_shape = [pltpu.VMEM((ROWS_BLK, K, TILE), F32)]
    if with_degree:
        out_shape.append(jax.ShapeDtypeStruct((ROWS_BLK, TILE), F32))
    terms = DEV * CAP + OWN
    return pl.pallas_call(
        functools.partial(product_kernel, with_degree),
        out_shape=out_shape,
        in_specs=[VMEM, SMEM, SMEM, VMEM, VMEM, ANY],
        out_specs=[VMEM] * len(out_shape),
        scratch_shapes=([pltpu.VMEM((ROWS_BLK, 1, TILE), F32)] if with_degree else []) + [
            pltpu.VMEM((NR, NC, SLOT_ROWS, TILE), BF), pltpu.SemaphoreType.DMA((NR,)),
            pltpu.SMEM((NR, NC, TILE), jnp.int32), pltpu.SemaphoreType.DMA,
        ],
        compiler_params=pltpu.CompilerParams(vmem_limit_bytes=40 * MIB),
        cost_estimate=pl.CostEstimate(flops=terms * 2 * K * TILE * TILE, bytes_accessed=terms * TILE * TILE * 2, transcendentals=0),
        name="product",
    )(places, own_rows, own_cols, xt, own, slots)


def inverse_factor(gram):
    eye = (lax.broadcasted_iota(jnp.int32, (K, K), 0) == lax.broadcasted_iota(jnp.int32, (K, K), 1)).astype(F32)
    work = jnp.concatenate([gram, eye], axis=1)
    index = lax.broadcasted_iota(jnp.int32, (K, 1), 0)
    pivots = jnp.ones((K, 1), F32)
    for j in range(0, K, 2):
        first_row, first_col = work[j:j + 1, :], work[:, j:j + 1]
        second_col = work[:, j + 1:j + 2]
        pivot, below = first_col[j:j + 1], first_col[j + 1:j + 2]
        beside = second_col[j:j + 1]
        inverse = 1.0 / pivot
        step = below * inverse
        second_row = work[j + 1:j + 2, :] - step * first_row
        second_pivot = second_col[j + 1:j + 2] - step * beside
        first_factor = jnp.where(index > j, first_col * inverse, 0.0)
        second_factor = jnp.where(index > j + 1, (second_col - first_factor * beside) * (1.0 / second_pivot), 0.0)
        pivots = jnp.where(index == j, pivot, jnp.where(index == j + 1, second_pivot, pivots))
        work = work - first_factor * first_row - second_factor * second_row
    return lax.rsqrt(pivots) * work[:, K:]


def gram_pack(gram):
    return jnp.concatenate([gram[:K // 2], gram[K // 2:]], axis=1)


def gram_unpack(packed):
    return jnp.concatenate([packed[:, :K], packed[:, K:]], axis=0)


def normalize_kernel(first, last, part_ref, degree_in_ref, *rest):
    rest = list(rest)
    take = lambda count: [rest.pop(0) for _ in range(count)]
    gram_in_ref = None if first else rest.pop(0)
    if last:
        (z_ref,) = take(1)
    else:
        xt_ref, gram_ref = take(2)
    degree_ref = rest.pop(0) if first else degree_in_ref
    y_ref, s1_ref, a1_ref, s2_ref, a2_ref, v_ref, g1_ref, g2_ref, g3_ref = take(9)
    s1_send, s1_recv, s2_send, s2_recv, g_send, g_recv = take(6)
    if first:
        dg_ref, dg_own, dg_send, dg_recv = take(4)
    if not last:
        xs_ref, xc_ref = take(2)
        sems = dict(zip(X_SEMS, rest))
    row = lax.axis_index("row")
    col = lax.axis_index("col")
    x, y = col // 4, lax.rem(col, 4)
    x_peer = lambda k: lax.rem(x + k, 4) * 4 + y
    y_peer = lambda k: x * 4 + lax.rem(y + k, 4)
    greet(row, col)

    ways = ((1, 3) * 3)

    def ring(stage, h, message):
        along_x = (h == 0) == (stage == 1)
        k = ways[message]
        src, dst, send_sem, recv_sem = (s1_ref, a1_ref, s1_send, s1_recv) if stage == 1 else (s2_ref, a2_ref, s2_send, s2_recv)
        return remote(src.at[h, message], dst.at[h, message], send_sem.at[h, message], recv_sem.at[h, message],
                      col=x_peer(k) if along_x else y_peer(k))

    def arrived(stage, h, message):
        dst, recv_sem = (a1_ref, s1_recv) if stage == 1 else (a2_ref, s2_recv)
        wait_bytes(dst.at[h, message], recv_sem.at[h, message])

    def mine(h, k, other, half):
        target = lax.rem((y if h else x) + k, 4)
        blocks = slice(h * 8 + half * 4, h * 8 + half * 4 + 4)
        return part_ref[other, target, blocks] if h else part_ref[target, other, blocks]

    plan = ((0, 2, 0), (1, 2, 1), (2, 1, 1), (3, 3, 0))
    for message, k, half in plan:
        for h in range(2):
            def narrow(other, carry):
                s1_ref[h, message, other] = mine(h, k, other, half).astype(BF)
                return carry

            lax.fori_loop(0, 4, narrow, 0)
            ring(1, h, message).start()
    if first:
        pltpu.make_async_copy(degree_in_ref.at[pl.ds(col * 16, 16)], dg_ref.at[col], dg_own).start()

        def send(k, carry):
            peer = col_peer(col, k)
            remote(degree_in_ref.at[pl.ds(peer * 16, 16)], dg_ref.at[col], dg_send, dg_recv, col=peer).start()
            return carry

        lax.fori_loop(1, NC, send, 0)
    else:
        inverse = inverse_factor(gram_unpack(gram_in_ref[...]))
    for message, k, half in ((4, 1, 0), (5, 3, 1)):
        for h in range(2):
            arrived(1, h, message - 4)

            def pass_on(other, carry):
                s1_ref[h, message, other] = (mine(h, k, other, half) + a1_ref[h, message - 4, other].astype(F32)).astype(BF)
                return carry

            lax.fori_loop(0, 4, pass_on, 0)
            ring(1, h, message).start()
    for h in range(2):
        for message in range(2, 6):
            arrived(1, h, message)
        place = x if h else y

        def value(k, half):
            other = lax.rem(place + k, 4)
            near, far = (3, 4) if half == 0 else (2, 5)
            return mine(h, 0, other, half) + a1_ref[h, near, other].astype(F32) + a1_ref[h, far, other].astype(F32)

        for message, k, half in plan:
            s2_ref[h, message] = value(k, half).astype(BF)
            ring(2, h, message).start()
        v_ref[h, 0] = value(1, 0)
        v_ref[h, 1] = value(3, 1)
        for half in range(2):
            y_ref[h * 8 + half * 4:h * 8 + half * 4 + 4] = value(0, half)
    for h in range(2):
        for message in (4, 5):
            arrived(2, h, message - 4)
            s2_ref[h, message] = (v_ref[h, message - 4] + a2_ref[h, message - 4].astype(F32)).astype(BF)
            ring(2, h, message).start()
    if first:
        pltpu.make_async_copy(degree_in_ref.at[pl.ds(col * 16, 16)], dg_ref.at[col], dg_own).wait()
        wait_bytes(dg_ref.at[pl.ds(0, NC - 1)], dg_recv)
        degree = dg_ref[0]
        for k in range(1, NC):
            degree = degree + dg_ref[k]
        degree_ref[...] = 1.0 + degree
    for h in range(2):
        for message in range(2, 6):
            arrived(2, h, message)
        for b in range(8):
            near, far = (3, 4) if b < 4 else (2, 5)
            value = y_ref[h * 8 + b] + a2_ref[h, near, b % 4].astype(F32) + a2_ref[h, far, b % 4].astype(F32)
            value = value * (1.0 / degree_ref[h * 8 + b:h * 8 + b + 1])
            if not first:
                value = dot(inverse, value, ((1,), (0,)), lax.Precision.HIGHEST)
            y_ref[h * 8 + b] = value

    if not last:
        x_pieces(lambda b: y_ref[b], xs_ref)
        x_first(row, col, xs_ref, xc_ref, sems)

    gram = jnp.zeros((K, K), F32)
    for b in range(16):
        block = y_ref[b]
        gram = gram + dot(block, block, ((1,), (1,)), lax.Precision.HIGHEST)

    def share(buffer, place, value, peers, base):
        buffer[place] = value
        for i, peer in enumerate(peers):
            remote(buffer.at[place], buffer.at[place], g_send.at[base + i], g_recv.at[base], **peer).start()

    def collect(buffer, count, base):
        wait_bytes(buffer.at[pl.ds(0, count - 1)], g_recv.at[base])
        total = buffer[0]
        for k in range(1, count):
            total = total + buffer[k]
        return total

    share(g1_ref, x, gram_pack(gram), [dict(col=x_peer(k)) for k in (1, 3, 2)], 0)
    if not last:
        x_second(row, col, xs_ref, xc_ref, sems)
    share(g2_ref, y, collect(g1_ref, 4, 0), [dict(col=y_peer(k)) for k in (1, 3, 2)], 3)
    share(g3_ref, row, collect(g2_ref, 4, 3), [dict(row=row_peer(row, dz, flip)) for dz, flip in ROW_ORDER], 6)
    if not last:
        x_third(row, col, xs_ref, xc_ref, sems)
    total = collect(g3_ref, NR, 6) * (1.0 / NODES)
    if last:
        final = inverse_factor(gram_unpack(total))
        for b in range(16):
            z_ref[:, b * TILE:(b + 1) * TILE] = dot(final, y_ref[b], ((1,), (0,)), lax.Precision.HIGHEST)
    else:
        gram_ref[...] = total
        x_finish(row, col, xs_ref, xc_ref, xt_ref, sems)
    for h in range(2):
        for message in range(6):
            wait_bytes(a1_ref.at[h, message], s1_send.at[h, message])
            wait_bytes(a2_ref.at[h, message], s2_send.at[h, message])
    if first:
        wait_bytes(dg_ref.at[pl.ds(0, NC - 1)], dg_send)
    for i in range(13):
        wait_bytes(g1_ref.at[0], g_send.at[i])


def normalize(first, last, part, degree, gram):
    dma = pltpu.SemaphoreType.DMA
    half = (K // 2, TILE)
    out_shape, out_specs = [], []
    if last:
        out_shape.append(jax.ShapeDtypeStruct((K, 16 * TILE), F32))
        out_specs.append(VMEM)
    else:
        out_shape += [pltpu.VMEM((X_BLOCKS, K, TILE), BF), jax.ShapeDtypeStruct(half, F32)]
        out_specs += [VMEM, VMEM]
    if first:
        out_shape.append(jax.ShapeDtypeStruct((16, TILE), F32))
        out_specs.append(VMEM)
    scratch = [
        pltpu.VMEM((16, K, TILE), F32), pltpu.VMEM((2, 6, 4, 4, K, TILE), BF), pltpu.VMEM((2, 6, 4, 4, K, TILE), BF),
        pltpu.VMEM((2, 6, 4, K, TILE), BF), pltpu.VMEM((2, 6, 4, K, TILE), BF), pltpu.VMEM((2, 2, 4, K, TILE), F32),
        pltpu.VMEM((4,) + half, F32), pltpu.VMEM((4,) + half, F32), pltpu.VMEM((NR,) + half, F32),
        dma((2, 6)), dma((2, 6)), dma((2, 6)), dma((2, 6)), dma((13,)), dma((13,)),
    ]
    if first:
        scratch += [pltpu.VMEM((NC, 16, TILE), F32), dma, dma, dma]
    if not last:
        scratch += [pltpu.VMEM((NC, 4, 16, TILE), BF), pltpu.VMEM((NR, NC, 4, 16, TILE), BF)] + x_sems()
    args = [part.reshape(4, 4, 16, K, TILE), degree] + ([] if first else [gram])
    return pl.pallas_call(
        functools.partial(normalize_kernel, first, last),
        out_shape=out_shape,
        in_specs=[VMEM, VMEM] + ([] if first else [VMEM]),
        out_specs=out_specs,
        scratch_shapes=scratch,
        compiler_params=pltpu.CompilerParams(
            collective_id=1 if first else (3 if last else 2), has_side_effects=True, vmem_limit_bytes=16 * MIB
        ),
        name="normalize",
    )(*args)


def block_index(block):
    return block // 32 * 32 + block % 16 * 2 + block // 16 % 2


def local(embed, tiles, tile_rows, tile_cols, chg_tiles, chg_rows, chg_cols):
    owners = chg_cols // 256 * NC + chg_rows // 128
    count = owners.shape[0]
    position = jnp.arange(count, dtype=jnp.int32)
    earlier = position[None, :] < position[:, None]
    rank = jnp.sum(jnp.logical_and(owners[:, None] == owners[None, :], earlier).astype(jnp.int32), axis=1)
    key = owners * CAP + rank
    hit = jnp.arange(DEV * CAP, dtype=jnp.int32)[:, None] == key[None, :]
    pick = jnp.sum(jnp.where(hit, position[None, :], 0), axis=1)
    code = jnp.sum(jnp.where(hit, (1 + chg_cols % 256 * 128 + block_index(chg_rows % 128))[None, :], 0), axis=1)
    slot_rows = jnp.where(code > 0, (code - 1) // 128, 0).reshape(DEV, CAP)
    slot_cols = jnp.where(code > 0, (code - 1) % 128, 128).reshape(DEV, CAP)
    meta = jnp.concatenate([slot_rows, slot_cols], axis=1).reshape(NR, NC, 2 * CAP).transpose(1, 0, 2)
    meta = jnp.pad(meta, ((0, 0), (0, 0), (0, TILE - 2 * CAP)))
    slots, tiles, places, xc = exchange(pick, chg_tiles, tiles, meta, embed.T)
    own_rows = tile_rows % 256
    own_cols = block_index(tile_cols % 128)
    part, degree = product(True, places, own_rows, own_cols, xc, tiles, slots)
    xc, gram, degree = normalize(True, False, part, degree, None)
    for iteration in range(1, ITERS):
        (part,) = product(False, places, own_rows, own_cols, xc, tiles, slots)
        last = iteration == ITERS - 1
        outs = normalize(False, last, part, degree, gram)
        if last:
            return outs[0].T
        xc, gram = outs


def solution(mesh):
    placed = (
        P(("row", "col"), None),
        P(("row", "col"), None, None),
        P(("row", "col")),
        P(("row", "col")),
        P(("row", "col"), None, None),
        P(("row", "col")),
        P(("row", "col")),
    )
    return jax.shard_map(
        local, mesh=mesh, in_specs=placed, out_specs=P(("row", "col"), None), check_vma=False
    )
```

```python
import functools

import jax
import jax.numpy as jnp
from jax import lax
from jax.experimental import pallas as pl
from jax.experimental.pallas import tpu as pltpu
from jax.sharding import PartitionSpec as P

ITERS = 3
CAP = 3
K = 64
TILE = 128
NR = 8
NC = 16
DEV = NR * NC
ROWS_BLK = 256
SLOT_ROWS = CAP * TILE
X_BLOCKS = 130
OWN = 64
NODES = 262144
BF = jnp.bfloat16
F32 = jnp.float32
ANY = pl.BlockSpec(memory_space=pl.ANY)

VMEM = pl.BlockSpec(memory_space=pltpu.VMEM)
SMEM = pl.BlockSpec(memory_space=pltpu.SMEM)
MIB = 1024 * 1024
ROW_ORDER = ((2, 0), (1, 1), (3, 0), (2, 1), (1, 0), (3, 1), (0, 1))


def dot(a, b, dims, precision=None):
    return lax.dot_general(a, b, (dims, ((), ())), precision=precision, preferred_element_type=F32)


def greet(row, col):
    barrier = pltpu.get_barrier_semaphore()

    def cols(k, carry):
        pl.semaphore_signal(barrier, inc=1, device_id={"col": lax.rem(col + k, NC)}, device_id_type=pl.DeviceIdType.MESH)
        return carry

    def rows(k, carry):
        pl.semaphore_signal(barrier, inc=1, device_id={"row": lax.rem(row + k, NR)}, device_id_type=pl.DeviceIdType.MESH)
        return carry

    lax.fori_loop(1, NC, cols, 0)
    lax.fori_loop(1, NR, rows, 0)
    pl.semaphore_wait(barrier, NC + NR - 2)


def remote(src, dst, send_sem, recv_sem, **peer):
    return pltpu.make_async_remote_copy(
        src_ref=src, dst_ref=dst, send_sem=send_sem, recv_sem=recv_sem,
        device_id=peer, device_id_type=pl.DeviceIdType.MESH,
    )


def wait_bytes(ref, sem):
    pltpu.make_async_copy(ref, ref, sem).wait()


def col_peer(col, k):
    return lax.rem(col // 4 + k // 4, 4) * 4 + lax.rem(lax.rem(col, 4) + lax.rem(k, 4), 4)


def row_peer(row, dz, flip=0):
    return lax.rem(row // 2 + dz, 4) * 2 + lax.rem(row + flip, 2)


def x_pieces(batch, block, xs):
    for i in range(2):
        for part in range(2):
            pair = batch * 2 + i
            both = jnp.concatenate([block(pair * 4 + part), block(pair * 4 + 2 + part)], axis=0).T
            xs[batch, part * 8:(part + 1) * 8, i] = both.astype(BF).reshape(8, 16, TILE)


def x_own_copy(batch, row, col, xs, xc, sems):
    return pltpu.make_async_copy(xs.at[batch, col], xc.at[batch, row, col], sems["x_own"].at[batch])


def x_first(batch, row, col, xs, xc, sems):
    x_own_copy(batch, row, col, xs, xc, sems).start()

    def send(k, carry):
        peer = col_peer(col, k)
        remote(xs.at[batch, peer], xc.at[batch, row, col], sems["xa_send"].at[batch], sems["xa_recv"].at[batch], col=peer).start()
        return carry

    lax.fori_loop(1, NC, send, 0)


def x_second(batch, row, col, xs, xc, sems):
    x_own_copy(batch, row, col, xs, xc, sems).wait()
    wait_bytes(xc.at[batch, row, pl.ds(0, NC - 1)], sems["xa_recv"].at[batch])
    for i, (dz, flip) in enumerate(((1, 0), (3, 0), (2, 0), (0, 1))):
        remote(xc.at[batch, row], xc.at[batch, row], sems["xb_send"].at[batch, i], sems["xb_recv"].at[batch, row],
               row=row_peer(row, dz, flip)).start()


def x_third(batch, row, col, xs, xc, sems):
    for i, dz in enumerate((1, 3, 2)):
        source = row_peer(row, dz)
        wait_bytes(xc.at[batch, source], sems["xb_recv"].at[batch, source])
        remote(xc.at[batch, source], xc.at[batch, source], sems["xb_send"].at[batch, 4 + i], sems["xb_recv"].at[batch, source],
               row=row_peer(row, 0, 1)).start()


def x_finish(batch, row, col, xs, xc, xt, sems):
    for dz in range(4):
        turn(batch, row_peer(row, dz), xc, xt)
    for dz in (0, 1, 3, 2):
        source = row_peer(row, dz, 1)
        wait_bytes(xc.at[batch, source], sems["xb_recv"].at[batch, source])
        turn(batch, source, xc, xt)
    wait_bytes(xs.at[batch, pl.ds(0, NC - 1)], sems["xa_send"].at[batch])
    for i in range(7):
        wait_bytes(xc.at[batch, row], sems["xb_send"].at[batch, i])
    if batch:
        xt[X_BLOCKS - 2:] = jnp.zeros((2, K, TILE), BF)


def turn(batch, source, xc, xt):
    for part in range(2):
        for i in range(2):
            block = xc[batch, source, part * 8:(part + 1) * 8, i].reshape(TILE, TILE)
            xt[pl.ds(((batch * 2 + i) * 16 + source * 2 + part) * 2, 2)] = block.T.reshape(2, K, TILE)


X_SEMS = ("x_own", "xa_send", "xa_recv", "xb_send", "xb_recv")


def x_sems():
    dma = pltpu.SemaphoreType.DMA
    return [dma((2,)), dma((2,)), dma((2,)), dma((2, 7)), dma((2, NR))]


XS_SHAPE = (2, NC, 2, 16, TILE)
XC_SHAPE = (2, NR, NC, 2, 16, TILE)


def exchange_kernel(pick_ref, tiles_in_ref, own_in_ref, meta_ref, embed_ref,
                    recv_ref, mid_ref, far_ref, own_out_ref, places_ref, xt_ref,
                    send_ref, xc_ref, meta_mid_ref, meta_next_ref, xs_ref, tiles_ref, own_ref, tiles_sem, own_load_sem, *sem_refs):
    sems = dict(zip(X_SEMS, sem_refs))
    (a_send, a_recv, b_send, b_recv, c_send, c_recv, d_send, d_recv,
     m_send, m_recv, n_send, n_recv, own_sem, far_sem) = sem_refs[len(X_SEMS):]
    load_tiles = pltpu.make_async_copy(tiles_in_ref, tiles_ref, tiles_sem)
    load_own = pltpu.make_async_copy(own_in_ref, own_ref, own_load_sem)
    load_tiles.start()
    load_own.start()
    half = SLOT_ROWS // 2
    head, tail = pl.ds(0, half), pl.ds(half, half)
    row = lax.axis_index("row")
    col = lax.axis_index("col")
    greet(row, col)
    for batch in range(2):
        x_pieces(batch, lambda b: embed_ref[:, b * TILE:(b + 1) * TILE], xs_ref)
        x_first(batch, row, col, xs_ref, xc_ref, sems)
    targets = [row_peer(row, dz, flip) for dz, flip in ROW_ORDER] + [row]
    sources = [row_peer(row, (4 - dz) % 4, flip) for dz, flip in ROW_ORDER]

    def send_meta(k, carry):
        peer = col_peer(col, k)
        remote(meta_ref.at[peer], meta_mid_ref.at[col], m_send, m_recv, col=peer).start()
        return carry

    lax.fori_loop(1, NC, send_meta, 0)
    meta_mid_ref[col] = meta_ref[col]

    def fill(target):
        def tiles(c, carry):
            for slot in range(CAP):
                send_ref[target, c, slot * TILE:(slot + 1) * TILE] = tiles_ref[pick_ref[(target * NC + c) * CAP + slot]]
            return carry

        lax.fori_loop(0, NC, tiles, 0)

    def first_own(step):
        target = targets[step]
        if step < NR - 1:
            return pltpu.make_async_copy(send_ref.at[target, col, head], mid_ref.at[target, col], own_sem.at[step])
        return pltpu.make_async_copy(send_ref.at[target, col, head], recv_ref.at[target, col, head], own_sem.at[step])

    def first(step):
        target = targets[step]

        def send(k, carry):
            peer = col_peer(col, k)
            dst = mid_ref.at[target, col] if step < NR - 1 else recv_ref.at[target, col, head]
            remote(send_ref.at[target, peer, head], dst, a_send.at[step], a_recv.at[step], col=peer).start()
            return carry

        lax.fori_loop(1, NC, send, 0)
        first_own(step).start()

    def second_own(step):
        if step < NR - 1:
            return pltpu.make_async_copy(far_ref.at[sources[step], col], recv_ref.at[sources[step], col, tail], far_sem.at[step])
        return pltpu.make_async_copy(send_ref.at[row, col, tail], recv_ref.at[row, col, tail], far_sem.at[step])

    def second(step):
        def send(k, carry):
            peer = col_peer(col, k)
            source = sources[step] if step < NR - 1 else row
            src = far_ref.at[source, peer] if step < NR - 1 else send_ref.at[row, peer, tail]
            remote(src, recv_ref.at[source, col, tail], d_send.at[step], d_recv.at[source], col=peer).start()
            return carry

        lax.fori_loop(1, NC, send, 0)
        second_own(step).start()

    load_tiles.wait()
    for step in range(NR):
        fill(targets[step])
        if step < NR - 1:
            remote(send_ref.at[targets[step], :, tail], far_ref.at[row], c_send.at[step], c_recv.at[row], row=targets[step]).start()
            first(step)
        if step < 2:
            x_second(step, row, col, xs_ref, xc_ref, sems)
    wait_bytes(meta_mid_ref.at[pl.ds(0, NC - 1)], m_recv)
    for c in range(NC):
        for r in range(NR):
            meta_next_ref[r, c:c + 1] = meta_mid_ref[c, r:r + 1]
    for step in range(NR - 1):
        remote(meta_next_ref.at[targets[step]], places_ref.at[row], n_send, n_recv, row=targets[step]).start()
    places_ref[row] = meta_next_ref[row]
    for batch in range(2):
        x_third(batch, row, col, xs_ref, xc_ref, sems)

    def flip_own(i, carry):
        for u in range(4):
            own_out_ref[i * 4 + u] = own_ref[i * 4 + u].T
        return carry

    load_own.wait()
    lax.fori_loop(0, OWN // 4, flip_own, 0)
    for step in range(NR - 1):
        target, source = targets[step], sources[step]
        wait_bytes(mid_ref.at[target, pl.ds(0, NC - 1)], a_recv.at[step])
        first_own(step).wait()
        remote(mid_ref.at[target], recv_ref.at[row, :, head], b_send.at[step], b_recv.at[row], row=target).start()
        wait_bytes(far_ref.at[source], c_recv.at[source])
        second(step)
    first(NR - 1)
    second(NR - 1)
    for batch in range(2):
        x_finish(batch, row, col, xs_ref, xc_ref, xt_ref, sems)
    some = mid_ref.at[0, pl.ds(0, NC - 1)]
    wait_bytes(some, a_recv.at[NR - 1])
    first_own(NR - 1).wait()
    wait_bytes(meta_mid_ref.at[pl.ds(0, NC - 1)], m_send)
    wait_bytes(places_ref.at[pl.ds(0, NR - 1)], n_send)
    wait_bytes(places_ref.at[pl.ds(0, NR - 1)], n_recv)
    for step in range(NR):
        wait_bytes(some, a_send.at[step])
        wait_bytes(some, d_send.at[step])
        wait_bytes(some, d_recv.at[sources[step] if step < NR - 1 else row])
        second_own(step).wait()
    for step in range(NR - 1):
        wait_bytes(mid_ref.at[0], b_send.at[step])
        wait_bytes(mid_ref.at[0], c_send.at[step])
        wait_bytes(mid_ref.at[0], b_recv.at[targets[step]])


def exchange(pick, chg_tiles, own, meta, xs):
    dma = pltpu.SemaphoreType.DMA
    slots = (NR, NC, SLOT_ROWS, TILE)
    halves = jax.ShapeDtypeStruct((NR, NC, SLOT_ROWS // 2, TILE), BF)
    recv, _, _, own, places, xt = pl.pallas_call(
        exchange_kernel,
        out_shape=(jax.ShapeDtypeStruct(slots, BF), halves, halves, pltpu.VMEM((OWN, TILE, TILE), BF),
                   jax.ShapeDtypeStruct((NR, NC, TILE), jnp.int32), pltpu.VMEM((X_BLOCKS, K, TILE), BF)),
        in_specs=[SMEM, ANY, ANY, VMEM, VMEM],
        out_specs=(ANY, ANY, ANY, VMEM, VMEM, VMEM),
        scratch_shapes=[
            pltpu.VMEM(slots, BF), pltpu.VMEM(XC_SHAPE, BF),
            pltpu.VMEM((NC, NR, TILE), jnp.int32), pltpu.VMEM((NR, NC, TILE), jnp.int32),
            pltpu.VMEM(XS_SHAPE, BF), pltpu.VMEM(chg_tiles.shape, BF), pltpu.VMEM(own.shape, BF), dma, dma,
        ] + x_sems() + [dma((NR,))] * 8 + [dma, dma, dma, dma, dma((NR,)), dma((NR,))],
        compiler_params=pltpu.CompilerParams(collective_id=0, has_side_effects=True, vmem_limit_bytes=58 * MIB),
        name="exchange",
    )(pick, chg_tiles, own, meta, xs)
    return recv, own, places, xt


def product_kernel(with_degree, places_ref, own_rows_ref, own_cols_ref, xt_ref, own_ref, slots_in_ref, acc_ref, *rest):
    slots_ref, slot_sem, table_ref, table_sem = rest[-4:]
    load_table = pltpu.make_async_copy(places_ref, table_ref, table_sem)
    load_table.start()
    loads = [
        pltpu.make_async_copy(slots_in_ref.at[i], slots_ref.at[i], slot_sem.at[i])
        for i in range(NR)
    ]
    for load in loads:
        load.start()
    ones = jnp.ones((8, TILE), BF)
    plain = ((1,), (0,))
    if with_degree:
        degree_out_ref, degree_ref = rest[:2]
        degree_ref[...] = jnp.zeros_like(degree_ref)

    def clear(i, carry):
        acc_ref[pl.ds(i * 8, 8)] = jnp.zeros((8, K, TILE), F32)
        return carry

    lax.fori_loop(0, ROWS_BLK // 8, clear, 0)

    def run(tiles, rows, cols):
        values = [dot(xt_ref[col], tile, plain) for tile, col in zip(tiles, cols)]
        sums = []
        if with_degree:
            sums = [
                dot(jnp.where(col < 128, ones, jnp.zeros_like(ones)), jnp.abs(tile), plain)[0:1]
                for tile, col in zip(tiles, cols)
            ]
        for row, value in zip(rows, values):
            acc_ref[row] += value
        for row, value in zip(rows, sums):
            degree_ref[row] += value

    def own(i, carry):
        places = [i * 16 + u for u in range(16)]
        run([own_ref[n] for n in places], [own_rows_ref[n] for n in places], [own_cols_ref[n] for n in places])
        return carry

    def taken(group, carry):
        places = [(source, slot) for source in range(NC) for slot in range(CAP)]
        run([slots_ref[group, source, slot * TILE:(slot + 1) * TILE] for source, slot in places],
            [table_ref[group, source, slot] for source, slot in places],
            [table_ref[group, source, CAP + slot] for source, slot in places])
        return carry

    lax.fori_loop(0, OWN // 16, own, 0)
    load_table.wait()
    for i, load in enumerate(loads):
        load.wait()
        lax.fori_loop(i, i + 1, taken, 0)
    if with_degree:
        degree_out_ref[...] = degree_ref[...].reshape(ROWS_BLK, TILE)


def product(with_degree, places, own_rows, own_cols, xt, own, slots):
    out_shape = [pltpu.VMEM((ROWS_BLK, K, TILE), F32)]
    if with_degree:
        out_shape.append(jax.ShapeDtypeStruct((ROWS_BLK, TILE), F32))
    terms = DEV * CAP + OWN
    return pl.pallas_call(
        functools.partial(product_kernel, with_degree),
        out_shape=out_shape,
        in_specs=[VMEM, SMEM, SMEM, VMEM, VMEM, ANY],
        out_specs=[VMEM] * len(out_shape),
        scratch_shapes=([pltpu.VMEM((ROWS_BLK, 1, TILE), F32)] if with_degree else []) + [
            pltpu.VMEM((NR, NC, SLOT_ROWS, TILE), BF), pltpu.SemaphoreType.DMA((NR,)),
            pltpu.SMEM((NR, NC, TILE), jnp.int32), pltpu.SemaphoreType.DMA,
        ],
        compiler_params=pltpu.CompilerParams(vmem_limit_bytes=40 * MIB),
        cost_estimate=pl.CostEstimate(flops=terms * 2 * K * TILE * TILE, bytes_accessed=terms * TILE * TILE * 2, transcendentals=0),
        name="product",
    )(places, own_rows, own_cols, xt, own, slots)


def inverse_factor(gram):
    eye = (lax.broadcasted_iota(jnp.int32, (K, K), 0) == lax.broadcasted_iota(jnp.int32, (K, K), 1)).astype(F32)
    work = jnp.concatenate([gram, eye], axis=1)
    index = lax.broadcasted_iota(jnp.int32, (K, 1), 0)
    pivots = jnp.ones((K, 1), F32)
    for j in range(0, K, 2):
        first_row, first_col = work[j:j + 1, :], work[:, j:j + 1]
        second_col = work[:, j + 1:j + 2]
        pivot, below = first_col[j:j + 1], first_col[j + 1:j + 2]
        beside = second_col[j:j + 1]
        inverse = 1.0 / pivot
        step = below * inverse
        second_row = work[j + 1:j + 2, :] - step * first_row
        second_pivot = second_col[j + 1:j + 2] - step * beside
        first_factor = jnp.where(index > j, first_col * inverse, 0.0)
        second_factor = jnp.where(index > j + 1, (second_col - first_factor * beside) * (1.0 / second_pivot), 0.0)
        pivots = jnp.where(index == j, pivot, jnp.where(index == j + 1, second_pivot, pivots))
        work = work - first_factor * first_row - second_factor * second_row
    return lax.rsqrt(pivots) * work[:, K:]


def gram_pack(gram):
    return jnp.concatenate([gram[:K // 2], gram[K // 2:]], axis=1)


def gram_unpack(packed):
    return jnp.concatenate([packed[:, :K], packed[:, K:]], axis=0)


def normalize_kernel(first, last, part_ref, degree_in_ref, *rest):
    rest = list(rest)
    take = lambda count: [rest.pop(0) for _ in range(count)]
    gram_in_ref = None if first else rest.pop(0)
    if last:
        (z_ref,) = take(1)
    else:
        xt_ref, gram_ref = take(2)
    degree_ref = rest.pop(0) if first else degree_in_ref
    y_ref, s1_ref, a1_ref, s2_ref, a2_ref, v_ref, g1_ref, g2_ref, g3_ref = take(9)
    s1_send, s1_recv, s2_send, s2_recv, g_send, g_recv = take(6)
    if first:
        dg_ref, dg_own, dg_send, dg_recv = take(4)
    if not last:
        xs_ref, xc_ref = take(2)
        sems = dict(zip(X_SEMS, rest))
    row = lax.axis_index("row")
    col = lax.axis_index("col")
    x, y = col // 4, lax.rem(col, 4)
    x_peer = lambda k: lax.rem(x + k, 4) * 4 + y
    y_peer = lambda k: x * 4 + lax.rem(y + k, 4)
    greet(row, col)

    ways = ((1, 3) * 3)

    def ring(stage, h, message):
        along_x = (h == 0) == (stage == 1)
        k = ways[message]
        src, dst, send_sem, recv_sem = (s1_ref, a1_ref, s1_send, s1_recv) if stage == 1 else (s2_ref, a2_ref, s2_send, s2_recv)
        return remote(src.at[h, message], dst.at[h, message], send_sem.at[h, message], recv_sem.at[h, message],
                      col=x_peer(k) if along_x else y_peer(k))

    def arrived(stage, h, message):
        dst, recv_sem = (a1_ref, s1_recv) if stage == 1 else (a2_ref, s2_recv)
        wait_bytes(dst.at[h, message], recv_sem.at[h, message])

    def mine(h, k, other, half):
        target = lax.rem((y if h else x) + k, 4)
        blocks = slice(h * 8 + half * 4, h * 8 + half * 4 + 4)
        return part_ref[other, target, blocks] if h else part_ref[target, other, blocks]

    plan = ((0, 2, 0), (1, 2, 1), (2, 1, 1), (3, 3, 0))
    for message, k, half in plan:
        for h in range(2):
            def narrow(other, carry):
                s1_ref[h, message, other] = mine(h, k, other, half).astype(BF)
                return carry

            lax.fori_loop(0, 4, narrow, 0)
            ring(1, h, message).start()
    if first:
        pltpu.make_async_copy(degree_in_ref.at[pl.ds(col * 16, 16)], dg_ref.at[col], dg_own).start()

        def send(k, carry):
            peer = col_peer(col, k)
            remote(degree_in_ref.at[pl.ds(peer * 16, 16)], dg_ref.at[col], dg_send, dg_recv, col=peer).start()
            return carry

        lax.fori_loop(1, NC, send, 0)
    else:
        inverse = inverse_factor(gram_unpack(gram_in_ref[...]))
    for message, k, half in ((4, 1, 0), (5, 3, 1)):
        for h in range(2):
            arrived(1, h, message - 4)

            def pass_on(other, carry):
                s1_ref[h, message, other] = (mine(h, k, other, half) + a1_ref[h, message - 4, other].astype(F32)).astype(BF)
                return carry

            lax.fori_loop(0, 4, pass_on, 0)
            ring(1, h, message).start()
    for h in range(2):
        for message in range(2, 6):
            arrived(1, h, message)
        place = x if h else y

        def value(k, half):
            other = lax.rem(place + k, 4)
            near, far = (3, 4) if half == 0 else (2, 5)
            return mine(h, 0, other, half) + a1_ref[h, near, other].astype(F32) + a1_ref[h, far, other].astype(F32)

        for message, k, half in plan:
            s2_ref[h, message] = value(k, half).astype(BF)
            ring(2, h, message).start()
        v_ref[h, 0] = value(1, 0)
        v_ref[h, 1] = value(3, 1)
        for half in range(2):
            y_ref[h * 8 + half * 4:h * 8 + half * 4 + 4] = value(0, half)
    for h in range(2):
        for message in (4, 5):
            arrived(2, h, message - 4)
            s2_ref[h, message] = (v_ref[h, message - 4] + a2_ref[h, message - 4].astype(F32)).astype(BF)
            ring(2, h, message).start()
    if first:
        pltpu.make_async_copy(degree_in_ref.at[pl.ds(col * 16, 16)], dg_ref.at[col], dg_own).wait()
        wait_bytes(dg_ref.at[pl.ds(0, NC - 1)], dg_recv)
        degree = dg_ref[0]
        for k in range(1, NC):
            degree = degree + dg_ref[k]
        degree_ref[...] = 1.0 + degree
    for h in range(2):
        for message in range(2, 6):
            arrived(2, h, message)
        for b in range(8):
            near, far = (3, 4) if b < 4 else (2, 5)
            value = y_ref[h * 8 + b] + a2_ref[h, near, b % 4].astype(F32) + a2_ref[h, far, b % 4].astype(F32)
            value = value * (1.0 / degree_ref[h * 8 + b:h * 8 + b + 1])
            if not first:
                value = dot(inverse, value, ((1,), (0,)), lax.Precision.HIGHEST)
            y_ref[h * 8 + b] = value
        if not last:
            x_pieces(h, lambda b: y_ref[b], xs_ref)
            x_first(h, row, col, xs_ref, xc_ref, sems)

    if not last:
        x_second(0, row, col, xs_ref, xc_ref, sems)

    gram = jnp.zeros((K, K), F32)
    for b in range(16):
        block = y_ref[b]
        gram = gram + dot(block, block, ((1,), (1,)), lax.Precision.HIGHEST)

    def share(buffer, place, value, peers, base):
        buffer[place] = value
        for i, peer in enumerate(peers):
            remote(buffer.at[place], buffer.at[place], g_send.at[base + i], g_recv.at[base], **peer).start()

    def collect(buffer, count, base):
        wait_bytes(buffer.at[pl.ds(0, count - 1)], g_recv.at[base])
        total = buffer[0]
        for k in range(1, count):
            total = total + buffer[k]
        return total

    share(g1_ref, x, gram_pack(gram), [dict(col=x_peer(k)) for k in (1, 3, 2)], 0)
    if not last:
        x_second(1, row, col, xs_ref, xc_ref, sems)
    share(g2_ref, y, collect(g1_ref, 4, 0), [dict(col=y_peer(k)) for k in (1, 3, 2)], 3)
    share(g3_ref, row, collect(g2_ref, 4, 3), [dict(row=row_peer(row, dz, flip)) for dz, flip in ROW_ORDER], 6)
    if not last:
        x_third(0, row, col, xs_ref, xc_ref, sems)
        x_third(1, row, col, xs_ref, xc_ref, sems)
    total = collect(g3_ref, NR, 6) * (1.0 / NODES)
    if last:
        final = inverse_factor(gram_unpack(total))
        for b in range(16):
            z_ref[:, b * TILE:(b + 1) * TILE] = dot(final, y_ref[b], ((1,), (0,)), lax.Precision.HIGHEST)
    else:
        gram_ref[...] = total
        x_finish(0, row, col, xs_ref, xc_ref, xt_ref, sems)
        x_finish(1, row, col, xs_ref, xc_ref, xt_ref, sems)
    for h in range(2):
        for message in range(6):
            wait_bytes(a1_ref.at[h, message], s1_send.at[h, message])
            wait_bytes(a2_ref.at[h, message], s2_send.at[h, message])
    if first:
        wait_bytes(dg_ref.at[pl.ds(0, NC - 1)], dg_send)
    for i in range(13):
        wait_bytes(g1_ref.at[0], g_send.at[i])


def normalize(first, last, part, degree, gram):
    dma = pltpu.SemaphoreType.DMA
    half = (K // 2, TILE)
    out_shape, out_specs = [], []
    if last:
        out_shape.append(jax.ShapeDtypeStruct((K, 16 * TILE), F32))
        out_specs.append(VMEM)
    else:
        out_shape += [pltpu.VMEM((X_BLOCKS, K, TILE), BF), jax.ShapeDtypeStruct(half, F32)]
        out_specs += [VMEM, VMEM]
    if first:
        out_shape.append(jax.ShapeDtypeStruct((16, TILE), F32))
        out_specs.append(VMEM)
    scratch = [
        pltpu.VMEM((16, K, TILE), F32), pltpu.VMEM((2, 6, 4, 4, K, TILE), BF), pltpu.VMEM((2, 6, 4, 4, K, TILE), BF),
        pltpu.VMEM((2, 6, 4, K, TILE), BF), pltpu.VMEM((2, 6, 4, K, TILE), BF), pltpu.VMEM((2, 2, 4, K, TILE), F32),
        pltpu.VMEM((4,) + half, F32), pltpu.VMEM((4,) + half, F32), pltpu.VMEM((NR,) + half, F32),
        dma((2, 6)), dma((2, 6)), dma((2, 6)), dma((2, 6)), dma((13,)), dma((13,)),
    ]
    if first:
        scratch += [pltpu.VMEM((NC, 16, TILE), F32), dma, dma, dma]
    if not last:
        scratch += [pltpu.VMEM(XS_SHAPE, BF), pltpu.VMEM(XC_SHAPE, BF)] + x_sems()
    args = [part.reshape(4, 4, 16, K, TILE), degree] + ([] if first else [gram])
    return pl.pallas_call(
        functools.partial(normalize_kernel, first, last),
        out_shape=out_shape,
        in_specs=[VMEM, VMEM] + ([] if first else [VMEM]),
        out_specs=out_specs,
        scratch_shapes=scratch,
        compiler_params=pltpu.CompilerParams(
            collective_id=1 if first else (3 if last else 2), has_side_effects=True, vmem_limit_bytes=16 * MIB
        ),
        name="normalize",
    )(*args)


def block_index(block):
    return block // 32 * 32 + block % 16 * 2 + block // 16 % 2


def local(embed, tiles, tile_rows, tile_cols, chg_tiles, chg_rows, chg_cols):
    owners = chg_cols // 256 * NC + chg_rows // 128
    count = owners.shape[0]
    position = jnp.arange(count, dtype=jnp.int32)
    earlier = position[None, :] < position[:, None]
    rank = jnp.sum(jnp.logical_and(owners[:, None] == owners[None, :], earlier).astype(jnp.int32), axis=1)
    key = owners * CAP + rank
    hit = jnp.arange(DEV * CAP, dtype=jnp.int32)[:, None] == key[None, :]
    pick = jnp.sum(jnp.where(hit, position[None, :], 0), axis=1)
    code = jnp.sum(jnp.where(hit, (1 + chg_cols % 256 * 128 + block_index(chg_rows % 128))[None, :], 0), axis=1)
    slot_rows = jnp.where(code > 0, (code - 1) // 128, 0).reshape(DEV, CAP)
    slot_cols = jnp.where(code > 0, (code - 1) % 128, 128).reshape(DEV, CAP)
    meta = jnp.concatenate([slot_rows, slot_cols], axis=1).reshape(NR, NC, 2 * CAP).transpose(1, 0, 2)
    meta = jnp.pad(meta, ((0, 0), (0, 0), (0, TILE - 2 * CAP)))
    slots, tiles, places, xc = exchange(pick, chg_tiles, tiles, meta, embed.T)
    own_rows = tile_rows % 256
    own_cols = block_index(tile_cols % 128)
    part, degree = product(True, places, own_rows, own_cols, xc, tiles, slots)
    xc, gram, degree = normalize(True, False, part, degree, None)
    for iteration in range(1, ITERS):
        (part,) = product(False, places, own_rows, own_cols, xc, tiles, slots)
        last = iteration == ITERS - 1
        outs = normalize(False, last, part, degree, gram)
        if last:
            return outs[0].T
        xc, gram = outs


def solution(mesh):
    placed = (
        P(("row", "col"), None),
        P(("row", "col"), None, None),
        P(("row", "col")),
        P(("row", "col")),
        P(("row", "col"), None, None),
        P(("row", "col")),
        P(("row", "col")),
    )
    return jax.shard_map(
        local, mesh=mesh, in_specs=placed, out_specs=P(("row", "col"), None), check_vma=False
    )
```

```python
import functools

import jax
import jax.numpy as jnp
from jax import lax
from jax.experimental import pallas as pl
from jax.experimental.pallas import tpu as pltpu
from jax.sharding import PartitionSpec as P

ITERS = 3
CAP = 3
K = 64
TILE = 128
NR = 8
NC = 16
DEV = NR * NC
ROWS_BLK = 256
SLOT_ROWS = CAP * TILE
X_BLOCKS = 130
OWN = 64
NODES = 262144
BF = jnp.bfloat16
F32 = jnp.float32
ANY = pl.BlockSpec(memory_space=pl.ANY)

VMEM = pl.BlockSpec(memory_space=pltpu.VMEM)
SMEM = pl.BlockSpec(memory_space=pltpu.SMEM)
MIB = 1024 * 1024
ROW_ORDER = ((2, 0), (1, 1), (3, 0), (2, 1), (1, 0), (3, 1), (0, 1))


def dot(a, b, dims, precision=None):
    return lax.dot_general(a, b, (dims, ((), ())), precision=precision, preferred_element_type=F32)


def greet(row, col):
    barrier = pltpu.get_barrier_semaphore()

    def cols(k, carry):
        pl.semaphore_signal(barrier, inc=1, device_id={"col": lax.rem(col + k, NC)}, device_id_type=pl.DeviceIdType.MESH)
        return carry

    def rows(k, carry):
        pl.semaphore_signal(barrier, inc=1, device_id={"row": lax.rem(row + k, NR)}, device_id_type=pl.DeviceIdType.MESH)
        return carry

    lax.fori_loop(1, NC, cols, 0)
    lax.fori_loop(1, NR, rows, 0)
    pl.semaphore_wait(barrier, NC + NR - 2)


def remote(src, dst, send_sem, recv_sem, **peer):
    return pltpu.make_async_remote_copy(
        src_ref=src, dst_ref=dst, send_sem=send_sem, recv_sem=recv_sem,
        device_id=peer, device_id_type=pl.DeviceIdType.MESH,
    )


def wait_bytes(ref, sem):
    pltpu.make_async_copy(ref, ref, sem).wait()


def col_peer(col, k):
    return lax.rem(col // 4 + k // 4, 4) * 4 + lax.rem(lax.rem(col, 4) + lax.rem(k, 4), 4)


def row_peer(row, dz, flip=0):
    return lax.rem(row // 2 + dz, 4) * 2 + lax.rem(row + flip, 2)


def x_pieces(batch, block, xs):
    for i in range(2):
        for part in range(2):
            pair = batch * 2 + i
            both = jnp.concatenate([block(pair * 4 + part), block(pair * 4 + 2 + part)], axis=0).T
            xs[batch, part * 8:(part + 1) * 8, i] = both.astype(BF).reshape(8, 16, TILE)


def x_own_copy(batch, row, col, xs, xc, sems):
    return pltpu.make_async_copy(xs.at[batch, col], xc.at[batch, row, col], sems["x_own"].at[batch])


def x_first(batch, row, col, xs, xc, sems):
    x_own_copy(batch, row, col, xs, xc, sems).start()

    def send(k, carry):
        peer = col_peer(col, k)
        remote(xs.at[batch, peer], xc.at[batch, row, col], sems["xa_send"].at[batch], sems["xa_recv"].at[batch], col=peer).start()
        return carry

    lax.fori_loop(1, NC, send, 0)


def x_second(batch, row, col, xs, xc, sems):
    x_own_copy(batch, row, col, xs, xc, sems).wait()
    wait_bytes(xc.at[batch, row, pl.ds(0, NC - 1)], sems["xa_recv"].at[batch])
    for i, (dz, flip) in enumerate(((1, 0), (3, 0), (2, 0), (0, 1))):
        remote(xc.at[batch, row], xc.at[batch, row], sems["xb_send"].at[batch, i], sems["xb_recv"].at[batch, row],
               row=row_peer(row, dz, flip)).start()


def x_third(batch, row, col, xs, xc, sems):
    for i, dz in enumerate((1, 3, 2)):
        source = row_peer(row, dz)
        wait_bytes(xc.at[batch, source], sems["xb_recv"].at[batch, source])
        remote(xc.at[batch, source], xc.at[batch, source], sems["xb_send"].at[batch, 4 + i], sems["xb_recv"].at[batch, source],
               row=row_peer(row, 0, 1)).start()


def x_finish(batch, row, col, xs, xc, xt, sems):
    for dz in range(4):
        turn(batch, row_peer(row, dz), xc, xt)
    for dz in (0, 1, 3, 2):
        source = row_peer(row, dz, 1)
        wait_bytes(xc.at[batch, source], sems["xb_recv"].at[batch, source])
        turn(batch, source, xc, xt)
    wait_bytes(xs.at[batch, pl.ds(0, NC - 1)], sems["xa_send"].at[batch])
    for i in range(7):
        wait_bytes(xc.at[batch, row], sems["xb_send"].at[batch, i])
    if batch:
        xt[X_BLOCKS - 2:] = jnp.zeros((2, K, TILE), BF)


def turn(batch, source, xc, xt):
    for part in range(2):
        for i in range(2):
            block = xc[batch, source, part * 8:(part + 1) * 8, i].reshape(TILE, TILE)
            xt[pl.ds(((batch * 2 + i) * 16 + source * 2 + part) * 2, 2)] = block.T.reshape(2, K, TILE)


X_SEMS = ("x_own", "xa_send", "xa_recv", "xb_send", "xb_recv")


def x_sems():
    dma = pltpu.SemaphoreType.DMA
    return [dma((2,)), dma((2,)), dma((2,)), dma((2, 7)), dma((2, NR))]


XS_SHAPE = (2, NC, 2, 16, TILE)
XC_SHAPE = (2, NR, NC, 2, 16, TILE)


def exchange_kernel(pick_ref, tiles_in_ref, own_in_ref, meta_ref, embed_ref,
                    recv_ref, mid_ref, far_ref, own_out_ref, places_ref, xt_ref,
                    send_ref, xc_ref, meta_mid_ref, meta_next_ref, xs_ref, tiles_ref, own_ref, tiles_sem, own_load_sem, *sem_refs):
    sems = dict(zip(X_SEMS, sem_refs))
    (a_send, a_recv, b_send, b_recv, c_send, c_recv, d_send, d_recv,
     m_send, m_recv, n_send, n_recv, own_sem, far_sem) = sem_refs[len(X_SEMS):]
    load_tiles = pltpu.make_async_copy(tiles_in_ref, tiles_ref, tiles_sem)
    load_own = pltpu.make_async_copy(own_in_ref, own_ref, own_load_sem)
    load_tiles.start()
    load_own.start()
    half = SLOT_ROWS // 2
    head, tail = pl.ds(0, half), pl.ds(half, half)
    row = lax.axis_index("row")
    col = lax.axis_index("col")
    greet(row, col)
    for batch in range(2):
        x_pieces(batch, lambda b: embed_ref[:, b * TILE:(b + 1) * TILE], xs_ref)
        x_first(batch, row, col, xs_ref, xc_ref, sems)
    targets = [row_peer(row, dz, flip) for dz, flip in ROW_ORDER] + [row]
    sources = [row_peer(row, (4 - dz) % 4, flip) for dz, flip in ROW_ORDER]

    def send_meta(k, carry):
        peer = col_peer(col, k)
        remote(meta_ref.at[peer], meta_mid_ref.at[col], m_send, m_recv, col=peer).start()
        return carry

    lax.fori_loop(1, NC, send_meta, 0)
    meta_mid_ref[col] = meta_ref[col]

    def fill(target):
        def tiles(c, carry):
            for slot in range(CAP):
                send_ref[target, c, slot * TILE:(slot + 1) * TILE] = tiles_ref[pick_ref[(target * NC + c) * CAP + slot]]
            return carry

        lax.fori_loop(0, NC, tiles, 0)

    def first_own(step):
        target = targets[step]
        if step < NR - 1:
            return pltpu.make_async_copy(send_ref.at[target, col, head], mid_ref.at[target, col], own_sem.at[step])
        return pltpu.make_async_copy(send_ref.at[target, col, head], recv_ref.at[target, col, head], own_sem.at[step])

    def first(step):
        target = targets[step]

        def send(k, carry):
            peer = col_peer(col, k)
            dst = mid_ref.at[target, col] if step < NR - 1 else recv_ref.at[target, col, head]
            remote(send_ref.at[target, peer, head], dst, a_send.at[step], a_recv.at[step], col=peer).start()
            return carry

        lax.fori_loop(1, NC, send, 0)
        first_own(step).start()

    def second_own(step):
        if step < NR - 1:
            return pltpu.make_async_copy(far_ref.at[sources[step], col], recv_ref.at[sources[step], col, tail], far_sem.at[step])
        return pltpu.make_async_copy(send_ref.at[row, col, tail], recv_ref.at[row, col, tail], far_sem.at[step])

    def second(step):
        def send(k, carry):
            peer = col_peer(col, k)
            source = sources[step] if step < NR - 1 else row
            src = far_ref.at[source, peer] if step < NR - 1 else send_ref.at[row, peer, tail]
            remote(src, recv_ref.at[source, col, tail], d_send.at[step], d_recv.at[source], col=peer).start()
            return carry

        lax.fori_loop(1, NC, send, 0)
        second_own(step).start()

    load_tiles.wait()
    for step in range(NR):
        fill(targets[step])
        if step < NR - 1:
            remote(send_ref.at[targets[step], :, tail], far_ref.at[row], c_send.at[step], c_recv.at[row], row=targets[step]).start()
            first(step)
        if step < 2:
            x_second(step, row, col, xs_ref, xc_ref, sems)
    wait_bytes(meta_mid_ref.at[pl.ds(0, NC - 1)], m_recv)
    for c in range(NC):
        for r in range(NR):
            meta_next_ref[r, c:c + 1] = meta_mid_ref[c, r:r + 1]
    for step in range(NR - 1):
        remote(meta_next_ref.at[targets[step]], places_ref.at[row], n_send, n_recv, row=targets[step]).start()
    places_ref[row] = meta_next_ref[row]
    for batch in range(2):
        x_third(batch, row, col, xs_ref, xc_ref, sems)

    def flip_own(i, carry):
        for u in range(4):
            own_out_ref[i * 4 + u] = own_ref[i * 4 + u].T
        return carry

    load_own.wait()
    lax.fori_loop(0, OWN // 4, flip_own, 0)
    for step in range(NR - 1):
        target, source = targets[step], sources[step]
        wait_bytes(mid_ref.at[target, pl.ds(0, NC - 1)], a_recv.at[step])
        first_own(step).wait()
        remote(mid_ref.at[target], recv_ref.at[row, :, head], b_send.at[step], b_recv.at[row], row=target).start()
        wait_bytes(far_ref.at[source], c_recv.at[source])
        second(step)
    first(NR - 1)
    second(NR - 1)
    for batch in range(2):
        x_finish(batch, row, col, xs_ref, xc_ref, xt_ref, sems)
    some = mid_ref.at[0, pl.ds(0, NC - 1)]
    wait_bytes(some, a_recv.at[NR - 1])
    first_own(NR - 1).wait()
    wait_bytes(meta_mid_ref.at[pl.ds(0, NC - 1)], m_send)
    wait_bytes(places_ref.at[pl.ds(0, NR - 1)], n_send)
    wait_bytes(places_ref.at[pl.ds(0, NR - 1)], n_recv)
    for step in range(NR):
        wait_bytes(some, a_send.at[step])
        wait_bytes(some, d_send.at[step])
        wait_bytes(some, d_recv.at[sources[step] if step < NR - 1 else row])
        second_own(step).wait()
    for step in range(NR - 1):
        wait_bytes(mid_ref.at[0], b_send.at[step])
        wait_bytes(mid_ref.at[0], c_send.at[step])
        wait_bytes(mid_ref.at[0], b_recv.at[targets[step]])


def exchange(pick, chg_tiles, own, meta, xs):
    dma = pltpu.SemaphoreType.DMA
    slots = (NR, NC, SLOT_ROWS, TILE)
    halves = jax.ShapeDtypeStruct((NR, NC, SLOT_ROWS // 2, TILE), BF)
    recv, _, _, own, places, xt = pl.pallas_call(
        exchange_kernel,
        out_shape=(jax.ShapeDtypeStruct(slots, BF), halves, halves, pltpu.VMEM((OWN, TILE, TILE), BF),
                   pltpu.VMEM((NR, NC, TILE), jnp.int32), pltpu.VMEM((X_BLOCKS, K, TILE), BF)),
        in_specs=[SMEM, ANY, ANY, VMEM, VMEM],
        out_specs=(ANY, ANY, ANY, VMEM, VMEM, VMEM),
        scratch_shapes=[
            pltpu.VMEM(slots, BF), pltpu.VMEM(XC_SHAPE, BF),
            pltpu.VMEM((NC, NR, TILE), jnp.int32), pltpu.VMEM((NR, NC, TILE), jnp.int32),
            pltpu.VMEM(XS_SHAPE, BF), pltpu.VMEM(chg_tiles.shape, BF), pltpu.VMEM(own.shape, BF), dma, dma,
        ] + x_sems() + [dma((NR,))] * 8 + [dma, dma, dma, dma, dma((NR,)), dma((NR,))],
        compiler_params=pltpu.CompilerParams(collective_id=0, has_side_effects=True, vmem_limit_bytes=56 * MIB),
        name="exchange",
    )(pick, chg_tiles, own, meta, xs)
    return recv, own, places, xt


def product_kernel(with_degree, places_ref, own_rows_ref, own_cols_ref, xt_ref, own_ref, slots_in_ref, acc_ref, *rest):
    slots_ref, slot_sem, table_ref, table_sem = rest[-4:]
    load_table = pltpu.make_async_copy(places_ref, table_ref, table_sem)
    load_table.start()
    loads = [
        pltpu.make_async_copy(slots_in_ref.at[i], slots_ref.at[i], slot_sem.at[i])
        for i in range(NR)
    ]
    for load in loads:
        load.start()
    ones = jnp.ones((8, TILE), BF)
    plain = ((1,), (0,))
    if with_degree:
        degree_out_ref, degree_ref = rest[:2]
        degree_ref[...] = jnp.zeros_like(degree_ref)

    def clear(i, carry):
        acc_ref[pl.ds(i * 8, 8)] = jnp.zeros((8, K, TILE), F32)
        return carry

    lax.fori_loop(0, ROWS_BLK // 8, clear, 0)

    def run(tiles, rows, cols):
        values = [dot(xt_ref[col], tile, plain) for tile, col in zip(tiles, cols)]
        sums = []
        if with_degree:
            sums = [
                dot(jnp.where(col < 128, ones, jnp.zeros_like(ones)), jnp.abs(tile), plain)[0:1]
                for tile, col in zip(tiles, cols)
            ]
        for row, value in zip(rows, values):
            acc_ref[row] += value
        for row, value in zip(rows, sums):
            degree_ref[row] += value

    def own(i, carry):
        places = [i * 16 + u for u in range(16)]
        run([own_ref[n] for n in places], [own_rows_ref[n] for n in places], [own_cols_ref[n] for n in places])
        return carry

    def taken(group, carry):
        places = [(source, slot) for source in range(NC) for slot in range(CAP)]
        run([slots_ref[group, source, slot * TILE:(slot + 1) * TILE] for source, slot in places],
            [table_ref[group, source, slot] for source, slot in places],
            [table_ref[group, source, CAP + slot] for source, slot in places])
        return carry

    lax.fori_loop(0, OWN // 16, own, 0)
    load_table.wait()
    for i, load in enumerate(loads):
        load.wait()
        lax.fori_loop(i, i + 1, taken, 0)
    if with_degree:
        degree_out_ref[...] = degree_ref[...].reshape(ROWS_BLK, TILE)


def product(with_degree, places, own_rows, own_cols, xt, own, slots):
    out_shape = [pltpu.VMEM((ROWS_BLK, K, TILE), F32)]
    if with_degree:
        out_shape.append(jax.ShapeDtypeStruct((ROWS_BLK, TILE), F32))
    terms = DEV * CAP + OWN
    return pl.pallas_call(
        functools.partial(product_kernel, with_degree),
        out_shape=out_shape,
        in_specs=[VMEM, SMEM, SMEM, VMEM, VMEM, ANY],
        out_specs=[VMEM] * len(out_shape),
        scratch_shapes=([pltpu.VMEM((ROWS_BLK, 1, TILE), F32)] if with_degree else []) + [
            pltpu.VMEM((NR, NC, SLOT_ROWS, TILE), BF), pltpu.SemaphoreType.DMA((NR,)),
            pltpu.SMEM((NR, NC, TILE), jnp.int32), pltpu.SemaphoreType.DMA,
        ],
        compiler_params=pltpu.CompilerParams(vmem_limit_bytes=40 * MIB),
        cost_estimate=pl.CostEstimate(flops=terms * 2 * K * TILE * TILE, bytes_accessed=terms * TILE * TILE * 2, transcendentals=0),
        name="product",
    )(places, own_rows, own_cols, xt, own, slots)


def inverse_factor(gram):
    eye = (lax.broadcasted_iota(jnp.int32, (K, K), 0) == lax.broadcasted_iota(jnp.int32, (K, K), 1)).astype(F32)
    work = jnp.concatenate([gram, eye], axis=1)
    index = lax.broadcasted_iota(jnp.int32, (K, 1), 0)
    pivots = jnp.ones((K, 1), F32)
    for j in range(0, K, 2):
        first_row, first_col = work[j:j + 1, :], work[:, j:j + 1]
        second_col = work[:, j + 1:j + 2]
        pivot, below = first_col[j:j + 1], first_col[j + 1:j + 2]
        beside = second_col[j:j + 1]
        inverse = 1.0 / pivot
        step = below * inverse
        second_row = work[j + 1:j + 2, :] - step * first_row
        second_pivot = second_col[j + 1:j + 2] - step * beside
        first_factor = jnp.where(index > j, first_col * inverse, 0.0)
        second_factor = jnp.where(index > j + 1, (second_col - first_factor * beside) * (1.0 / second_pivot), 0.0)
        pivots = jnp.where(index == j, pivot, jnp.where(index == j + 1, second_pivot, pivots))
        work = work - first_factor * first_row - second_factor * second_row
    return lax.rsqrt(pivots) * work[:, K:]


def gram_pack(gram):
    return jnp.concatenate([gram[:K // 2], gram[K // 2:]], axis=1)


def gram_unpack(packed):
    return jnp.concatenate([packed[:, :K], packed[:, K:]], axis=0)


def normalize_kernel(first, last, part_ref, degree_in_ref, *rest):
    rest = list(rest)
    take = lambda count: [rest.pop(0) for _ in range(count)]
    gram_in_ref = None if first else rest.pop(0)
    if last:
        (z_ref,) = take(1)
    else:
        xt_ref, gram_ref = take(2)
    degree_ref = rest.pop(0) if first else degree_in_ref
    y_ref, s1_ref, a1_ref, s2_ref, a2_ref, v_ref, g1_ref, g2_ref, g3_ref = take(9)
    s1_send, s1_recv, s2_send, s2_recv, g_send, g_recv = take(6)
    if first:
        dg_ref, dg_own, dg_send, dg_recv = take(4)
    if not last:
        xs_ref, xc_ref = take(2)
        sems = dict(zip(X_SEMS, rest))
    row = lax.axis_index("row")
    col = lax.axis_index("col")
    x, y = col // 4, lax.rem(col, 4)
    x_peer = lambda k: lax.rem(x + k, 4) * 4 + y
    y_peer = lambda k: x * 4 + lax.rem(y + k, 4)
    greet(row, col)

    ways = ((1, 3) * 3)

    def ring(stage, h, message):
        along_x = (h == 0) == (stage == 1)
        k = ways[message]
        src, dst, send_sem, recv_sem = (s1_ref, a1_ref, s1_send, s1_recv) if stage == 1 else (s2_ref, a2_ref, s2_send, s2_recv)
        return remote(src.at[h, message], dst.at[h, message], send_sem.at[h, message], recv_sem.at[h, message],
                      col=x_peer(k) if along_x else y_peer(k))

    def arrived(stage, h, message):
        dst, recv_sem = (a1_ref, s1_recv) if stage == 1 else (a2_ref, s2_recv)
        wait_bytes(dst.at[h, message], recv_sem.at[h, message])

    def mine(h, k, other, half):
        target = lax.rem((y if h else x) + k, 4)
        blocks = slice(h * 8 + half * 4, h * 8 + half * 4 + 4)
        return part_ref[other, target, blocks] if h else part_ref[target, other, blocks]

    plan = ((0, 2, 0), (1, 2, 1), (2, 1, 1), (3, 3, 0))
    for message, k, half in plan:
        for h in range(2):
            def narrow(other, carry):
                s1_ref[h, message, other] = mine(h, k, other, half).astype(BF)
                return carry

            lax.fori_loop(0, 4, narrow, 0)
            ring(1, h, message).start()
    if first:
        pltpu.make_async_copy(degree_in_ref.at[pl.ds(col * 16, 16)], dg_ref.at[col], dg_own).start()

        def send(k, carry):
            peer = col_peer(col, k)
            remote(degree_in_ref.at[pl.ds(peer * 16, 16)], dg_ref.at[col], dg_send, dg_recv, col=peer).start()
            return carry

        lax.fori_loop(1, NC, send, 0)
    else:
        inverse = inverse_factor(gram_unpack(gram_in_ref[...]))
    for message, k, half in ((4, 1, 0), (5, 3, 1)):
        for h in range(2):
            arrived(1, h, message - 4)

            def pass_on(other, carry):
                s1_ref[h, message, other] = (mine(h, k, other, half) + a1_ref[h, message - 4, other].astype(F32)).astype(BF)
                return carry

            lax.fori_loop(0, 4, pass_on, 0)
            ring(1, h, message).start()
    for h in range(2):
        for message in range(2, 6):
            arrived(1, h, message)
        place = x if h else y

        def value(k, half):
            other = lax.rem(place + k, 4)
            near, far = (3, 4) if half == 0 else (2, 5)
            return mine(h, 0, other, half) + a1_ref[h, near, other].astype(F32) + a1_ref[h, far, other].astype(F32)

        for message, k, half in plan:
            s2_ref[h, message] = value(k, half).astype(BF)
            ring(2, h, message).start()
        v_ref[h, 0] = value(1, 0)
        v_ref[h, 1] = value(3, 1)
        for half in range(2):
            y_ref[h * 8 + half * 4:h * 8 + half * 4 + 4] = value(0, half)
    for h in range(2):
        for message in (4, 5):
            arrived(2, h, message - 4)
            s2_ref[h, message] = (v_ref[h, message - 4] + a2_ref[h, message - 4].astype(F32)).astype(BF)
            ring(2, h, message).start()
    if first:
        pltpu.make_async_copy(degree_in_ref.at[pl.ds(col * 16, 16)], dg_ref.at[col], dg_own).wait()
        wait_bytes(dg_ref.at[pl.ds(0, NC - 1)], dg_recv)
        degree = dg_ref[0]
        for k in range(1, NC):
            degree = degree + dg_ref[k]
        degree_ref[...] = 1.0 + degree
    for h in range(2):
        for message in range(2, 6):
            arrived(2, h, message)
        for b in range(8):
            near, far = (3, 4) if b < 4 else (2, 5)
            value = y_ref[h * 8 + b] + a2_ref[h, near, b % 4].astype(F32) + a2_ref[h, far, b % 4].astype(F32)
            value = value * (1.0 / degree_ref[h * 8 + b:h * 8 + b + 1])
            if not first:
                value = dot(inverse, value, ((1,), (0,)), lax.Precision.HIGHEST)
            y_ref[h * 8 + b] = value
        if not last:
            x_pieces(h, lambda b: y_ref[b], xs_ref)
            x_first(h, row, col, xs_ref, xc_ref, sems)

    if not last:
        x_second(0, row, col, xs_ref, xc_ref, sems)

    gram = jnp.zeros((K, K), F32)
    for b in range(16):
        block = y_ref[b]
        gram = gram + dot(block, block, ((1,), (1,)), lax.Precision.HIGHEST)

    def share(buffer, place, value, peers, base):
        buffer[place] = value
        for i, peer in enumerate(peers):
            remote(buffer.at[place], buffer.at[place], g_send.at[base + i], g_recv.at[base], **peer).start()

    def collect(buffer, count, base):
        wait_bytes(buffer.at[pl.ds(0, count - 1)], g_recv.at[base])
        total = buffer[0]
        for k in range(1, count):
            total = total + buffer[k]
        return total

    share(g1_ref, x, gram_pack(gram), [dict(col=x_peer(k)) for k in (1, 3, 2)], 0)
    if not last:
        x_second(1, row, col, xs_ref, xc_ref, sems)
    share(g2_ref, y, collect(g1_ref, 4, 0), [dict(col=y_peer(k)) for k in (1, 3, 2)], 3)
    share(g3_ref, row, collect(g2_ref, 4, 3), [dict(row=row_peer(row, dz, flip)) for dz, flip in ROW_ORDER], 6)
    if not last:
        x_third(0, row, col, xs_ref, xc_ref, sems)
        x_third(1, row, col, xs_ref, xc_ref, sems)
    total = collect(g3_ref, NR, 6) * (1.0 / NODES)
    if last:
        final = inverse_factor(gram_unpack(total))
        for b in range(16):
            z_ref[:, b * TILE:(b + 1) * TILE] = dot(final, y_ref[b], ((1,), (0,)), lax.Precision.HIGHEST)
    else:
        gram_ref[...] = total
        x_finish(0, row, col, xs_ref, xc_ref, xt_ref, sems)
        x_finish(1, row, col, xs_ref, xc_ref, xt_ref, sems)
    for h in range(2):
        for message in range(6):
            wait_bytes(a1_ref.at[h, message], s1_send.at[h, message])
            wait_bytes(a2_ref.at[h, message], s2_send.at[h, message])
    if first:
        wait_bytes(dg_ref.at[pl.ds(0, NC - 1)], dg_send)
    for i in range(13):
        wait_bytes(g1_ref.at[0], g_send.at[i])


def normalize(first, last, part, degree, gram):
    dma = pltpu.SemaphoreType.DMA
    half = (K // 2, TILE)
    out_shape, out_specs = [], []
    if last:
        out_shape.append(jax.ShapeDtypeStruct((K, 16 * TILE), F32))
        out_specs.append(VMEM)
    else:
        out_shape += [pltpu.VMEM((X_BLOCKS, K, TILE), BF), jax.ShapeDtypeStruct(half, F32)]
        out_specs += [VMEM, VMEM]
    if first:
        out_shape.append(jax.ShapeDtypeStruct((16, TILE), F32))
        out_specs.append(VMEM)
    scratch = [
        pltpu.VMEM((16, K, TILE), F32), pltpu.VMEM((2, 6, 4, 4, K, TILE), BF), pltpu.VMEM((2, 6, 4, 4, K, TILE), BF),
        pltpu.VMEM((2, 6, 4, K, TILE), BF), pltpu.VMEM((2, 6, 4, K, TILE), BF), pltpu.VMEM((2, 2, 4, K, TILE), F32),
        pltpu.VMEM((4,) + half, F32), pltpu.VMEM((4,) + half, F32), pltpu.VMEM((NR,) + half, F32),
        dma((2, 6)), dma((2, 6)), dma((2, 6)), dma((2, 6)), dma((13,)), dma((13,)),
    ]
    if first:
        scratch += [pltpu.VMEM((NC, 16, TILE), F32), dma, dma, dma]
    if not last:
        scratch += [pltpu.VMEM(XS_SHAPE, BF), pltpu.VMEM(XC_SHAPE, BF)] + x_sems()
    args = [part.reshape(4, 4, 16, K, TILE), degree] + ([] if first else [gram])
    return pl.pallas_call(
        functools.partial(normalize_kernel, first, last),
        out_shape=out_shape,
        in_specs=[VMEM, VMEM] + ([] if first else [VMEM]),
        out_specs=out_specs,
        scratch_shapes=scratch,
        compiler_params=pltpu.CompilerParams(
            collective_id=1 if first else (3 if last else 2), has_side_effects=True, vmem_limit_bytes=16 * MIB
        ),
        name="normalize",
    )(*args)


def block_index(block):
    return block // 32 * 32 + block % 16 * 2 + block // 16 % 2


def local(embed, tiles, tile_rows, tile_cols, chg_tiles, chg_rows, chg_cols):
    owners = chg_cols // 256 * NC + chg_rows // 128
    count = owners.shape[0]
    position = jnp.arange(count, dtype=jnp.int32)
    earlier = position[None, :] < position[:, None]
    rank = jnp.sum(jnp.logical_and(owners[:, None] == owners[None, :], earlier).astype(jnp.int32), axis=1)
    key = owners * CAP + rank
    hit = jnp.arange(DEV * CAP, dtype=jnp.int32)[:, None] == key[None, :]
    pick = jnp.sum(jnp.where(hit, position[None, :], 0), axis=1)
    code = jnp.sum(jnp.where(hit, (1 + chg_cols % 256 * 128 + block_index(chg_rows % 128))[None, :], 0), axis=1)
    slot_rows = jnp.where(code > 0, (code - 1) // 128, 0).reshape(DEV, CAP)
    slot_cols = jnp.where(code > 0, (code - 1) % 128, 128).reshape(DEV, CAP)
    meta = jnp.concatenate([slot_rows, slot_cols], axis=1).reshape(NR, NC, 2 * CAP).transpose(1, 0, 2)
    meta = jnp.pad(meta, ((0, 0), (0, 0), (0, TILE - 2 * CAP)))
    slots, tiles, places, xc = exchange(pick, chg_tiles, tiles, meta, embed.T)
    own_rows = tile_rows % 256
    own_cols = block_index(tile_cols % 128)
    part, degree = product(True, places, own_rows, own_cols, xc, tiles, slots)
    xc, gram, degree = normalize(True, False, part, degree, None)
    for iteration in range(1, ITERS):
        (part,) = product(False, places, own_rows, own_cols, xc, tiles, slots)
        last = iteration == ITERS - 1
        outs = normalize(False, last, part, degree, gram)
        if last:
            return outs[0].T
        xc, gram = outs


def solution(mesh):
    placed = (
        P(("row", "col"), None),
        P(("row", "col"), None, None),
        P(("row", "col")),
        P(("row", "col")),
        P(("row", "col"), None, None),
        P(("row", "col")),
        P(("row", "col")),
    )
    return jax.shard_map(
        local, mesh=mesh, in_specs=placed, out_specs=P(("row", "col"), None), check_vma=False
    )
```
